32 devices in a mesh: seq: 8 (over z, y), rows: 4 (over x, core).
Axes of the slice: x: 2, y: 2, z: 4, core: 2. Of those that a mesh axis runs over, the one named last changes fastest.
Arguments:
- hidden: bfloat16 [4, 1024, 768], P('rows', 'seq'), may hold values from -6 to 6
- cotangent: bfloat16 [4, 1024, 768], P('rows', 'seq'), may hold values from -6 to 6
- segment_ids: int32 [4, 1024], P('rows', 'seq'), may hold values from 0 to 15, never falling along the last dimension, each value on 1 to 768 neighbouring positions
- timesteps: int32 [4, 16], P('rows'), may hold values from 0 to 4999
- qkv_weight: bfloat16 [768, 2304], replicated, may hold values from -0.21875 to 0.21875
- qv_bias: float32 [1536], replicated, may hold values from -3 to 3
- out_weight: bfloat16 [768, 768], replicated, may hold values from -1.75 to 1.75
- out_bias: float32 [768], replicated, may hold values from -3 to 3
- up_weight: bfloat16 [768, 3072], replicated, may hold values from -0.21875 to 0.21875
- up_bias: float32 [3072], replicated, may hold values from -3 to 3
- down_weight: bfloat16 [3072, 768], replicated, may hold values from -0.109375 to 0.109375
- down_bias: float32 [768], replicated, may hold values from -3 to 3
- norm_gain: float32 [2, 768], replicated, may hold values from 0.1 to 1.9
- norm_bias: float32 [2, 768], replicated, may hold values from -3 to 3
- time_weight: bfloat16 [768, 768], replicated, may hold values from -0.21875 to 0.21875
Outputs:
- result: bfloat16 [4, 1024, 768], P('rows', 'seq')
- input_grad: float32 [4, 1024, 768], P('rows', 'seq')
- grad_qkv_weight: float32 [768, 2304], P('seq')
- grad_qv_bias: float32 [1536], P('seq')
- grad_out_weight: float32 [768, 768], P('seq')
- grad_out_bias: float32 [768], P('seq')
- grad_up_weight: float32 [768, 3072], P('seq')
- grad_up_bias: float32 [3072], P('seq')
- grad_down_weight: float32 [3072, 768], P('seq')
- grad_down_bias: float32 [768], P('seq')
- grad_norm_gain: float32 [2, 768], P(None, 'seq')
- grad_norm_bias: float32 [2, 768], P(None, 'seq')
- grad_time_weight: float32 [768, 768], P('seq')
The draws below stay inside these ranges and needn't reach their ends.
Inputs may be any that keep to these rules, and one draw needn't show every extreme that they name: `segment_ids`: along each row the ids never fall; each of the 16 documents covers 1 to 768 consecutive tokens, and one of each row covers exactly 768.
All inputs are finite; a program needn't handle non-finite values.
Results may differ from the reference program's by a relative error of at most 0.023.
Values may be sent and summed in bfloat16 or wider, within the bound.
No kernel may reach another device: no remote copies, remote signals or barrier semaphores. Data moves between devices by JAX's collectives and lax.ppermute only.
A program may use at most 192 MiB of HBM per device.

```python
import math
from functools import partial
import jax
import jax.numpy as jnp
import numpy as np
from jax import lax

D = 768
H = 12
HD = 64
FF = 3072
DOCS = 16
TSTEPS = 5000
LEN = 1024
ROWS = 4
DOC_MOST = 768


def place_ends(array, own_key, smallest, high):
    longest = array.shape.index(max(array.shape))
    spots = []
    for shift in (0, 1):
        where = [jax.random.randint(jax.random.fold_in(own_key, axis), (), 0, length) for axis, length in enumerate(array.shape)]
        where[longest] = (where[longest] + shift) % array.shape[longest]
        spots.append(tuple(where))
    return array.at[spots[0]].set(smallest).at[spots[1]].set(high)


def level_of(stream_key, extent, shards, least, high):
    def one(axis_at, shards_of):
        heights = jax.random.uniform(jax.random.fold_in(jax.random.fold_in(stream_key, 6), axis_at), (shards_of,), jnp.float32, least / len(shards), high / len(shards))
        return jnp.repeat(jnp.exp(heights), extent[axis_at] // shards_of).reshape((-1,) + (1,) * (len(extent) - axis_at - 1))

    level = one(*shards[0])
    for cut in shards[1:]:
        level = level * one(*cut)
    return level


def split_up(amount, total, reach, slope):
    weights = [(1 << 20) // math.isqrt(standing ** slope) + 1 for standing in range(2, amount + 1)]
    surplus, holding = total - reach - (amount - 1), [1] * (amount - 1)
    while surplus > 0:
        free = [i for i in range(amount - 1) if holding[i] < reach]
        mass, remaining = sum([weights[i] for i in free]), surplus
        for i in free:
            more = min(reach - holding[i], max(1, remaining * weights[i] // mass), surplus)
            holding[i] = holding[i] + more
            surplus = surplus - more
    return np.array([reach] + holding)


def ragged_sizes(stream_key, count, total, most, lean):
    if count == 2:
        one = jax.random.randint(stream_key, (), max(1, total - most), min(most, total - 1) + 1)
        return jnp.stack([one, total - one])
    tallies = jnp.asarray(split_up(count, total, most, lean), jnp.int32)
    couples = (count - 1) // 2
    giver, receiver = tallies[1:1 + 2 * couples:2], tallies[2:2 + 2 * couples:2]
    room = jnp.minimum(giver - 1, most - receiver)
    passed = jax.random.randint(jax.random.fold_in(stream_key, 1), (couples,), 0, 1 << 20) % (room + 1)
    tallies = tallies.at[1:1 + 2 * couples:2].set(giver - passed).at[2:2 + 2 * couples:2].set(receiver + passed)
    return tallies[jax.random.permutation(jax.random.fold_in(stream_key, 2), count)]


def bell_draw(key, shape, width, reach, split=(), held_as=jnp.bfloat16):
    values = width * jax.random.normal(key, shape, jnp.float32)
    if split:
        values = values * level_of(key, shape, split, -0.22, 0.18)
    return jnp.clip(values, -reach, reach).astype(held_as)


def setup_inputs(seed: int = 0) -> dict:
    keys = jax.random.split(jax.random.key(seed), 16)
    return {
        "hidden": bell_draw(keys[0], (ROWS, LEN, D), 1.0, 6.0, ((0, 4), (1, 8))),
        "cotangent": bell_draw(keys[1], (ROWS, LEN, D), 1.0, 6.0, ((0, 4), (1, 8))),
        "segment_ids": jax.vmap(lambda own: jnp.searchsorted(jnp.cumsum(ragged_sizes(own, DOCS, LEN, DOC_MOST, 1)), jnp.arange(LEN), side="right"))(jax.random.split(keys[2], ROWS)).reshape((ROWS, LEN)).astype(jnp.int32),
        "timesteps": place_ends(jax.random.randint(keys[3], (ROWS, DOCS), 0, TSTEPS), jax.random.fold_in(keys[3], 1), 0, TSTEPS - 1).astype(jnp.int32),
        "qkv_weight": bell_draw(keys[4], (D, 3 * D), D ** -0.5, 0.21875),
        "qv_bias": bell_draw(keys[5], (2 * D,), 0.5, 3.0, (), jnp.float32),
        "out_weight": bell_draw(keys[6], (D, D), (D // 64) ** -0.5, 1.75),
        "out_bias": bell_draw(keys[7], (D,), 0.5, 3.0, (), jnp.float32),
        "up_weight": bell_draw(keys[8], (D, FF), D ** -0.5, 0.21875),
        "up_bias": bell_draw(keys[9], (FF,), 0.5, 3.0, (), jnp.float32),
        "down_weight": bell_draw(keys[10], (FF, D), FF ** -0.5, 0.109375),
        "down_bias": bell_draw(keys[11], (D,), 0.5, 3.0, (), jnp.float32),
        "norm_gain": jnp.clip(1.0 + 0.18 * jax.random.normal(keys[12], (2, D), jnp.float32), 0.1, 1.9),
        "norm_bias": bell_draw(keys[13], (2, D), 0.5, 3.0, (), jnp.float32),
        "time_weight": bell_draw(keys[14], (D, D), D ** -0.5, 0.21875),
    }


EPS = 1e-05
NEG_BIG = -1e+30
precise = lax.Precision.HIGHEST

@jax.custom_vjp
def low(v):
    return lax.optimization_barrier(v.astype(jnp.bfloat16)).astype(jnp.float32)

@jax.custom_vjp
def low_back(v):
    return v

def low_keep(v):
    return (low(v), None)

def low_pass(kept, grad):
    return (grad,)

def back_keep(v):
    return (v, None)

def back_low(kept, grad):
    return (low(grad),)
low.defvjp(low_keep, low_pass)
low_back.defvjp(back_keep, back_low)

def time_features(timesteps):
    half_width = D // 2
    frequency = jnp.exp(jnp.arange(half_width, dtype=jnp.float32) * (-math.log(10000.0) / half_width))
    phases = timesteps.astype(jnp.float32)[..., None] * frequency
    return jnp.concatenate([jnp.sin(phases), jnp.cos(phases)], axis=-1)

def layer_norm(residual, gain_row, offset):
    average = lax.optimization_barrier(jnp.mean(residual, axis=-1, keepdims=True))
    centered = residual - average
    inverse = lax.rsqrt(lax.optimization_barrier(jnp.mean(centered * centered, axis=-1, keepdims=True)) + EPS)
    return centered * inverse * gain_row + offset

def attend_row(row_item):
    q_row, k_row, v_row, seg_row = row_item
    length = q_row.shape[0]
    block_rows = math.gcd(length, 512)
    block_count = length // block_rows
    k_heads = k_row.reshape(length, H, HD)
    v_heads = v_row.reshape(length, H, HD)

    def one_block(block_item):
        q_block, seg_block = block_item
        scores = jnp.einsum('qhd,khd->hqk', q_block, k_heads, precision=precise) * HD ** (-0.5)
        scores = low_back(scores)
        same_doc = seg_block[:, None] == seg_row[None, :]
        scores = jnp.where(same_doc[None], scores, NEG_BIG)
        probabilities = jax.nn.softmax(scores, axis=-1)
        mixture = jnp.einsum('hqk,khd->qhd', low(probabilities), v_heads, precision=precise)
        return mixture.reshape(block_rows, D)
    blocks = lax.map(jax.checkpoint(one_block), (q_row.reshape(block_count, block_rows, H, HD), seg_row.reshape(block_count, block_rows)))
    return blocks.reshape(length, D)

def layer_forward(segment_ids, timesteps, hidden, qkv_weight, qv_bias, out_weight, out_bias, up_weight, up_bias, down_weight, down_bias, norm_gain, norm_bias, time_weight):
    features = low(time_features(timesteps))
    doc_embed = jnp.einsum('rkd,de->rke', features, time_weight, precision=precise)
    onehot = (segment_ids[..., None] == jnp.arange(DOCS, dtype=jnp.int32)).astype(jnp.float32)
    inputs = hidden + jnp.einsum('rsk,rke->rse', onehot, doc_embed, precision=precise)
    inputs_low = low(inputs)
    projected = jnp.einsum('rsd,de->rse', inputs_low, qkv_weight, precision=precise)
    queries = low_back(low(projected[..., :D] + qv_bias[:D]))
    keys_all = low_back(low(projected[..., D:2 * D]))
    values = low_back(low(projected[..., 2 * D:] + qv_bias[D:]))
    attended = lax.map(attend_row, (queries, keys_all, values, segment_ids))
    attended = low_back(low(attended))
    branch = low_back(jnp.einsum('rsd,de->rse', attended, out_weight, precision=precise) + out_bias)
    normed_one = layer_norm(inputs + branch, norm_gain[0], norm_bias[0])
    up_values = low_back(jnp.einsum('rsd,df->rsf', low(normed_one), up_weight, precision=precise) + up_bias)
    activated = low(jax.nn.gelu(up_values, approximate=False))
    ffn_out = low_back(jnp.einsum('rsf,fd->rsd', activated, down_weight, precision=precise) + down_bias)
    return layer_norm(normed_one + ffn_out, norm_gain[1], norm_bias[1])

def reference(hidden, cotangent, segment_ids, timesteps, qkv_weight, qv_bias, out_weight, out_bias, up_weight, up_bias, down_weight, down_bias, norm_gain, norm_bias, time_weight):
    floats = tuple((weight_item.astype(jnp.float32) for weight_item in (hidden, qkv_weight, qv_bias, out_weight, out_bias, up_weight, up_bias, down_weight, down_bias, norm_gain, norm_bias, time_weight)))
    output, pullback = jax.vjp(partial(layer_forward, segment_ids, timesteps), *floats)
    gradients = pullback(cotangent.astype(jnp.float32))
    return (output.astype(jnp.bfloat16), gradients[0], gradients[1], gradients[2], gradients[3], gradients[4], gradients[5], gradients[6], gradients[7], gradients[8], gradients[9], gradients[10], gradients[11])
```

```python
import functools
import math

import jax
import jax.numpy as jnp
from jax import lax
from jax.experimental import pallas as pl
from jax.experimental.pallas import tpu as pltpu
from jax.sharding import PartitionSpec as P

D = 768
H = 12
HD = 64
FF = 3072
DOCS = 16
PAIR = 2 * HD
PAIRS = D // PAIR
Z_STEPS = 4
SUMS = 16

EPS = 1e-05
MASKED = -1e30
BF = jnp.bfloat16
F32 = jnp.float32
precise = lax.Precision.HIGHEST
VMEM = pl.BlockSpec(memory_space=pltpu.VMEM)


def swap(block, axis, bit):
    return lax.ppermute(block, axis, [(i, i ^ bit) for i in range(lax.axis_size(axis))])


def dot(a, b, dims):
    return lax.dot_general(a, b, (dims, ((), ())), preferred_element_type=F32)


def nn(a, b):
    return dot(a, b, ((1,), (0,)))


def nt(a, b):
    return dot(a, b, ((1,), (1,)))


def tn(a, b):
    return dot(a, b, ((0,), (0,)))


def call(kernel, name, ins, outs, scratch=(), vmem=16):
    return pl.pallas_call(
        kernel,
        out_shape=tuple(jax.ShapeDtypeStruct(*one) for one in outs),
        in_specs=[VMEM] * len(ins),
        out_specs=tuple([VMEM] * len(outs)),
        scratch_shapes=[pltpu.VMEM(*one) for one in scratch],
        compiler_params=pltpu.CompilerParams(vmem_limit_bytes=vmem << 20),
        name=name,
    )(*ins)


def at_rows(index, size):
    return pl.ds(pl.multiple_of(index * size, 8), size)


def at_lanes(index, size):
    return pl.ds(pl.multiple_of(index * size, 128), size)


def time_features(timesteps):
    half_width = D // 2
    frequency = jnp.exp(
        jnp.arange(half_width, dtype=F32) * (-math.log(10000.0) / half_width)
    )
    phases = timesteps.astype(F32)[..., None] * frequency
    return jnp.concatenate([jnp.sin(phases), jnp.cos(phases)], axis=-1)


def gather_seq(block):
    size = lax.axis_size("seq")
    inner = size // Z_STEPS
    found = [None] * size
    for far in range(Z_STEPS):
        found[far * inner] = block if far == 0 else swap(block, "seq", far * inner)
    for far in range(Z_STEPS):
        for near in range(1, inner):
            found[far * inner + near] = swap(found[far * inner], "seq", near)
    return found


def split2(value):
    high = value.astype(BF)
    return high, (value - high.astype(F32)).astype(BF)


def split3(value):
    high = value.astype(BF)
    rest = value - high.astype(F32)
    middle = rest.astype(BF)
    low = (rest - middle.astype(F32)).astype(BF)
    return high, middle, low


def head_start(seq, share):
    return jnp.minimum(seq * share // HD, H - 2) * HD


def heads_kernel(share, qkv_ref, bias_ref, w_ref, b_ref):
    start = head_start(lax.axis_index("seq"), share)
    base = jnp.minimum(start // PAIR, PAIRS - 2) * PAIR
    back = (2 * PAIR - (start - base)) % (2 * PAIR)
    for kind in range(3):
        cols = pl.ds(pl.multiple_of(base + kind * D, PAIR), 2 * PAIR)
        here = slice(kind * PAIR, (kind + 1) * PAIR)
        w_ref[:, here] = pltpu.roll(qkv_ref[:, cols].astype(F32), back, 1)[:, :PAIR].astype(BF)
        if kind == 1:
            b_ref[:, here] = jnp.zeros((1, PAIR), F32)
        else:
            cols = pl.ds(pl.multiple_of(base + (kind // 2) * D, PAIR), 2 * PAIR)
            bias = jnp.broadcast_to(bias_ref[:, cols], (8, 2 * PAIR))
            b_ref[:, here] = pltpu.roll(bias, back, 1)[:1, :PAIR]


def attend_kernel(count, *refs):
    shards = refs[:count]
    embed_ref, qkv_ref, bias_ref = refs[count : count + 3]
    x_ref, xlow_ref, q_ref, k_ref, v_ref, attn_ref, lse_ref, hot_ref = refs[count + 3 : count + 11]
    mask_ref = refs[count + 11]
    seq = lax.axis_index("seq")
    rows = attn_ref.shape[0]
    embed = jnp.concatenate(split3(embed_ref[...]), axis=0)
    places = lax.broadcasted_iota(jnp.int32, (DOCS, rows), 0).astype(F32)
    hot_own = None
    for at in range(count):
        ids = shards[at][rows : rows + 8, :rows].astype(F32)[:1]
        hot = (places == ids).astype(BF)
        hot_ref[:, at_lanes(seq ^ at, rows)] = hot
        x = shards[at][:rows, :].astype(F32) + tn(jnp.concatenate([hot] * 3, axis=0), embed)
        if at == 0:
            hot_own = hot
            x_ref[...] = x
            own = x.astype(BF)
        xlow_ref[at_rows(seq ^ at, rows), :] = x.astype(BF)
    q_ref[...] = (
        (nn(own, qkv_ref[:, :D]) + bias_ref[:, :D]).astype(BF).astype(F32) * (HD**-0.5)
    ).astype(BF)
    step = 2 * rows
    for at in range(count * rows // step):
        piece = slice(at * step, (at + 1) * step)
        every = xlow_ref[piece, :]
        k_ref[piece, :] = nn(every, qkv_ref[:, D : 2 * D]).astype(BF)
        v_ref[piece, :] = (nn(every, qkv_ref[:, 2 * D :]) + bias_ref[:, D:]).astype(BF)
    mask_ref[...] = (tn(hot_own, hot_ref[...]) - 1.0) * -MASKED
    first = lax.broadcasted_iota(jnp.int32, (rows, PAIR), 1) < HD
    lane = lax.broadcasted_iota(jnp.int32, (rows, 128), 1)
    lse = jnp.zeros((rows, 128), F32)
    for pair in range(PAIRS):
        cols = slice(pair * PAIR, (pair + 1) * PAIR)
        q = q_ref[:, cols]
        halves = []
        for half in range(2):
            q_one = jnp.where(first if half == 0 else ~first, q, jnp.zeros_like(q))
            scores = nt(q_one, k_ref[:, cols]) + mask_ref[...]
            top = jnp.max(scores, axis=-1, keepdims=True)
            weights = jnp.exp(scores - top)
            total = jnp.sum(weights, axis=-1, keepdims=True)
            halves.append(nn(weights.astype(BF), v_ref[:, cols]) / total)
            lse = jnp.where(lane == 2 * pair + half, top + jnp.log(total), lse)
        attn_ref[:, cols] = jnp.where(first, halves[0], halves[1]).astype(BF)
    lse_ref[...] = lse


def normalize(value):
    centered = value - jnp.mean(value, axis=-1, keepdims=True)
    inverse = lax.rsqrt(jnp.mean(centered * centered, axis=-1, keepdims=True) + EPS)
    return centered * inverse, inverse


def normalize_back(z, inverse, grad):
    return inverse * (
        grad
        - jnp.mean(grad, axis=-1, keepdims=True)
        - z * jnp.mean(grad * z, axis=-1, keepdims=True)
    )


def total(value):
    return jnp.sum(value, axis=0, keepdims=True)


def gelu_parts(u):
    phi = 0.5 * (1.0 + lax.erf(u * math.sqrt(0.5)))
    return phi, phi + u * (jnp.exp(-0.5 * u * u) * (1.0 / math.sqrt(2.0 * math.pi)))


def chain_kernel(
    starts,
    x_ref, attn_ref, cot_ref, hot_ref, wo_ref, bo_ref, up_ref, bu_ref, down_ref, bd_ref, gain_ref,
    off_ref,
    result_ref, ydf_ref, ado_ref, dr1_ref, da_ref, packed_ref, docs_ref,
    slope_ref, sums_ref,
):
    rows = x_ref.shape[0]
    attn = attn_ref[...]
    r1 = x_ref[...] + nn(attn, wo_ref[...]) + bo_ref[...]
    z1, inverse1 = normalize(r1)
    y1 = z1 * gain_ref[0:1, :] + off_ref[0:1, :]
    y1_low = y1.astype(BF)
    ydf_ref[:rows, :D] = y1_low
    ado_ref[:, :D] = attn
    r2 = y1 + bd_ref[...]
    width = D
    for at in range(FF // width):
        cols = slice(at * width, (at + 1) * width)
        u = nn(y1_low, up_ref[:, cols]) + bu_ref[:, cols]
        phi, slope = gelu_parts(u)
        slope_ref[:, cols] = slope
        r2 = r2 + nn((u * phi).astype(BF), down_ref[cols, :])
    z2, inverse2 = normalize(r2)
    result_ref[...] = (z2 * gain_ref[1:2, :] + off_ref[1:2, :]).astype(BF)
    cot = cot_ref[...].astype(F32)
    dr2 = normalize_back(z2, inverse2, cot * gain_ref[1:2, :])
    df_low = dr2.astype(BF)
    ydf_ref[:rows, D:] = df_low
    dy1 = dr2
    for at in range(FF // width):
        cols = slice(at * width, (at + 1) * width)
        du_low = (nt(df_low, down_ref[cols, :]) * slope_ref[:, cols]).astype(BF)
        sums_ref[6 + at : 7 + at, :] = total(du_low.astype(F32))
        dy1 = dy1 + nt(du_low, up_ref[:, cols])
    dr1 = normalize_back(z1, inverse1, dy1 * gain_ref[0:1, :])
    dr1_ref[...] = dr1
    do_low = dr1.astype(BF)
    ado_ref[:, D:] = do_low
    da = nt(do_low, wo_ref[...])
    da_ref[...] = da.astype(BF)
    for at, start in enumerate(starts):
        packed_ref[at * rows : (at + 1) * rows, :] = da[:, start : start + PAIR].astype(BF)
    hot = hot_ref[:, at_lanes(lax.axis_index("seq"), rows)]
    high, middle, low = split3(dr1)
    docs_ref[...] = nn(hot, high) + nn(hot, middle) + nn(hot, low)
    sums_ref[0:1, :] = total(dy1 * z1)
    sums_ref[1:2, :] = total(cot * z2)
    sums_ref[2:3, :] = total(dy1)
    sums_ref[3:4, :] = total(cot)
    sums_ref[4:5, :] = total(do_low.astype(F32))
    sums_ref[5:6, :] = total(df_low.astype(F32))
    sums_ref[6 + FF // width :, :] = jnp.zeros((SUMS - 6 - FF // width, D), F32)
    high, low = split2(sums_ref[...])
    ydf_ref[rows:, :D] = high
    ydf_ref[rows:, D:] = low


def query_grad_kernel(q_ref, k_ref, v_ref, da_ref, lse_ref, hot_ref, dq_ref, mask_ref):
    rows = q_ref.shape[0]
    hot = hot_ref[:, at_lanes(lax.axis_index("seq"), rows)]
    mask_ref[...] = (tn(hot, hot_ref[...]) - 1.0) * -MASKED
    first = lax.broadcasted_iota(jnp.int32, (rows, PAIR), 1) < HD
    lane = lax.broadcasted_iota(jnp.int32, (rows, 128), 1)
    for pair in range(PAIRS):
        cols = slice(pair * PAIR, (pair + 1) * PAIR)
        q, da = q_ref[:, cols], da_ref[:, cols]
        halves = []
        for half in range(2):
            here = first if half == 0 else ~first
            scores = nt(jnp.where(here, q, jnp.zeros_like(q)), k_ref[:, cols]) + mask_ref[...]
            lse = jnp.sum(jnp.where(lane == 2 * pair + half, lse_ref[...], 0.0), -1, keepdims=True)
            probs = jnp.exp(scores - lse)
            dprobs = nt(jnp.where(here, da, jnp.zeros_like(da)), v_ref[:, cols])
            delta = jnp.sum(probs * dprobs, axis=-1, keepdims=True)
            ds = (probs * (dprobs - delta)).astype(BF)
            halves.append(nn(ds, k_ref[:, cols]))
        dq_ref[:, cols] = (jnp.where(first, halves[0], halves[1]) * (HD**-0.5)).astype(BF)


def head_grad_kernel(
    step, share, split, x_ref, w_ref, b_ref, da_ref, hot_ref, docs_ref, *refs
):
    if split:
        back_ref, *sent, mine_ref = refs[: split + 1]
        refs = refs[split + 1 :]
    else:
        back_ref, whole_ref, bias_ref = refs[:3]
        refs = refs[3:]
    q_ref, k_ref, v_ref, dq_ref, dk_ref, dv_ref, heads_ref, grad_ref = refs
    length = x_ref.shape[0]
    seq = lax.axis_index("seq")
    for at in range(length // step):
        piece = slice(at * step, (at + 1) * step)
        all_three = nn(x_ref[piece, :], w_ref[...]) + b_ref[...]
        q_ref[piece, :] = (
            all_three[:, :PAIR].astype(BF).astype(F32) * (HD**-0.5)
        ).astype(BF)
        k_ref[piece, :] = all_three[:, PAIR : 2 * PAIR].astype(BF)
        v_ref[piece, :] = all_three[:, 2 * PAIR :].astype(BF)
    first = lax.broadcasted_iota(jnp.int32, (step, PAIR), 1) < HD
    for at in range(length // step):
        piece = slice(at * step, (at + 1) * step)
        mask = (tn(hot_ref[:, piece], hot_ref[...]) - 1.0) * -MASKED
        halves = []
        for half in range(2):
            here = first if half == 0 else ~first
            q = jnp.where(here, q_ref[piece, :], jnp.zeros((step, PAIR), BF))
            da = jnp.where(here, da_ref[piece, :], jnp.zeros((step, PAIR), BF))
            scores = nt(q, k_ref[...]) + mask
            weights = jnp.exp(scores - jnp.max(scores, axis=-1, keepdims=True))
            probs = weights / jnp.sum(weights, axis=-1, keepdims=True)
            dprobs = nt(da, v_ref[...])
            delta = jnp.sum(probs * dprobs, axis=-1, keepdims=True)
            ds = (probs * (dprobs - delta)).astype(BF)
            halves.append(nn(ds, k_ref[...]))
            dk, dv = tn(ds, q), tn(probs.astype(BF), da)
            if at == 0 and half == 0:
                dk_ref[...], dv_ref[...] = dk, dv
            else:
                dk_ref[...] += dk
                dv_ref[...] += dv
        dq_ref[piece, :] = jnp.where(first, halves[0], halves[1]) * (HD**-0.5)
    offset = seq * share - head_start(seq, share)
    left = (PAIR - offset) % PAIR
    for at in range(length // step):
        piece = slice(at * step, (at + 1) * step)
        heads_ref[piece, :] = jnp.concatenate(
            [pltpu.roll(ref[piece, :], left, 1)[:, :share] for ref in (dq_ref, dk_ref, dv_ref)],
            axis=1,
        ).astype(BF)
    doc_sums = nn(hot_ref[...], heads_ref[...])
    docs = docs_ref[...]
    for kind in range(3):
        piece = doc_sums[:, kind * share : (kind + 1) * share]
        piece = jnp.concatenate([piece, jnp.zeros((DOCS, PAIR - share), F32)], axis=1)
        parts = jnp.concatenate(split3(pltpu.roll(piece, offset, 1)), axis=0)
        product = nt(parts, w_ref[:, kind * PAIR : (kind + 1) * PAIR])
        docs = docs + (product[:DOCS] + product[DOCS : 2 * DOCS] + product[2 * DOCS :])
    high, low = split2(docs)
    wide = 2 * share
    rows = length // (D // share)
    for at in range(D // share):
        back_ref[at, :rows, :] = heads_ref[at * rows : (at + 1) * rows, share:]
        for part, value in enumerate((high, low)):
            for col in range(D // wide):
                here = rows + (part * (D // wide) + col) * DOCS
                back_ref[at, here : here + DOCS, :] = value[:, col * wide : (col + 1) * wide]
    grad_ref[...] = tn(x_ref[...], heads_ref[...])
    sums = total(doc_sums)
    if not split:
        whole_ref[...] = grad_ref[...]
        bias_ref[...] = sums
        return
    rank = lax.axis_index("rows")
    part = share // split
    high, low = split2(jnp.broadcast_to(sums, (8, 3 * share)))
    row = lax.broadcasted_iota(jnp.int32, (8, 3 * share), 0)
    tail = jnp.where(row == 0, high.astype(F32), jnp.where(row == 1, low.astype(F32), 0.0))
    for to, ref in enumerate([mine_ref] + list(sent)):
        for at in range(D // share):
            here = pl.ds(pl.multiple_of(at * share + (rank ^ to) * part, 8), part)
            ref[at, :part, :] = grad_ref[here, :].astype(ref.dtype)
            ref[at, part:, :] = tail.astype(ref.dtype)


def head_grad(x_low, weight, bias, da, hot, docs, share, split):
    length = x_low.shape[0]
    count = D // share
    rows = length // count
    outs = [((count, rows + 2 * DOCS * D // (2 * share), 2 * share), BF)]
    if split:
        block = (count, share // split + 8, 3 * share)
        outs += [(block, BF)] * (split - 1) + [(block, F32)]
    else:
        outs += [((D, 3 * share), F32), ((1, 3 * share), F32)]
    scratch = [((length, PAIR), BF)] * 3 + [((length, PAIR), F32)] * 3
    scratch += [((length, 3 * share), BF), ((D, 3 * share), F32)]
    return call(
        functools.partial(head_grad_kernel, 256, share, split),
        "head_grad",
        (x_low, weight, bias, da, hot, docs),
        outs,
        scratch,
        24,
    )


def input_grad_kernel(share, back_ref, dr1_ref, dq_ref, qkv_ref, grad_ref, docs_ref):
    rows = dr1_ref.shape[0]
    wide = 2 * share
    count = D // share
    result = dr1_ref[...] + nt(dq_ref[...], qkv_ref[:, :D])
    dk = jnp.concatenate([back_ref[at, :rows, :share] for at in range(count)], axis=1)
    dv = jnp.concatenate([back_ref[at, :rows, share:] for at in range(count)], axis=1)
    result = result + nt(dk, qkv_ref[:, D : 2 * D]) + nt(dv, qkv_ref[:, 2 * D :])
    grad_ref[...] = result
    docs = jnp.zeros((back_ref.shape[1] - rows, wide), F32)
    for at in range(count):
        docs = docs + back_ref[at, rows:, :].astype(F32)
    half = docs.shape[0] // 2
    docs = docs[:half] + docs[half:]
    docs_ref[...] = jnp.concatenate(
        [docs[at * DOCS : (at + 1) * DOCS] for at in range(D // wide)], axis=1
    )


def part_weights_kernel(up_ref, bu_ref, down_ref, up_out, bu_out, down_out):
    rank = lax.axis_index("rows")
    back = (384 - rank * 96) % 384
    ups, biases = [], []
    for at in range(8):
        share = 2 * (at % 4) + at // 4
        cols = slice(share * 384, (share + 1) * 384)
        ups.append(pltpu.roll(up_ref[:, cols].astype(F32), back, 1)[:, :96])
        bias = jnp.broadcast_to(bu_ref[:, cols], (8, 384))
        biases.append(pltpu.roll(bias, back, 1)[:1, :96])
        down_out[at * 96 : (at + 1) * 96, :] = down_ref[
            pl.ds(pl.multiple_of(share * 384 + rank * 96, 16), 96), :
        ]
    up_out[...] = jnp.concatenate(ups, axis=1).astype(BF)
    bu_out[...] = jnp.concatenate(biases, axis=1)


def feed_grad_kernel(*refs):
    pieces = refs[:8]
    up_ref, bu_ref, down_ref = refs[8:11]
    own_ref, one_ref, two_ref, three_ref, sums_ref = refs[11:16]
    y1_ref, df_ref, g_ref, du_ref, up_grad_ref, down_grad_ref = refs[16:]
    seq = lax.axis_index("seq")
    near, far = seq % 2, seq // 2
    rows = pieces[0].shape[0] - SUMS
    sums = jnp.zeros((SUMS, D), F32)
    for at, piece in enumerate(pieces):
        here = slice(at * rows, (at + 1) * rows)
        y1_ref[here, :] = piece[:rows, :D]
        df_ref[here, :] = piece[:rows, D:]
        sums = sums + (piece[rows:, :D].astype(F32) + piece[rows:, D:].astype(F32))
    sums_ref[...] = sums
    step = 2 * rows
    for at in range(4):
        here = slice(at * step, (at + 1) * step)
        u = nn(y1_ref[here, :], up_ref[...]) + bu_ref[...]
        phi, slope = gelu_parts(u)
        g_ref[here, :] = (u * phi).astype(BF)
        du_ref[here, :] = (nt(df_ref[here, :], down_ref[...]) * slope).astype(BF)
    down_grad_ref[...] = tn(g_ref[:, at_lanes(near, 384)], df_ref[...])
    up_grad_ref[...] = tn(y1_ref[...], du_ref[...])
    for to, ref in enumerate((own_ref, one_ref, two_ref, three_ref)):
        z = far ^ to
        up_rows = pl.ds(pl.multiple_of((2 * z + near) * 96, 8), 96)
        ref[:, :D] = up_grad_ref[up_rows, :].astype(ref.dtype)
        ref[:, D:] = down_grad_ref[pl.ds(pl.multiple_of(z * 96, 8), 96), :].astype(ref.dtype)


def feed_grad(pieces, up, bias, down):
    tokens = 8 * (pieces[0].shape[0] - SUMS)
    block = (96, 2 * D)
    return call(
        feed_grad_kernel,
        "feed_grad",
        (*pieces, up, bias, down),
        [(block, F32), (block, BF), (block, BF), (block, BF), ((SUMS, D), F32)],
        [((tokens, D), BF)] * 4 + [((D, D), F32), ((384, D), F32)],
        28,
    )


def out_grad_kernel(*refs):
    pieces = refs[:8]
    own_ref, one_ref, two_ref, three_ref = refs[9:13]
    sums_in = refs[8]
    attn_ref, do_ref, grad_ref = refs[13:]
    seq, rank = lax.axis_index("seq"), lax.axis_index("rows")
    near, far = seq % 2, seq // 2
    rows = pieces[0].shape[0]
    base = rank * 192 // 128 * 128
    back = (256 - (rank * 192 - base)) % 256
    for at, piece in enumerate(pieces):
        here = slice(at * rows, (at + 1) * rows)
        attn_ref[here, :] = piece[:, :D]
        do_ref[here, :] = piece[:, pl.ds(pl.multiple_of(D + base, 128), 256)]
    grad_ref[...] = pltpu.roll(tn(attn_ref[...], do_ref[...]), back, 1)
    high, low = split2(sums_in[...])
    for to, ref in enumerate((own_ref, one_ref, two_ref, three_ref)):
        here = pl.ds(pl.multiple_of((2 * (far ^ to) + near) * 96, 8), 96)
        ref[:96, :] = grad_ref[here, :192].astype(ref.dtype)
        for part, value in enumerate((high, low)):
            for col in range(4):
                at = 96 + (part * 4 + col) * SUMS
                ref[at : at + SUMS, :] = value[:, col * 192 : (col + 1) * 192].astype(ref.dtype)


def out_grad(pieces, sums):
    rows = pieces[0].shape[0]
    block = (96 + 8 * SUMS, 192)
    return call(
        out_grad_kernel,
        "out_grad",
        (*pieces, sums),
        [(block, F32), (block, BF), (block, BF), (block, BF)],
        [((8 * rows, D), BF), ((8 * rows, 256), BF), ((D, 256), F32)],
        16,
    )


def finish_feed_kernel(a_ref, b_ref, c_ref, d_ref, up_ref, down_ref, held_ref):
    rank = lax.axis_index("rows")
    for at, ref in enumerate((a_ref, b_ref, c_ref, d_ref)):
        value = ref[...].astype(F32)
        held_ref[rank ^ at] = value[:, :D]
        down_ref[pl.ds(pl.multiple_of((rank ^ at) * 96, 8), 96), :] = value[:, D:]
    for share in range(8):
        at = (share // 2) + 4 * (share % 2)
        up_ref[:, share * 384 : (share + 1) * 384] = jnp.concatenate(
            [held_ref[r, :, at * 96 : (at + 1) * 96] for r in range(4)], axis=1
        )


def finish_out_kernel(a_ref, b_ref, c_ref, d_ref, out_ref, held_ref):
    rank = lax.axis_index("rows")
    for at, ref in enumerate((a_ref, b_ref, c_ref, d_ref)):
        held_ref[rank ^ at] = ref[...].astype(F32)
    out_ref[...] = jnp.concatenate([held_ref[r] for r in range(4)], axis=1)


def finish_heads_kernel(a_ref, b_ref, c_ref, d_ref, out_ref, bias_ref):
    rank = lax.axis_index("rows")
    order = [(kind, at) for kind in range(3) for at in range(8)]
    for to, ref in enumerate((a_ref, b_ref, c_ref, d_ref)):
        value = jnp.concatenate(
            [ref[at, :24, kind * 96 : (kind + 1) * 96].astype(F32) for kind, at in order], axis=1
        )
        out_ref[pl.ds(pl.multiple_of((rank ^ to) * 24, 8), 24), :] = value
    tail = jnp.concatenate(
        [a_ref[at, 24:, kind * 96 : (kind + 1) * 96].astype(F32) for kind, at in order], axis=1
    )
    bias_ref[...] = tail[0:1] + tail[1:2]


def combine_kernel(tail, own_ref, a_ref, b_ref, c_ref, out_ref):
    value = own_ref[...]
    for ref in (a_ref, b_ref, c_ref):
        value = value + ref[...].astype(F32)
    if tail:
        count, rows, wide = value.shape
        out_ref[:, : rows - 8, :] = value[:, : rows - 8].astype(out_ref.dtype)
        row = lax.broadcasted_iota(jnp.int32, (8, wide), 0)
        for at in range(count):
            last = value[at, rows - 8 :]
            high, low = split2(jnp.broadcast_to(last[0:1] + last[1:2], (8, wide)))
            out_ref[at, rows - 8 :, :] = jnp.where(
                row == 0, high.astype(F32), jnp.where(row == 1, low.astype(F32), 0.0)
            ).astype(out_ref.dtype)
    else:
        out_ref[...] = value.astype(out_ref.dtype)


def combine(blocks, dtype, tail=False):
    return call(
        functools.partial(combine_kernel, tail), "combine", blocks, [(blocks[0].shape, dtype)]
    )[0]


def spread_rows(block):
    across = swap(block, "rows", 2)
    return block, swap(block, "rows", 1), across, swap(across, "rows", 1)


def pick(blocks, index, axis=0):
    return lax.dynamic_index_in_dim(blocks, index, axis, keepdims=False)


def reduce_rows(blocks, place):
    bit = 1
    while blocks.shape[0] > 1:
        pairs = blocks.reshape((blocks.shape[0] // 2, 2) + blocks.shape[1:])
        mine = (place // bit) % 2
        sent = swap(pick(pairs, 1 - mine, 1).astype(BF), "rows", bit)
        blocks = pick(pairs, mine, 1).astype(F32) + sent.astype(F32)
        bit *= 2
    return blocks[0]


def gather_rows(block, place):
    count = lax.axis_size("rows")
    found = block[None]
    bit = count // 2
    while bit >= 1:
        other = swap(found, "rows", bit)
        mine = (place // bit) % 2
        low, high = jnp.where(mine == 0, found, other), jnp.where(mine == 0, other, found)
        if bit == count // 2:
            found = jnp.concatenate([low, high], axis=0)
        else:
            found = jnp.stack([low, high], axis=1).reshape((-1,) + block.shape)
        bit //= 2
    return found


def general_grads(ydf, ado, grad_heads, head_sums, up_weight, up_bias, down_weight):
    seqs, ranks = lax.axis_size("seq"), lax.axis_size("rows")
    seq, rank = lax.axis_index("seq"), lax.axis_index("rows")
    inner = seqs // Z_STEPS
    near = seq % inner
    share = D // seqs
    ff_share = FF // seqs
    ff_part = ff_share // ranks
    rows = ydf.shape[0] - SUMS

    part = share // ranks
    grad_heads = grad_heads.reshape(seqs, ranks, part, 3 * share)
    mine = reduce_rows(jnp.moveaxis(grad_heads, 1, 0), rank)
    spread = lax.all_to_all(mine.astype(BF), "seq", 0, 0, tiled=True)
    columns = [
        spread[i, :, kind * share : (kind + 1) * share] for kind in range(3) for i in range(seqs)
    ]
    quarter = jnp.concatenate(columns, axis=1)
    grad_qkv = gather_rows(quarter, rank).reshape(share, 3 * D).astype(F32)

    def gather_near(block):
        found = [block]
        bit = 2
        while bit < ranks:
            found = found + [swap(one, "rows", bit) for one in found]
            bit *= 2
        for step in range(1, inner):
            found = found + [swap(one, "seq", step) for one in found[: len(found) // step]]
        mine = jnp.concatenate(found, axis=0)
        return jnp.concatenate([mine, swap(mine, "rows", 1)], axis=0)

    ydf_all = gather_near(ydf[:rows])
    y1_all, df_all = ydf_all[:, :D], ydf_all[:, D:]
    order = [far * inner + i for i in range(inner) for far in range(Z_STEPS)]
    ff_starts = [i * ff_share + rank * ff_part for i in order]
    take = lambda array, axis: jnp.concatenate(
        [lax.dynamic_slice_in_dim(array, a, ff_part, axis) for a in ff_starts], axis=axis
    )
    up_mine, down_mine, bias_mine = take(up_weight, 1), take(down_weight, 0), take(up_bias, 0)
    u = nn(y1_all, up_mine) + bias_mine
    phi, slope = gelu_parts(u)
    du_all = (nt(df_all, down_mine) * slope).astype(BF)
    g_all = (u * phi).astype(BF)
    group = Z_STEPS * ff_part
    g_near = lax.dynamic_slice_in_dim(g_all, near * group, group, 1)
    grad_down = tn(g_near, df_all).reshape(Z_STEPS, ff_part, D)
    grad_up = pick(tn(y1_all, du_all).reshape(Z_STEPS, inner, share, seqs * ff_part), near, 1)
    ado, grad_up, grad_down = lax.optimization_barrier((ado, grad_up, grad_down))
    ado_all = gather_near(ado)
    attn_all, do_all = ado_all[:, :D], ado_all[:, D:]
    out_part = D // ranks
    do_mine = lax.dynamic_slice_in_dim(do_all, rank * out_part, out_part, 1)
    grad_out = pick(tn(attn_all, do_mine).reshape(Z_STEPS, inner, share, out_part), near, 1)

    def reduce_far(blocks):
        blocks = blocks.astype(BF)
        far = seq // inner
        summed = pick(blocks, far).astype(F32)
        for step in range(1, Z_STEPS):
            summed = summed + swap(pick(blocks, far ^ step), "seq", step * inner).astype(F32)
        return gather_rows(summed.astype(BF), rank)

    grad_down = reduce_far(grad_down).reshape(ff_share, D).astype(F32)
    grad_up = reduce_far(grad_up).reshape(ranks, share, inner, Z_STEPS, ff_part)
    grad_up = jnp.transpose(grad_up, (1, 3, 2, 0, 4)).reshape(share, FF).astype(F32)
    grad_out = jnp.transpose(reduce_far(grad_out), (1, 0, 2)).reshape(share, D).astype(F32)

    sums = ydf[rows:, :D].astype(F32) + ydf[rows:, D:].astype(F32)
    placed = lambda kind: lax.dynamic_update_slice_in_dim(
        jnp.zeros((D,), F32), head_sums[0, kind * share : (kind + 1) * share], seq * share, 0
    )
    sums = sums.at[10].set(placed(0)).at[11].set(placed(2))
    for axis, count in (("rows", ranks), ("seq", seqs)):
        bit = 1
        while bit < count:
            sums = sums + swap(sums, axis, bit)
            bit *= 2
    return grad_qkv, sums[10:12].reshape(-1), grad_out, grad_up, grad_down, sums


def body(
    hidden, cotangent, segment_ids, timesteps, qkv_weight, qv_bias, out_weight, out_bias,
    up_weight, up_bias, down_weight, down_bias, norm_gain, norm_bias, time_weight,
):
    assert hidden.shape[0] == 1
    rows = hidden.shape[1]
    seqs, ranks = lax.axis_size("seq"), lax.axis_size("rows")
    length = seqs * rows
    seq, rank = lax.axis_index("seq"), lax.axis_index("rows")
    share = D // seqs
    fast = seqs == 8 and ranks == 4

    ids = jnp.pad(segment_ids.astype(BF), ((0, 7), (0, D - rows)))
    shards = gather_seq(jnp.concatenate([hidden[0], ids], axis=0))

    features = time_features(timesteps[0]).astype(BF)
    embed = nn(features, time_weight)
    all_features = gather_rows(features, rank)
    all_features = lax.dynamic_slice_in_dim(all_features, seq * share, share, 2)
    qv_row, up_row = qv_bias.reshape(1, -1), up_bias.reshape(1, -1)
    head_weight, head_bias = call(
        functools.partial(heads_kernel, share),
        "heads",
        (qkv_weight, qv_row),
        [((D, 3 * PAIR), BF), ((1, 3 * PAIR), F32)],
    )
    if fast:
        up_part, bias_part, down_part = call(
            part_weights_kernel,
            "part_weights",
            (up_weight, up_row, down_weight),
            [((D, D), BF), ((1, D), F32), ((D, D), BF)],
        )

    tile = ((rows, D), BF)
    wide = ((length, D), BF)
    x, x_low, q, k, v, attn, lse, hot = call(
        functools.partial(attend_kernel, seqs),
        "attend",
        (*shards, embed, qkv_weight, qv_row),
        [((rows, D), F32), wide, tile, wide, wide, tile, ((rows, 128), F32), ((DOCS, length), BF)],
        [((rows, length), F32)],
    )
    starts = [min(i * share // HD, H - 2) * HD for i in range(seqs)]
    result, ydf, ado, dr1, da_low, packed, docs = call(
        functools.partial(chain_kernel, starts),
        "chain",
        (
            x, attn, cotangent[0], hot, out_weight, out_bias.reshape(1, -1), up_weight, up_row,
            down_weight, down_bias.reshape(1, -1), norm_gain, norm_bias,
        ),
        [
            tile, ((rows + SUMS, 2 * D), BF), ((rows, 2 * D), BF), ((rows, D), F32), tile,
            ((length, PAIR), BF), ((DOCS, D), F32),
        ],
        [((rows, FF), F32), ((SUMS, D), F32)],
    )

    arrived = lax.all_to_all(packed, "seq", 0, 0, tiled=True)
    dq_low = call(
        query_grad_kernel, "query_grad", (q, k, v, da_low, lse, hot), [tile],
        [((rows, length), F32)],
    )[0]
    back, *grads = head_grad(
        x_low, head_weight, head_bias, arrived, hot, docs, share, 4 if fast else 0
    )
    back = lax.all_to_all(back, "seq", 0, 0, tiled=True)
    input_grad, doc_grad = call(
        functools.partial(input_grad_kernel, share),
        "input_grad",
        (back, dr1, dq_low, qkv_weight),
        [((rows, D), F32), ((DOCS, D), F32)],
    )
    doc_grad = gather_rows(doc_grad, rank).reshape(ranks * DOCS, D)
    grad_time_weight = lax.dot_general(
        all_features.reshape(ranks * DOCS, share).astype(F32),
        doc_grad,
        (((0,), (0,)), ((), ())),
        precision=precise,
    )

    if fast:
        *sent, own = grads
        sent = [swap(block, "rows", to + 1) for to, block in enumerate(sent)]
        mine = combine((own, *sent), BF, True)
        spread = lax.all_to_all(mine, "seq", 0, 0, tiled=True)
        grad_qkv_weight, qkv_sums = call(
            finish_heads_kernel, "finish_heads", spread_rows(spread),
            [((share, 3 * D), F32), ((1, 3 * D), F32)],
        )
        qv_sums = jnp.concatenate([qkv_sums[0, :D], qkv_sums[0, 2 * D :]])

        def gather_near(block):
            across = swap(block, "rows", 2)
            found = [block, across, swap(block, "seq", 1), swap(across, "seq", 1)]
            return found + [swap(one, "rows", 1) for one in found]

        own, *sent, sums = feed_grad(gather_near(ydf), up_part, bias_part, down_part)
        sent = [swap(block, "seq", 2 * (to + 1)) for to, block in enumerate(sent)]
        feed = spread_rows(combine((own, *sent), BF))
        grad_up_weight, grad_down_weight = call(
            finish_feed_kernel, "finish_feed", feed,
            [((share, FF), F32), ((FF // seqs, D), F32)], [((4, 96, D), F32)],
        )
        own, *sent = out_grad(gather_near(ado), sums)
        sent = [swap(block, "seq", 2 * (to + 1)) for to, block in enumerate(sent)]
        summed = combine((own, *sent), F32)
        tail = summed[96:].reshape(2, 4, SUMS, 192).sum(0)
        totals = jnp.transpose(tail, (1, 0, 2)).reshape(SUMS, D)
        grad_out_weight = call(
            finish_out_kernel, "finish_out", spread_rows(summed[:96].astype(BF)),
            [((share, D), F32)], [((4, 96, 192), F32)],
        )[0]
    else:
        grad_qkv_weight, qv_sums, grad_out_weight, grad_up_weight, grad_down_weight, totals = (
            general_grads(ydf, ado, *grads, up_weight, up_bias, down_weight)
        )

    def part_of(vector, axis=0):
        size = vector.shape[axis] // seqs
        return lax.dynamic_slice_in_dim(vector, seq * size, size, axis)

    return (
        result[None],
        input_grad[None],
        grad_qkv_weight,
        part_of(qv_sums),
        grad_out_weight,
        part_of(totals[4]),
        grad_up_weight,
        part_of(totals[6 : 6 + FF // D].reshape(-1)),
        grad_down_weight,
        part_of(totals[5]),
        part_of(totals[0:2], 1),
        part_of(totals[2:4], 1),
        grad_time_weight,
    )


def solution(mesh):
    tokens = P("rows", "seq", None)
    whole = P()
    return jax.shard_map(
        body,
        mesh=mesh,
        in_specs=(tokens, tokens, P("rows", "seq"), P("rows", None)) + (whole,) * 11,
        out_specs=(
            tokens,
            tokens,
            P("seq", None),
            P("seq"),
            P("seq", None),
            P("seq"),
            P("seq", None),
            P("seq"),
            P("seq", None),
            P("seq"),
            P(None, "seq"),
            P(None, "seq"),
            P("seq", None),
        ),
        check_vma=False,
    )
```

```python
import functools
import math

import jax
import jax.numpy as jnp
from jax import lax
from jax.experimental import pallas as pl
from jax.experimental.pallas import tpu as pltpu
from jax.sharding import PartitionSpec as P

D = 768
H = 12
HD = 64
FF = 3072
DOCS = 16
PAIR = 2 * HD
PAIRS = D // PAIR
Z_STEPS = 4
SUMS = 16

EPS = 1e-05
MASKED = -1e30
BF = jnp.bfloat16
F32 = jnp.float32
precise = lax.Precision.HIGHEST
VMEM = pl.BlockSpec(memory_space=pltpu.VMEM)


def swap(block, axis, bit):
    return lax.ppermute(block, axis, [(i, i ^ bit) for i in range(lax.axis_size(axis))])


def dot(a, b, dims):
    return lax.dot_general(a, b, (dims, ((), ())), preferred_element_type=F32)


def nn(a, b):
    return dot(a, b, ((1,), (0,)))


def nt(a, b):
    return dot(a, b, ((1,), (1,)))


def tn(a, b):
    return dot(a, b, ((0,), (0,)))


APART = pl.BlockSpec(memory_space=pltpu.HBM)
FAR = "far"


def far(value):
    return FAR, value


def call(kernel, name, ins, outs, scratch=(), vmem=8, copies=0):
    specs = [APART if isinstance(one, tuple) else VMEM for one in ins]
    values = [
        pltpu.with_memory_space_constraint(one[1], pltpu.HBM) if isinstance(one, tuple) else one
        for one in ins
    ]
    held = [pltpu.VMEM(*one) for one in scratch]
    if copies:
        held.append(pltpu.SemaphoreType.DMA((copies,)))
    return pl.pallas_call(
        kernel,
        out_shape=tuple(
            pltpu.HBM(*one[:2]) if one[2:] else jax.ShapeDtypeStruct(*one) for one in outs
        ),
        in_specs=specs,
        out_specs=tuple(APART if one[2:] else VMEM for one in outs),
        scratch_shapes=held,
        compiler_params=pltpu.CompilerParams(vmem_limit_bytes=vmem << 20),
        cost_estimate=pl.CostEstimate(flops=int(COSTS[name] * 1e9), transcendentals=0, bytes_accessed=0),
        name=name,
    )(*values)


def copy(source, target, sems, at):
    moved = pltpu.make_async_copy(source, target, sems.at[at])
    moved.start()
    return moved


def copies(pairs, sems, first):
    return [copy(one, to, sems, first + at) for at, (one, to) in enumerate(pairs)]


def wait(moved):
    for one in moved:
        one.wait()


def at_rows(index, size):
    return pl.ds(pl.multiple_of(index * size, 8), size)


def at_lanes(index, size):
    return pl.ds(pl.multiple_of(index * size, 128), size)


def time_features(timesteps):
    half_width = D // 2
    frequency = jnp.exp(
        jnp.arange(half_width, dtype=F32) * (-math.log(10000.0) / half_width)
    )
    phases = timesteps.astype(F32)[..., None] * frequency
    return jnp.concatenate([jnp.sin(phases), jnp.cos(phases)], axis=-1)


def gather_seq(block):
    size = lax.axis_size("seq")
    inner = size // Z_STEPS
    found = [None] * size
    for far in range(Z_STEPS):
        found[far * inner] = block if far == 0 else swap(block, "seq", far * inner)
    for far in range(Z_STEPS):
        for near in range(1, inner):
            found[far * inner + near] = swap(found[far * inner], "seq", near)
    return found


COSTS = {
    "forward": 12, "backward": 5, "query_grad": 7, "part_weights": 3, "feed_grad": 8,
    "head_grad": 9, "head_weights": 2, "input_grad": 2, "out_grad": 2, "combine": 1, "combine_half": 1,
    "combine_all": 1, "finish_all": 2, "finish_heads": 1, "time_grad": 1,
}


def split2(value):
    high = value.astype(BF)
    return high, (value - high.astype(F32)).astype(BF)


def split3(value):
    high = value.astype(BF)
    rest = value - high.astype(F32)
    middle = rest.astype(BF)
    low = (rest - middle.astype(F32)).astype(BF)
    return high, middle, low


def head_start(seq, share):
    return jnp.minimum(seq * share // HD, H - 2) * HD


def head_window(share):
    start = head_start(lax.axis_index("seq"), share)
    base = jnp.minimum(start // PAIR, PAIRS - 2) * PAIR
    return base, (2 * PAIR - (start - base)) % (2 * PAIR)


def normalize(value):
    centered = value - jnp.mean(value, axis=-1, keepdims=True)
    inverse = lax.rsqrt(jnp.mean(centered * centered, axis=-1, keepdims=True) + EPS)
    return centered * inverse, inverse


def normalize_back(z, inverse, grad):
    return inverse * (
        grad
        - jnp.mean(grad, axis=-1, keepdims=True)
        - z * jnp.mean(grad * z, axis=-1, keepdims=True)
    )


def total(value):
    return jnp.sum(value, axis=0, keepdims=True)


def gelu_parts(u):
    phi = 0.5 * (1.0 + lax.erf(u * math.sqrt(0.5)))
    return phi, phi + u * (jnp.exp(-0.5 * u * u) * (1.0 / math.sqrt(2.0 * math.pi)))


def forward_kernel(count, *refs):
    shards = refs[:count]
    embed_ref, qkv_in, bias_ref, wo_in, bo_ref, gain_ref, off_ref = refs[count : count + 7]
    cot_ref, up_in, bu_ref, down_in, bd_ref = refs[count + 7 : count + 12]
    refs = refs[count + 12 :]
    xlow_out, k_out, v_out, q_out = refs[:4]
    lse_ref, attn_ref, hot_ref, z1_ref, inverse_ref = refs[4:9]
    result_ref, ydf_ref, dr2_ref, slope_ref, z2_sum_ref = refs[9:14]
    mask_ref, x_ref, xlow_ref, k_ref, v_ref, q_ref = refs[14:20]
    qkv_ref, wo_ref, up_ref, down_ref, sems = refs[20:]
    seq = lax.axis_index("seq")
    rows = attn_ref.shape[0]
    width = D
    parts = [slice(at * width, (at + 1) * width) for at in range(FF // width)]
    qkv_loads = copies([(qkv_in.at[:, c], qkv_ref.at[:, c]) for c in parts[:3]], sems, 4)
    wo_load = copy(wo_in, wo_ref, sems, 7)
    up_loads = copies([(up_in.at[:, c], up_ref.at[:, c]) for c in parts], sems, 8)
    down_loads = copies([(down_in.at[c, :], down_ref.at[c, :]) for c in parts], sems, 12)
    embed = jnp.concatenate(split3(embed_ref[...]), axis=0)
    places = lax.broadcasted_iota(jnp.int32, (DOCS, rows), 0).astype(F32)
    hot_own = None
    for at in range(count):
        ids = shards[at][rows : rows + 8, :rows].astype(F32)[:1]
        hot = (places == ids).astype(BF)
        hot_ref[:, at_lanes(seq ^ at, rows)] = hot
        x = shards[at][:rows, :].astype(F32) + tn(jnp.concatenate([hot] * 3, axis=0), embed)
        if at == 0:
            hot_own = hot
            x_ref[...] = x
            own = x.astype(BF)
        xlow_ref[at_rows(seq ^ at, rows), :] = x.astype(BF)
    moved = [copy(xlow_ref, xlow_out, sems, 0)]
    wait(qkv_loads)
    q_ref[...] = (
        (nn(own, qkv_ref[:, :D]) + bias_ref[:, :D]).astype(BF).astype(F32) * (HD**-0.5)
    ).astype(BF)
    moved.append(copy(q_ref, q_out, sems, 1))
    step = 2 * rows
    for at in range(count * rows // step):
        piece = slice(at * step, (at + 1) * step)
        every = xlow_ref[piece, :]
        k_ref[piece, :] = nn(every, qkv_ref[:, D : 2 * D]).astype(BF)
        v_ref[piece, :] = (nn(every, qkv_ref[:, 2 * D :]) + bias_ref[:, D:]).astype(BF)
    moved.append(copy(k_ref, k_out, sems, 2))
    moved.append(copy(v_ref, v_out, sems, 3))
    mask_ref[...] = (tn(hot_own, hot_ref[...]) - 1.0) * -MASKED
    first = lax.broadcasted_iota(jnp.int32, (rows, PAIR), 1) < HD
    lane = lax.broadcasted_iota(jnp.int32, (rows, 128), 1)
    lse = jnp.zeros((rows, 128), F32)
    for pair in range(PAIRS):
        cols = slice(pair * PAIR, (pair + 1) * PAIR)
        q = q_ref[:, cols]
        halves = []
        for half in range(2):
            q_one = jnp.where(first if half == 0 else ~first, q, jnp.zeros_like(q))
            scores = nt(q_one, k_ref[:, cols]) + mask_ref[...]
            top = jnp.max(scores, axis=-1, keepdims=True)
            weights = jnp.exp(scores - top)
            summed = jnp.sum(weights, axis=-1, keepdims=True)
            halves.append(nn(weights.astype(BF), v_ref[:, cols]) / summed)
            lse = jnp.where(lane == 2 * pair + half, top + jnp.log(summed), lse)
        attn_ref[:, cols] = jnp.where(first, halves[0], halves[1])
    lse_ref[...] = lse
    wo_load.wait()
    z1, inverse = normalize(x_ref[...] + nn(attn_ref[...].astype(BF), wo_ref[...]) + bo_ref[...])
    z1_ref[...] = z1
    inverse_ref[...] = jnp.broadcast_to(inverse, (rows, 128))
    y1 = z1 * gain_ref[0:1, :] + off_ref[0:1, :]
    y1_low = y1.astype(BF)
    ydf_ref[:, :D] = y1_low
    r2 = y1 + bd_ref[...]
    for at, cols in enumerate(parts):
        up_loads[at].wait()
        down_loads[at].wait()
        u = nn(y1_low, up_ref[:, cols]) + bu_ref[:, cols]
        phi, slope = gelu_parts(u)
        slope_ref[:, cols] = slope
        r2 = r2 + nn((u * phi).astype(BF), down_ref[cols, :])
    z2, inverse2 = normalize(r2)
    result_ref[...] = (z2 * gain_ref[1:2, :] + off_ref[1:2, :]).astype(BF)
    cot = cot_ref[...].astype(F32)
    dr2 = normalize_back(z2, inverse2, cot * gain_ref[1:2, :])
    ydf_ref[:, D:] = dr2.astype(BF)
    dr2_ref[...] = dr2
    z2_sum_ref[...] = total(cot * z2)
    for one in moved:
        one.wait()


def backward_kernel(
    starts, chips,
    z1_ref, inverse_ref, dr2_ref, slope_ref, z2_sum_ref, attn_ref, cot_ref, hot_ref, lse_ref,
    wo_in, up_in, down_in, gain_ref,
    packed_ref, dr1_out, da_out, docs_out, stats_out, hot_out, *refs,
):
    ado_outs, ados = refs[:chips], refs[-chips - 1 : -1]
    dr1_ref, da_ref, docs_ref, stats_ref, sums_ref, wo_ref, up_ref, down_ref = refs[
        chips : chips + 8
    ]
    sems = refs[-1]
    rows = z1_ref.shape[0]
    loads = []
    for at in range(FF // D):
        cols = slice(at * D, (at + 1) * D)
        first = 5 + chips + 2 * at
        loads.append(copy(down_in.at[cols, :], down_ref.at[cols, :], sems, first))
        loads.append(copy(up_in.at[:, cols], up_ref.at[:, cols], sems, first + 1))
    loads.append(copy(wo_in, wo_ref, sems, 5 + chips + 2 * (FF // D)))
    moved = [copy(hot_ref, hot_out, sems, 0)]
    z1 = z1_ref[...]
    dr2 = dr2_ref[...]
    df_low = dr2.astype(BF)
    dy1 = dr2
    width = D
    for at in range(FF // width):
        cols = slice(at * width, (at + 1) * width)
        loads[2 * at].wait()
        du_low = (nt(df_low, down_ref[cols, :]) * slope_ref[:, cols]).astype(BF)
        sums_ref[6 + at : 7 + at, :] = total(du_low.astype(F32))
        loads[2 * at + 1].wait()
        dy1 = dy1 + nt(du_low, up_ref[:, cols])
    dr1 = normalize_back(z1, inverse_ref[:, 0:1], dy1 * gain_ref[0:1, :])
    dr1_ref[...] = dr1
    moved.append(copy(dr1_ref, dr1_out, sems, 1))
    do_low = dr1.astype(BF)
    loads[-1].wait()
    da = nt(do_low, wo_ref[...]).astype(BF)
    da_ref[...] = da
    moved.append(copy(da_ref, da_out, sems, 2))
    attn = attn_ref[...]
    to_heads = (
        lax.broadcasted_iota(jnp.int32, (D, 128), 0) // HD
        == lax.broadcasted_iota(jnp.int32, (D, 128), 1)
    ).astype(BF)
    high, middle, low = split3(da.astype(F32) * attn)
    delta = nn(high, to_heads) + nn(middle, to_heads) + nn(low, to_heads)
    stats_ref[:, :128] = lse_ref[...]
    stats_ref[:, 128:] = delta
    moved.append(copy(stats_ref, stats_out, sems, 3))
    lse_first, delta_first = lse_ref[...].T, delta.T
    for at, start in enumerate(starts):
        packed_ref[at, :rows, :] = da[:, start : start + PAIR]
        head = start // HD
        four = jnp.concatenate([lse_first[head : head + 2], delta_first[head : head + 2]], axis=0)
        four = jnp.concatenate([four, jnp.zeros((4, rows), F32)], axis=0)
        parts = jnp.concatenate([one.astype(F32) for one in split3(four)], axis=0).astype(BF)
        packed_ref[at, rows : rows + 24, :rows] = parts
    hot = hot_ref[:, at_lanes(lax.axis_index("seq"), rows)]
    high, middle, low = split3(dr1)
    docs_ref[...] = nn(hot, high) + nn(hot, middle) + nn(hot, low)
    moved.append(copy(docs_ref, docs_out, sems, 4))
    cot = cot_ref[...].astype(F32)
    sums_ref[0:1, :] = total(dy1 * z1)
    sums_ref[1:2, :] = z2_sum_ref[...]
    sums_ref[2:3, :] = total(dy1)
    sums_ref[3:4, :] = total(cot)
    sums_ref[4:5, :] = total(do_low.astype(F32))
    sums_ref[5:6, :] = total(df_low.astype(F32))
    sums_ref[6 + FF // width :, :] = jnp.zeros((SUMS - 6 - FF // width, D), F32)
    high, low = split2(sums_ref[...])
    attn = attn.astype(BF)
    if chips == 1:
        ados[0][:rows, :D] = attn
        ados[0][:rows, D:] = do_low
        ados[0][rows:, :D] = high
        ados[0][rows:, D:] = low
    else:
        near, across = lax.axis_index("seq") % 2, lax.axis_index("rows") // 2
        shares = [
            jnp.concatenate(
                [attn[:, (2 * z + y) * 96 : (2 * z + y + 1) * 96] for z in range(4)], axis=1
            )
            for y in range(2)
        ]
        sides = do_low[:, : D // 2], do_low[:, D // 2 :]
        for to, ref in enumerate(ados):
            swapped, over = to // 2, to % 2
            ref[:rows, : D // 2] = jnp.where(near == swapped, shares[0], shares[1])
            ref[:rows, D // 2 :] = jnp.where(across == over, sides[0], sides[1])
            ref[rows : rows + SUMS, :] = high
            ref[rows + SUMS :, :] = low
    moved += copies(zip(ados, ado_outs), sems, 5)
    wait(moved)


def query_grad_kernel(share, *refs):
    q_in, k_in, v_in, da_in, stats_in, hot_in, x_in, qkv_in, bias_ref = refs[:9]
    dq_ref, q_two_out, k_two_out, v_two_out, w_out = refs[9:14]
    x_ref, q_two, k_two, v_two, w_ref, wide_ref = refs[14:20]
    q_ref, k_ref, v_ref, da_ref, stats_ref, hot_ref, mask_ref, sems = refs[20:]
    rows = q_ref.shape[0]
    length = k_ref.shape[0]
    base, back = head_window(share)
    loads = copies(
        (
            (hot_in, hot_ref), (k_in, k_ref), (q_in, q_ref), (stats_in, stats_ref), (da_in, da_ref),
            (v_in, v_ref), (x_in, x_ref),
        ),
        sems,
        3,
    )
    windows = copies(
        [
            (qkv_in.at[:, pl.ds(pl.multiple_of(base + kind * D, PAIR), 2 * PAIR)], wide_ref.at[kind])
            for kind in range(3)
        ],
        sems,
        0,
    )
    wait(loads[:-1])
    hot = hot_ref[:, at_lanes(lax.axis_index("seq"), rows)]
    mask_ref[...] = (tn(hot, hot_ref[...]) - 1.0) * -MASKED
    first = lax.broadcasted_iota(jnp.int32, (rows, PAIR), 1) < HD
    for pair in range(PAIRS):
        cols = slice(pair * PAIR, (pair + 1) * PAIR)
        q, da = q_ref[:, cols], da_ref[:, cols]
        halves = []
        for half in range(2):
            here = first if half == 0 else ~first
            head = 2 * pair + half
            scores = nt(jnp.where(here, q, jnp.zeros_like(q)), k_ref[:, cols]) + mask_ref[...]
            probs = jnp.exp(scores - stats_ref[:, head : head + 1])
            dprobs = nt(jnp.where(here, da, jnp.zeros_like(da)), v_ref[:, cols])
            ds = (probs * (dprobs - stats_ref[:, 128 + head : 129 + head])).astype(BF)
            halves.append(nn(ds, k_ref[:, cols]))
        dq_ref[:, cols] = (jnp.where(first, halves[0], halves[1]) * (HD**-0.5)).astype(BF)
    wait(windows)
    biases = []
    for kind in range(3):
        turned = pltpu.roll(wide_ref[kind].astype(F32), back, 1)[:, :PAIR]
        w_ref[:, kind * PAIR : (kind + 1) * PAIR] = turned.astype(BF)
        if kind == 1:
            biases.append(jnp.zeros((1, PAIR), F32))
        else:
            cols = pl.ds(pl.multiple_of(base + (kind // 2) * D, PAIR), 2 * PAIR)
            bias = jnp.broadcast_to(bias_ref[:, cols], (8, 2 * PAIR))
            biases.append(pltpu.roll(bias, back, 1)[:1, :PAIR])
    moved = [copy(w_ref, w_out, sems, 10)]
    loads[-1].wait()
    step = 256
    for at in range(length // step):
        piece = slice(at * step, (at + 1) * step)
        three = nn(x_ref[piece, :], w_ref[...])
        q_two[piece, :] = (
            (three[:, :PAIR] + biases[0]).astype(BF).astype(F32) * (HD**-0.5)
        ).astype(BF)
        k_two[piece, :] = three[:, PAIR : 2 * PAIR].astype(BF)
        v_two[piece, :] = (three[:, 2 * PAIR :] + biases[2]).astype(BF)
    moved += copies(((q_two, q_two_out), (k_two, k_two_out), (v_two, v_two_out)), sems, 11)
    wait(moved)


def head_grad_kernel(step, share, *refs):
    w_in, q_in, k_in, v_in, hot_in, docs_in, da_ref = refs[:7]
    back_ref, heads_out, bias_ref = refs[7:10]
    w_ref, q_ref, k_ref, v_ref, hot_ref, docs_ref = refs[10:16]
    dq_ref, dk_ref, dv_ref, heads_ref, sems = refs[16:]
    length = q_ref.shape[0]
    rows = length // (D // share)
    seq = lax.axis_index("seq")
    loads = copies(
        (
            (hot_in, hot_ref), (v_in, v_ref), (k_in, k_ref), (q_in, q_ref),
            (w_in, w_ref), (docs_in, docs_ref),
        ),
        sems,
        0,
    )
    wait(loads[:4])
    first = lax.broadcasted_iota(jnp.int32, (step, PAIR), 1) < HD
    each = step // rows
    for at in range(length // step):
        piece = slice(at * step, (at + 1) * step)
        blocks = range(at * each, (at + 1) * each)
        da_all = jnp.concatenate([da_ref[one, :rows, :] for one in blocks], axis=0)
        stats = jnp.concatenate(
            [da_ref[one, rows : rows + 24, :rows].astype(F32) for one in blocks], axis=1
        )
        stats = stats[:8] + stats[8:16] + stats[16:]
        mask = (tn(hot_ref[...], hot_ref[:, piece]) - 1.0) * -MASKED
        halves = []
        for half in range(2):
            here = first if half == 0 else ~first
            q = jnp.where(here, q_ref[piece, :], jnp.zeros((step, PAIR), BF))
            da = jnp.where(here, da_all, jnp.zeros((step, PAIR), BF))
            probs = jnp.exp(nt(k_ref[...], q) + (mask - stats[half : half + 1]))
            ds = (probs * (nt(v_ref[...], da) - stats[2 + half : 3 + half])).astype(BF)
            halves.append(tn(ds, k_ref[...]))
            dk, dv = nn(ds, q), nn(probs.astype(BF), da)
            if at == 0 and half == 0:
                dk_ref[...], dv_ref[...] = dk, dv
            else:
                dk_ref[...] += dk
                dv_ref[...] += dv
        dq_ref[piece, :] = jnp.where(first, halves[0], halves[1]) * (HD**-0.5)
    wait(loads[4:])
    offset = seq * share - head_start(seq, share)
    left = (PAIR - offset) % PAIR
    for at in range(length // step):
        piece = slice(at * step, (at + 1) * step)
        heads_ref[piece, :] = jnp.concatenate(
            [pltpu.roll(ref[piece, :], left, 1)[:, :share] for ref in (dq_ref, dk_ref, dv_ref)],
            axis=1,
        ).astype(BF)
    moved = copy(heads_ref, heads_out, sems, 6)
    doc_sums = nn(hot_ref[...], heads_ref[...])
    bias_ref[...] = total(doc_sums)
    docs = docs_ref[...]
    for kind in range(3):
        piece = doc_sums[:, kind * share : (kind + 1) * share]
        piece = jnp.concatenate([piece, jnp.zeros((DOCS, PAIR - share), F32)], axis=1)
        parts = jnp.concatenate(split3(pltpu.roll(piece, offset, 1)), axis=0)
        product = nt(parts, w_ref[:, kind * PAIR : (kind + 1) * PAIR])
        docs = docs + (product[:DOCS] + product[DOCS : 2 * DOCS] + product[2 * DOCS :])
    docs = docs.astype(BF)
    extra = back_ref.shape[1] - 6 * DOCS
    for at in range(D // share):
        here = heads_ref[at * rows : (at + 1) * rows, share:]
        if 2 * share <= PAIR:
            back_ref[at, :rows, : 2 * share] = here
        else:
            back_ref[at, :rows, :] = here[:, :PAIR]
            rest = here[:, PAIR:]
            back_ref[at, rows:extra, :] = jnp.concatenate(
                [rest[: rows // 2], rest[rows // 2 :]], axis=1
            )
        for col in range(PAIRS):
            back_ref[at, extra + col * DOCS : extra + (col + 1) * DOCS, :] = docs[
                :, col * PAIR : (col + 1) * PAIR
            ]
    moved.wait()


def head_weights_kernel(share, split, x_in, heads_in, bias_ref, *refs):
    outs, (x_ref, heads_ref, grad_ref, sems) = refs[:-4], refs[-4:]
    wait(copies(((heads_in, heads_ref), (x_in, x_ref)), sems, 0))
    if not split:
        outs[0][...] = tn(x_ref[...], heads_ref[...])
        return
    *sent, mine_ref = outs
    grad_ref[...] = tn(x_ref[...], heads_ref[...])
    rank = lax.axis_index("rows")
    part = share // split
    high, low = split2(jnp.broadcast_to(bias_ref[...], (8, 3 * share)))
    row = lax.broadcasted_iota(jnp.int32, (8, 3 * share), 0)
    tail = jnp.where(row == 0, high.astype(F32), jnp.where(row == 1, low.astype(F32), 0.0))
    for to, ref in enumerate([mine_ref] + list(sent)):
        for at in range(D // share):
            here = pl.ds(pl.multiple_of(at * share + (rank ^ to) * part, 8), part)
            ref[at, :part, :] = grad_ref[here, :].astype(ref.dtype)
            ref[at, part:, :] = tail.astype(ref.dtype)


def head_grad(apart, da, share):
    length = apart[1].shape[0]
    count = D // share
    rows = length // count
    outs = [((count, rows + (rows // 2 if 2 * share > PAIR else 0) + 6 * DOCS, PAIR), BF)]
    outs += [((length, 3 * share), BF, FAR), ((1, 3 * share), F32)]
    scratch = [(one.shape, one.dtype) for one in apart] + [((length, PAIR), F32)] * 3
    scratch += [((length, 3 * share), BF)]
    return call(
        functools.partial(head_grad_kernel, 256, share),
        "head_grad",
        (*(far(one) for one in apart), da),
        outs,
        scratch,
        20 if length <= 1024 else 40,
        7,
    )


def head_weights(x_low, heads, bias, share, split):
    block = (D // share, share // split + 8, 3 * share) if split else (D, 3 * share)
    return call(
        functools.partial(head_weights_kernel, share, split),
        "head_weights",
        (far(x_low), far(heads), bias),
        [(block, BF)] * (split - 1) + [(block, F32)] if split else [(block, F32)],
        [(x_low.shape, BF), (heads.shape, BF), ((D, 3 * share), F32)],
        16,
        2,
    )


def input_grad_kernel(
    share, back_ref, dr1_in, dq_ref, qkv_in, grad_ref, docs_ref, dr1_ref, qkv_ref, sems
):
    loads = copies(((qkv_in, qkv_ref), (dr1_in, dr1_ref)), sems, 0)
    rows = dr1_ref.shape[0]
    count = D // share
    extra = back_ref.shape[1] - 6 * DOCS
    keys, values = [], []
    for at in range(count):
        here = back_ref[at, :rows, :]
        if 2 * share > PAIR:
            rest = back_ref[at, rows:extra, :]
            rest = jnp.concatenate([rest[:, : PAIR // 2], rest[:, PAIR // 2 :]], axis=0)
            here = jnp.concatenate([here, rest], axis=1)
        keys.append(here[:, :share])
        values.append(here[:, share : 2 * share])
    wait(loads)
    result = dr1_ref[...] + nt(dq_ref[...], qkv_ref[:, :D])
    result = result + nt(jnp.concatenate(keys, axis=1), qkv_ref[:, D : 2 * D])
    grad_ref[...] = result + nt(jnp.concatenate(values, axis=1), qkv_ref[:, 2 * D :])
    docs = jnp.zeros((6 * DOCS, PAIR), F32)
    for at in range(count):
        docs = docs + back_ref[at, extra:, :].astype(F32)
    docs_ref[...] = jnp.concatenate(
        [docs[at * DOCS : (at + 1) * DOCS] for at in range(PAIRS)], axis=1
    )


def unit_share(at):
    return 2 * (at % 4) + at // 4


def part_weights_kernel(up_in, bu_ref, up_out, bu_out, held_ref, up_ref, sems):
    back = (384 - lax.axis_index("rows") * 96) % 384
    loads = copies(
        [
            (up_in.at[:, unit_share(at) * 384 : (unit_share(at) + 1) * 384], held_ref.at[at])
            for at in range(8)
        ],
        sems,
        0,
    )
    ups, biases = [], []
    for at in range(8):
        cols = slice(unit_share(at) * 384, (unit_share(at) + 1) * 384)
        loads[at].wait()
        ups.append(pltpu.roll(held_ref[at].astype(F32), back, 1)[:, :96].astype(BF))
        bias = jnp.broadcast_to(bu_ref[:, cols], (8, 384))
        biases.append(pltpu.roll(bias, back, 1)[:1, :96])
    up_ref[...] = jnp.concatenate(ups, axis=1)
    moved = copy(up_ref, up_out, sems, 8)
    bu_out[...] = jnp.concatenate(biases, axis=1)
    moved.wait()


def feed_grad_kernel(*refs):
    pieces = refs[:8]
    up_in, bu_ref, down_in = refs[8:11]
    own_ref, sent_ref = refs[11:13]
    y1_ref, df_ref, up_ref, down_ref, g_ref, du_ref, up_grad_ref, down_grad_ref, sems = refs[13:]
    seq = lax.axis_index("seq")
    near, z = seq % 2, seq // 2
    rows = pieces[0].shape[0]
    here = [slice(at * rows, (at + 1) * rows) for at in range(8)]
    loads = [copy(up_in, up_ref, sems, 16)]
    loads += copies([(piece.at[:, :D], y1_ref.at[r, :]) for piece, r in zip(pieces, here)], sems, 0)
    first = lax.axis_index("rows") * 96
    downs = copies(
        [
            (
                down_in.at[pl.ds(pl.multiple_of(unit_share(at) * 384 + first, 32), 96), :],
                down_ref.at[at * 96 : (at + 1) * 96, :],
            )
            for at in range(8)
        ],
        sems,
        17,
    )
    grads = copies([(piece.at[:, D:], df_ref.at[r, :]) for piece, r in zip(pieces, here)], sems, 8)
    step = 2 * rows
    wait(loads)
    for at in range(4):
        piece = slice(at * step, (at + 1) * step)
        u = nn(y1_ref[piece, :], up_ref[...]) + bu_ref[...]
        phi, slope = gelu_parts(u)
        if at == 0:
            wait(downs)
            wait(grads)
        g_ref[piece, :] = (u * phi).astype(BF)
        du_ref[piece, :] = (nt(df_ref[piece, :], down_ref[...]) * slope).astype(BF)
    down_grad_ref[...] = tn(g_ref[:, at_lanes(near, 384)], df_ref[...])
    up_grad_ref[...] = tn(y1_ref[...], du_ref[...])
    for to in range(4):
        up_rows = pl.ds(pl.multiple_of((2 * (z ^ to) + near) * 96, 8), 96)
        down_rows = pl.ds(pl.multiple_of((z ^ to) * 96, 8), 96)
        ref = own_ref.at[to // 2] if to % 2 == 0 else sent_ref.at[to // 2]
        ref[:, :D] = up_grad_ref[up_rows, :].astype(ref.dtype)
        ref[:, D:] = down_grad_ref[down_rows, :].astype(ref.dtype)


def feed_grad(pieces, up, bias, down):
    tokens = 8 * pieces[0].shape[0]
    block = (2, 96, 2 * D)
    wide = ((tokens, D), BF)
    return call(
        feed_grad_kernel,
        "feed_grad",
        (*(far(one) for one in pieces), far(up), bias, far(down)),
        [(block, F32), (block, BF)],
        [wide, wide, ((D, D), BF), ((D, D), BF), wide, wide, ((D, D), F32), ((384, D), F32)],
        24,
        25,
    )


def out_grad_kernel(*refs):
    pieces = refs[:8]
    own_ref, one_ref, two_ref, three_ref, attn_ref, do_ref, sums_ref, grad_ref, sems = refs[8:]
    seq, rank = lax.axis_index("seq"), lax.axis_index("rows")
    z = seq // 2
    rows = pieces[0].shape[0] - 2 * SUMS
    base = pl.multiple_of(D // 2 + (rank % 2) * 128, 128)
    back = (256 - (rank % 2) * 64) % 256
    loads = []
    for at, piece in enumerate(pieces):
        here = slice(at * rows, (at + 1) * rows)
        loads += copies(
            (
                (piece.at[:rows, : D // 2], attn_ref.at[here, :]),
                (piece.at[:rows, pl.ds(base, 256)], do_ref.at[here, :]),
                (piece.at[rows:, :], sums_ref.at[at]),
            ),
            sems,
            3 * at,
        )
    wait(loads)
    sums = jnp.zeros((2 * SUMS, D), F32)
    for at in range(8):
        sums = sums + sums_ref[at].astype(F32)
    grad_ref[...] = pltpu.roll(tn(attn_ref[...], do_ref[...]), back, 1)
    high, low = split2(sums[:SUMS] + sums[SUMS:])
    for to, ref in enumerate((own_ref, one_ref, two_ref, three_ref)):
        here = pl.ds(pl.multiple_of((z ^ to) * 96, 8), 96)
        ref[:96, :] = grad_ref[here, :192].astype(ref.dtype)
        for part, value in enumerate((high, low)):
            for col in range(4):
                at = 96 + (part * 4 + col) * SUMS
                ref[at : at + SUMS, :] = value[:, col * 192 : (col + 1) * 192].astype(ref.dtype)


def out_grad(pieces):
    rows = pieces[0].shape[0] - 2 * SUMS
    block = (96 + 8 * SUMS, 192)
    return call(
        out_grad_kernel,
        "out_grad",
        [far(one) for one in pieces],
        [(block, F32), (block, BF), (block, BF), (block, BF)],
        [
            ((8 * rows, D // 2), BF), ((8 * rows, 256), BF), ((8, 2 * SUMS, D), BF),
            ((D // 2, 256), F32),
        ],
        8,
        24,
    )


def combine_half_kernel(own_ref, got_ref, mine_ref, sent_ref):
    mine_ref[...] = own_ref[0] + got_ref[0].astype(F32)
    sent_ref[...] = (own_ref[1] + got_ref[1].astype(F32)).astype(BF)


def combine_all_kernel(
    feed_ref, got_ref, own_ref, a_ref, b_ref, c_ref, out_ref, norm_ref, bias_ref, up_ref
):
    seq = lax.axis_index("seq")
    out_ref[:96, :] = (feed_ref[...] + got_ref[...].astype(F32)).astype(BF)
    value = own_ref[...]
    for ref in (a_ref, b_ref, c_ref):
        value = value + ref[...].astype(F32)
    for at in range(6):
        cols = slice(at * 192, (at + 1) * 192)
        out_ref[96:, cols] = value[at * 16 : (at + 1) * 16].astype(BF)
    tail = value[96 : 96 + 4 * SUMS] + value[96 + 4 * SUMS :]
    sums = jnp.concatenate([tail[at * SUMS : (at + 1) * SUMS] for at in range(4)], axis=1)
    mine = pltpu.roll(sums, (D - seq * 96) % D, 1)[:, :96]
    norm_ref[...] = mine[:4]
    bias_ref[...] = mine[4:6]
    row = jnp.where(
        lax.broadcasted_iota(jnp.int32, (SUMS, D), 0) == 6 + seq // 2, sums, 0.0
    )
    row = total(row)
    up_ref[...] = jnp.where(seq % 2 == 0, row[:, :384], row[:, 384:])


def finish_all_kernel(a_ref, b_ref, c_ref, d_ref, up_ref, down_ref, out_ref, held_ref, side_ref):
    rank = lax.axis_index("rows")
    for at, ref in enumerate((a_ref, b_ref, c_ref, d_ref)):
        held_ref[rank ^ at] = ref[:96, :D].astype(F32)
        down_ref[pl.ds(pl.multiple_of((rank ^ at) * 96, 8), 96), :] = ref[:96, D:].astype(F32)
        side_ref[rank ^ at] = ref[96:, : 6 * 192].astype(F32)
    for share in range(8):
        at = (share // 2) + 4 * (share % 2)
        up_ref[:, share * 384 : (share + 1) * 384] = jnp.concatenate(
            [held_ref[r, :, at * 96 : (at + 1) * 96] for r in range(4)], axis=1
        )
    for at in range(6):
        out_ref[at * 16 : (at + 1) * 16, :] = jnp.concatenate(
            [side_ref[r, :, at * 192 : (at + 1) * 192] for r in range(4)], axis=1
        )


def time_grad_kernel(*refs):
    features, docs, (out_ref, left_ref, sems) = refs[:4], refs[4:8], refs[8:]
    seq = lax.axis_index("seq")
    wait(
        copies([(ref, left_ref.at[at * DOCS : (at + 1) * DOCS]) for at, ref in enumerate(features)], sems, 0)
    )
    left = left_ref[...].astype(F32)
    left = pltpu.roll(left, (D - seq * 96) % D, 1)[:, :96].astype(BF)
    high, middle, low = split3(jnp.concatenate([ref[...] for ref in docs], axis=0))
    out_ref[...] = tn(left, high) + tn(left, middle) + tn(left, low)


def finish_heads_kernel(a_ref, b_ref, c_ref, d_ref, out_ref, bias_ref):
    rank = lax.axis_index("rows")
    order = [(kind, at) for kind in range(3) for at in range(8)]
    for to, ref in enumerate((a_ref, b_ref, c_ref, d_ref)):
        value = jnp.concatenate(
            [ref[at, :24, kind * 96 : (kind + 1) * 96].astype(F32) for kind, at in order], axis=1
        )
        out_ref[pl.ds(pl.multiple_of((rank ^ to) * 24, 8), 24), :] = value
    tail = jnp.concatenate(
        [a_ref[at, 24:, kind * 96 : (kind + 1) * 96].astype(F32) for kind, at in order], axis=1
    )
    sums = tail[0:1] + tail[1:2]
    sums = jnp.concatenate([sums[:, :D], sums[:, 2 * D :]], axis=1)
    back = (2 * D - lax.axis_index("seq") * 192) % (2 * D)
    bias_ref[...] = pltpu.roll(jnp.broadcast_to(sums, (8, 2 * D)), back, 1)[:1, :192]


def combine_kernel(tail, own_ref, a_ref, b_ref, c_ref, out_ref):
    value = own_ref[...]
    for ref in (a_ref, b_ref, c_ref):
        value = value + ref[...].astype(F32)
    if tail:
        count, rows, wide = value.shape
        out_ref[:, : rows - 8, :] = value[:, : rows - 8].astype(out_ref.dtype)
        row = lax.broadcasted_iota(jnp.int32, (8, wide), 0)
        for at in range(count):
            last = value[at, rows - 8 :]
            high, low = split2(jnp.broadcast_to(last[0:1] + last[1:2], (8, wide)))
            out_ref[at, rows - 8 :, :] = jnp.where(
                row == 0, high.astype(F32), jnp.where(row == 1, low.astype(F32), 0.0)
            ).astype(out_ref.dtype)
    else:
        out_ref[...] = value.astype(out_ref.dtype)


def combine(blocks, dtype, tail=False):
    return call(
        functools.partial(combine_kernel, tail), "combine", blocks, [(blocks[0].shape, dtype)]
    )[0]


def after(value, *others):
    return lax.optimization_barrier((value,) + others)[0]


def after_all(values, *others):
    return list(lax.optimization_barrier((tuple(values), others))[0])


def far_swaps(blocks):
    return [swap(block, "seq", 2 * (to + 1)) for to, block in enumerate(blocks)]


def from_chips(own, over, near, both):
    pairs = [((s * 4 + r), ((s ^ 1) * 4 + (r ^ 2))) for s in range(8) for r in range(4)]
    across = lax.ppermute(both, ("seq", "rows"), pairs)
    return [own, swap(over, "rows", 2), swap(near, "seq", 1), across]


def with_twin(blocks):
    return blocks + [swap(one, "rows", 1) for one in blocks]


def spread_rows(block):
    across = swap(block, "rows", 2)
    return block, swap(block, "rows", 1), across, swap(across, "rows", 1)


def pick(blocks, index, axis=0):
    return lax.dynamic_index_in_dim(blocks, index, axis, keepdims=False)


def reduce_rows(blocks, place):
    bit = 1
    while blocks.shape[0] > 1:
        pairs = blocks.reshape((blocks.shape[0] // 2, 2) + blocks.shape[1:])
        mine = (place // bit) % 2
        sent = swap(pick(pairs, 1 - mine, 1).astype(BF), "rows", bit)
        blocks = pick(pairs, mine, 1).astype(F32) + sent.astype(F32)
        bit *= 2
    return blocks[0]


def gather_rows(block, place):
    count = lax.axis_size("rows")
    found = block[None]
    bit = count // 2
    while bit >= 1:
        other = swap(found, "rows", bit)
        mine = (place // bit) % 2
        low, high = jnp.where(mine == 0, found, other), jnp.where(mine == 0, other, found)
        if bit == count // 2:
            found = jnp.concatenate([low, high], axis=0)
        else:
            found = jnp.stack([low, high], axis=1).reshape((-1,) + block.shape)
        bit //= 2
    return found


def general_grads(ydf, ado, grad_heads, head_sums, up_weight, up_bias, down_weight):
    seqs, ranks = lax.axis_size("seq"), lax.axis_size("rows")
    seq, rank = lax.axis_index("seq"), lax.axis_index("rows")
    inner = seqs // Z_STEPS
    near = seq % inner
    share = D // seqs
    ff_share = FF // seqs
    ff_part = ff_share // ranks
    rows = ydf.shape[0]

    part = share // ranks
    grad_heads = grad_heads.reshape(seqs, ranks, part, 3 * share)
    mine = reduce_rows(jnp.moveaxis(grad_heads, 1, 0), rank)
    spread = lax.all_to_all(mine.astype(BF), "seq", 0, 0, tiled=True)
    columns = [
        spread[i, :, kind * share : (kind + 1) * share] for kind in range(3) for i in range(seqs)
    ]
    quarter = jnp.concatenate(columns, axis=1)
    grad_qkv = gather_rows(quarter, rank).reshape(share, 3 * D).astype(F32)

    def gather_near(block):
        found = [block]
        bit = 2
        while bit < ranks:
            found = found + [swap(one, "rows", bit) for one in found]
            bit *= 2
        for step in range(1, inner):
            found = found + [swap(one, "seq", step) for one in found[: len(found) // step]]
        mine = jnp.concatenate(found, axis=0)
        return jnp.concatenate([mine, swap(mine, "rows", 1)], axis=0)

    ydf_all = gather_near(ydf)
    y1_all, df_all = ydf_all[:, :D], ydf_all[:, D:]
    order = [far * inner + i for i in range(inner) for far in range(Z_STEPS)]
    ff_starts = [i * ff_share + rank * ff_part for i in order]
    take = lambda array, axis: jnp.concatenate(
        [lax.dynamic_slice_in_dim(array, a, ff_part, axis) for a in ff_starts], axis=axis
    )
    up_mine, down_mine, bias_mine = take(up_weight, 1), take(down_weight, 0), take(up_bias, 0)
    u = nn(y1_all, up_mine) + bias_mine
    phi, slope = gelu_parts(u)
    du_all = (nt(df_all, down_mine) * slope).astype(BF)
    g_all = (u * phi).astype(BF)
    group = Z_STEPS * ff_part
    g_near = lax.dynamic_slice_in_dim(g_all, near * group, group, 1)
    grad_down = tn(g_near, df_all).reshape(Z_STEPS, ff_part, D)
    grad_up = pick(tn(y1_all, du_all).reshape(Z_STEPS, inner, share, seqs * ff_part), near, 1)
    ado, grad_up, grad_down = lax.optimization_barrier((ado, grad_up, grad_down))
    ado_all = gather_near(ado[:rows])
    attn_all, do_all = ado_all[:, :D], ado_all[:, D:]
    out_part = D // ranks
    do_mine = lax.dynamic_slice_in_dim(do_all, rank * out_part, out_part, 1)
    grad_out = pick(tn(attn_all, do_mine).reshape(Z_STEPS, inner, share, out_part), near, 1)

    def reduce_far(blocks):
        blocks = blocks.astype(BF)
        far = seq // inner
        summed = pick(blocks, far).astype(F32)
        for step in range(1, Z_STEPS):
            summed = summed + swap(pick(blocks, far ^ step), "seq", step * inner).astype(F32)
        return gather_rows(summed.astype(BF), rank)

    grad_down = reduce_far(grad_down).reshape(ff_share, D).astype(F32)
    grad_up = reduce_far(grad_up).reshape(ranks, share, inner, Z_STEPS, ff_part)
    grad_up = jnp.transpose(grad_up, (1, 3, 2, 0, 4)).reshape(share, FF).astype(F32)
    grad_out = jnp.transpose(reduce_far(grad_out), (1, 0, 2)).reshape(share, D).astype(F32)

    sums = ado[rows:, :D].astype(F32) + ado[rows:, D:].astype(F32)
    placed = lambda kind: lax.dynamic_update_slice_in_dim(
        jnp.zeros((D,), F32), head_sums[0, kind * share : (kind + 1) * share], seq * share, 0
    )
    sums = sums.at[10].set(placed(0)).at[11].set(placed(2))
    for axis, count in (("rows", ranks), ("seq", seqs)):
        bit = 1
        while bit < count:
            sums = sums + swap(sums, axis, bit)
            bit *= 2
    return grad_qkv, sums[10:12].reshape(-1), grad_out, grad_up, grad_down, sums


def body(
    hidden, cotangent, segment_ids, timesteps, qkv_weight, qv_bias, out_weight, out_bias,
    up_weight, up_bias, down_weight, down_bias, norm_gain, norm_bias, time_weight,
):
    assert hidden.shape[0] == 1
    rows = hidden.shape[1]
    seqs, ranks = lax.axis_size("seq"), lax.axis_size("rows")
    length = seqs * rows
    seq, rank = lax.axis_index("seq"), lax.axis_index("rows")
    share = D // seqs
    fast = seqs == 8 and ranks == 4
    starts = [min(i * share // HD, H - 2) * HD for i in range(seqs)]

    ids = jnp.pad(segment_ids.astype(BF), ((0, 7), (0, D - rows)))
    shards = gather_seq(jnp.concatenate([hidden[0], ids], axis=0))

    features = time_features(timesteps[0]).astype(BF)
    embed = nn(features, time_weight)
    if fast:
        all_features = spread_rows(after(features, shards[2]))
        embed = after(embed, *all_features)
    else:
        all_features = gather_rows(features, rank)
        all_features = lax.dynamic_slice_in_dim(all_features, seq * share, share, 2)
    qv_row, up_row = qv_bias.reshape(1, -1), up_bias.reshape(1, -1)
    tile = ((rows, D), BF)
    tile32 = ((rows, D), F32)
    narrow32 = ((rows, 128), F32)
    wide = ((length, D), BF)
    weights = [((D, 3 * D), BF), ((D, D), BF), ((D, FF), BF), ((FF, D), BF)]
    out_row, down_row = out_bias.reshape(1, -1), down_bias.reshape(1, -1)
    if fast:
        up_part, bias_part = call(
            part_weights_kernel,
            "part_weights",
            (far(up_weight), after(up_row, shards[2])),
            [((D, D), BF, FAR), ((1, D), F32)],
            [((8, D, 384), BF), ((D, D), BF)],
            12,
            9,
        )
        embed = after(embed, bias_part)
    x_low, k, v, q, lse, attn, hot, z1, inverse1, result, ydf, dr2, slope, z2_sum = call(
        functools.partial(forward_kernel, seqs),
        "forward",
        (
            *shards, embed, far(qkv_weight), qv_row, far(out_weight), out_row, norm_gain,
            norm_bias, cotangent[0], far(up_weight), up_row, far(down_weight), down_row,
        ),
        [
            (*wide, FAR), (*wide, FAR), (*wide, FAR), (*tile, FAR), narrow32,
            tile32, ((DOCS, length), BF), tile32, narrow32,
            tile, ((rows, 2 * D), BF), tile32, ((rows, FF), F32), ((1, D), F32),
        ],
        [((rows, length), F32), tile32, wide, wide, wide, tile, *weights],
        32 if fast else 48,
        16,
    )
    if fast:
        ados = [((rows + 2 * SUMS, D), BF)] * 4
        near_ydf = from_chips(ydf, ydf, ydf, ydf)
    else:
        ados = [((rows + SUMS, 2 * D), BF)]
    hots = ((DOCS, length), BF)
    stats_shape = ((rows, 256), F32)
    docs_shape = ((DOCS, D), F32)
    packed, dr1, da_low, docs, stats, hot, *ado = call(
        functools.partial(backward_kernel, starts, len(ados)),
        "backward",
        (
            z1, inverse1, dr2, slope, z2_sum, attn, cotangent[0], hot, lse, far(out_weight),
            far(up_weight), far(down_weight), norm_gain,
        ),
        [
            ((seqs, rows + 24, PAIR), BF), (*tile32, FAR), (*tile, FAR), (*docs_shape, FAR),
            (*stats_shape, FAR), (*hots, FAR), *((*one, FAR) for one in ados),
        ],
        [tile32, tile, docs_shape, stats_shape, ((SUMS, D), F32), *weights[1:], *ados],
        20,
        6 + len(ados) + 2 * (FF // D),
    )

    arrived = lax.all_to_all(packed, "seq", 0, 0, tiled=True)
    pair = ((length, PAIR), BF)
    head_shape = ((D, 3 * PAIR), BF)
    dq_low, q_two, k_two, v_two, head_weight = call(
        functools.partial(query_grad_kernel, share),
        "query_grad",
        (*(far(one) for one in (q, k, v, da_low, stats, hot, x_low, qkv_weight)), qv_row),
        [tile] + [(*one, FAR) for one in (pair, pair, pair, head_shape)],
        [wide, pair, pair, pair, head_shape, ((3, D, 2 * PAIR), BF)]
        + [tile, wide, wide, tile, stats_shape, hots, ((rows, length), F32)],
        20 if fast else 32,
        14,
    )
    if fast:
        near_ydf = with_twin(after_all(near_ydf, dq_low))
        feed_own, feed_sent = feed_grad(near_ydf, up_part, bias_part, down_weight)
        feed_got = swap(feed_sent, "seq", 2)
        near_ado = from_chips(*after_all(ado, near_ydf[3]))
        arrived = after(arrived, feed_own)
    back, heads, head_sums = head_grad(
        (head_weight, q_two, k_two, v_two, hot, docs), arrived, share
    )
    if fast:
        back, heads, head_sums, *near_ado = after_all((back, heads, head_sums, *near_ado))
    grads = head_weights(x_low, heads, head_sums, share, 4 if fast else 0)
    back = lax.all_to_all(back, "seq", 0, 0, tiled=True)
    input_grad, doc_grad = call(
        functools.partial(input_grad_kernel, share),
        "input_grad",
        (back, far(dr1), dq_low, far(qkv_weight)),
        [tile32, ((DOCS, D), F32)],
        [tile32, ((D, 3 * D), BF)],
        10,
        2,
    )
    if fast:
        feed_mine, feed_sent = call(
            combine_half_kernel, "combine_half", (feed_own, feed_got),
            [((96, 2 * D), F32), ((96, 2 * D), BF)],
        )
        feed_got = swap(feed_sent, "seq", 4)
        *sent, own = after_all(grads, feed_mine)
        sent = [swap(block, "rows", to + 1) for to, block in enumerate(sent)]
        mine = combine((own, *sent), BF, True)
        out_own, *out_sent = out_grad(with_twin(after_all(near_ado, feed_mine)))
        out_got = far_swaps(out_sent)
        merged, norm_sums, bias_sums, grad_up_bias = call(
            combine_all_kernel, "combine_all",
            (feed_mine, after(feed_got, mine), out_own, *out_got),
            [((112, 2 * D), BF), ((4, 96), F32), ((2, 96), F32), ((1, 384), F32)],
        )
        grad_up_weight, grad_down_weight, grad_out_weight = call(
            finish_all_kernel, "finish_all", spread_rows(merged),
            [((share, FF), F32), ((FF // seqs, D), F32), ((share, D), F32)],
            [((4, 96, D), F32), ((4, 16, 6 * 192), F32)],
        )
        mine = after(mine, merged, input_grad)
        spread = lax.all_to_all(mine, "seq", 0, 0, tiled=True)
        grad_qkv_weight, grad_qv_bias = call(
            finish_heads_kernel, "finish_heads", spread_rows(spread),
            [((share, 3 * D), F32), ((1, 192), F32)],
        )
        grad_time_weight = call(
            time_grad_kernel, "time_grad", (*(far(one) for one in all_features), *spread_rows(doc_grad)),
            [((share, D), F32)], [((4 * DOCS, D), BF)], 8, 4,
        )[0]
        grad_qv_bias, grad_up_bias = grad_qv_bias[0], grad_up_bias[0]
        grad_out_bias, grad_down_bias = bias_sums[0], bias_sums[1]
        grad_norm_gain, grad_norm_bias = norm_sums[:2], norm_sums[2:]
    else:
        doc_grad = gather_rows(doc_grad, rank).reshape(ranks * DOCS, D)
        grad_time_weight = lax.dot_general(
            all_features.reshape(ranks * DOCS, share).astype(F32),
            doc_grad,
            (((0,), (0,)), ((), ())),
            precision=precise,
        )
        grad_qkv_weight, qv_sums, grad_out_weight, grad_up_weight, grad_down_weight, totals = (
            general_grads(ydf, ado[0], grads[0], head_sums, up_weight, up_bias, down_weight)
        )

        def part_of(vector, axis=0):
            size = vector.shape[axis] // seqs
            return lax.dynamic_slice_in_dim(vector, seq * size, size, axis)

        grad_qv_bias, grad_out_bias = part_of(qv_sums), part_of(totals[4])
        grad_up_bias = part_of(totals[6 : 6 + FF // D].reshape(-1))
        grad_down_bias = part_of(totals[5])
        grad_norm_gain, grad_norm_bias = part_of(totals[0:2], 1), part_of(totals[2:4], 1)

    return (
        result[None],
        input_grad[None],
        grad_qkv_weight,
        grad_qv_bias,
        grad_out_weight,
        grad_out_bias,
        grad_up_weight,
        grad_up_bias,
        grad_down_weight,
        grad_down_bias,
        grad_norm_gain,
        grad_norm_bias,
        grad_time_weight,
    )


def solution(mesh):
    tokens = P("rows", "seq", None)
    whole = P()
    return jax.shard_map(
        body,
        mesh=mesh,
        in_specs=(tokens, tokens, P("rows", "seq"), P("rows", None)) + (whole,) * 11,
        out_specs=(
            tokens,
            tokens,
            P("seq", None),
            P("seq"),
            P("seq", None),
            P("seq"),
            P("seq", None),
            P("seq"),
            P("seq", None),
            P("seq"),
            P(None, "seq"),
            P(None, "seq"),
            P("seq", None),
        ),
        check_vma=False,
    )
```

```python
import functools
import math

import jax
import jax.numpy as jnp
from jax import lax
from jax.experimental import pallas as pl
from jax.experimental.pallas import tpu as pltpu
from jax.sharding import PartitionSpec as P

D = 768
H = 12
HD = 64
FF = 3072
DOCS = 16
PAIR = 2 * HD
PAIRS = D // PAIR
Z_STEPS = 4
SUMS = 16

EPS = 1e-05
MASKED = -1e30
BF = jnp.bfloat16
F32 = jnp.float32
precise = lax.Precision.HIGHEST
VMEM = pl.BlockSpec(memory_space=pltpu.VMEM)


def swap(block, axis, bit):
    return lax.ppermute(block, axis, [(i, i ^ bit) for i in range(lax.axis_size(axis))])


def dot(a, b, dims):
    return lax.dot_general(a, b, (dims, ((), ())), preferred_element_type=F32)


def nn(a, b):
    return dot(a, b, ((1,), (0,)))


def nt(a, b):
    return dot(a, b, ((1,), (1,)))


def tn(a, b):
    return dot(a, b, ((0,), (0,)))


APART = pl.BlockSpec(memory_space=pltpu.HBM)
FAR = "far"
NEAR = "near"


def far(value):
    return FAR, value


def call(kernel, name, ins, outs, scratch=(), vmem=8, copies=0):
    specs = [APART if isinstance(one, tuple) else VMEM for one in ins]
    values = [
        pltpu.with_memory_space_constraint(one[1], pltpu.HBM) if isinstance(one, tuple) else one
        for one in ins
    ]
    held = [pltpu.VMEM(*one) for one in scratch]
    if copies:
        held.append(pltpu.SemaphoreType.DMA((copies,)))
    return pl.pallas_call(
        kernel,
        out_shape=tuple(
            (pltpu.HBM if FAR in one else pltpu.VMEM)(*one[:2])
            if one[2:]
            else jax.ShapeDtypeStruct(*one)
            for one in outs
        ),
        in_specs=specs,
        out_specs=tuple(APART if FAR in one else VMEM for one in outs),
        scratch_shapes=held,
        compiler_params=pltpu.CompilerParams(vmem_limit_bytes=vmem << 20),
        cost_estimate=pl.CostEstimate(flops=int(COSTS[name] * 1e9), transcendentals=0, bytes_accessed=0),
        name=name,
    )(*values)


def copy(source, target, sems, at):
    moved = pltpu.make_async_copy(source, target, sems.at[at])
    moved.start()
    return moved


def copies(pairs, sems, first):
    return [copy(one, to, sems, first + at) for at, (one, to) in enumerate(pairs)]


def wait(moved):
    for one in moved:
        one.wait()


def loop(count, step):
    def body(at, carry):
        step(at)
        return carry

    lax.fori_loop(0, count, body, 0)


def at_rows(index, size):
    return pl.ds(pl.multiple_of(index * size, 8), size)


def at_lanes(index, size):
    return pl.ds(pl.multiple_of(index * size, 128), size)


def time_features(timesteps):
    half_width = D // 2
    frequency = jnp.exp(
        jnp.arange(half_width, dtype=F32) * (-math.log(10000.0) / half_width)
    )
    phases = timesteps.astype(F32)[..., None] * frequency
    return jnp.concatenate([jnp.sin(phases), jnp.cos(phases)], axis=-1)


def gather_seq(block, known, gate):
    size = lax.axis_size("seq")
    inner = size // Z_STEPS
    found = [None] * size
    found[0] = block
    for far in range(1, Z_STEPS):
        name = "Z%d" % far
        found[far * inner] = swap(gate(name, block), "seq", far * inner)
        known[name] = found[far * inner]
    for far in range(Z_STEPS):
        name = "Y%d" % far
        held = gate(name, found[far * inner])
        for near in range(1, inner):
            found[far * inner + near] = swap(held, "seq", near)
        known[name] = found[far * inner + inner - 1]
    return found


ORDER = {
    "fetch": ("Y0", ),
    "part": ("Z1", ),
    "feat": ("Y0", ),
    "Z3": ("Z1", ),
    "backward": ("forward", ),
    "head": ("heads", ),
    "Etwin": ("head", ),
    "headend": ("E", ),
    "half": ("hw", ),
    "all": ("GA2A", "in", ),
    "finh": ("AGF", ),
    "AGF": ("DOCS", ),
    "time": ("AGG", ),
}
COSTS = {
    "fetch": 7, "forward": 12, "backward": 5, "heads": 3, "part_weights": 3, "feed_grad": 8,
    "head_grad": 9, "head_weights": 2, "input_grad": 2, "combine": 1, "combine_half": 1,
    "combine_all": 1, "finish_all": 2, "finish_heads": 1, "time_grad": 1,
}


def split2(value):
    high = value.astype(BF)
    return high, (value - high.astype(F32)).astype(BF)


def split3(value):
    high = value.astype(BF)
    rest = value - high.astype(F32)
    middle = rest.astype(BF)
    low = (rest - middle.astype(F32)).astype(BF)
    return high, middle, low


def head_start(seq, share):
    return jnp.minimum(seq * share // HD, H - 2) * HD


def head_window(share):
    start = head_start(lax.axis_index("seq"), share)
    base = jnp.minimum(start // PAIR, PAIRS - 2) * PAIR
    return base, (2 * PAIR - (start - base)) % (2 * PAIR)


def normalize(value):
    centered = value - jnp.mean(value, axis=-1, keepdims=True)
    inverse = lax.rsqrt(jnp.mean(centered * centered, axis=-1, keepdims=True) + EPS)
    return centered * inverse, inverse


def normalize_back(z, inverse, grad):
    return inverse * (
        grad
        - jnp.mean(grad, axis=-1, keepdims=True)
        - z * jnp.mean(grad * z, axis=-1, keepdims=True)
    )


def total(value):
    return jnp.sum(value, axis=0, keepdims=True)


def gelu_parts(u):
    phi = 0.5 * (1.0 + lax.erf(u * math.sqrt(0.5)))
    return phi, phi + u * (jnp.exp(-0.5 * u * u) * (1.0 / math.sqrt(2.0 * math.pi)))


def fetch_kernel(*refs):
    count = (len(refs) - 1) // 2
    wait(copies(zip(refs[:count], refs[count:-1]), refs[-1], 0))


def forward_kernel(count, *refs):
    shards = refs[:count]
    embed_ref, qkv_ref, bias_ref, wo_ref, bo_ref, gain_ref, off_ref = refs[count : count + 7]
    cot_ref, up_ref, bu_ref, down_ref, bd_ref = refs[count + 7 : count + 12]
    refs = refs[count + 12 :]
    xlow_out, lse_ref, attn_ref, hot_ref, z1_ref, inverse_ref = refs[:6]
    result_ref, ydf_ref, dr2_ref, slope_ref, z2_sum_ref = refs[6:11]
    mask_ref, x_ref, xlow_ref, k_ref, v_ref, q_ref, sems = refs[11:]
    seq = lax.axis_index("seq")
    rows = attn_ref.shape[0]
    width = D
    parts = [slice(at * width, (at + 1) * width) for at in range(FF // width)]
    embed = jnp.concatenate(split3(embed_ref[...]), axis=0)
    places = lax.broadcasted_iota(jnp.int32, (DOCS, rows), 0).astype(F32)
    hot_own = None
    for at in range(count):
        ids = shards[at][rows : rows + 8, :rows].astype(F32)[:1]
        hot = (places == ids).astype(BF)
        hot_ref[:, at_lanes(seq ^ at, rows)] = hot
        x = shards[at][:rows, :].astype(F32) + tn(jnp.concatenate([hot] * 3, axis=0), embed)
        if at == 0:
            hot_own = hot
            x_ref[...] = x
            own = x.astype(BF)
        xlow_ref[at_rows(seq ^ at, rows), :] = x.astype(BF)
    moved = copy(xlow_ref, xlow_out, sems, 0)
    q_ref[...] = (
        (nn(own, qkv_ref[:, :D]) + bias_ref[:, :D]).astype(BF).astype(F32) * (HD**-0.5)
    ).astype(BF)
    step = 2 * rows
    for at in range(count * rows // step):
        piece = slice(at * step, (at + 1) * step)
        every = xlow_ref[piece, :]
        k_ref[piece, :] = nn(every, qkv_ref[:, D : 2 * D]).astype(BF)
        v_ref[piece, :] = (nn(every, qkv_ref[:, 2 * D :]) + bias_ref[:, D:]).astype(BF)
    mask_ref[...] = (tn(hot_own, hot_ref[...]) - 1.0) * -MASKED
    first = lax.broadcasted_iota(jnp.int32, (rows, PAIR), 1) < HD
    lane = lax.broadcasted_iota(jnp.int32, (rows, 128), 1)
    lse = jnp.zeros((rows, 128), F32)
    for pair in range(PAIRS):
        cols = slice(pair * PAIR, (pair + 1) * PAIR)
        q = q_ref[:, cols]
        halves = []
        for half in range(2):
            q_one = jnp.where(first if half == 0 else ~first, q, jnp.zeros_like(q))
            scores = nt(q_one, k_ref[:, cols]) + mask_ref[...]
            top = jnp.max(scores, axis=-1, keepdims=True)
            weights = jnp.exp(scores - top)
            summed = jnp.sum(weights, axis=-1, keepdims=True)
            halves.append(nn(weights.astype(BF), v_ref[:, cols]) / summed)
            lse = jnp.where(lane == 2 * pair + half, top + jnp.log(summed), lse)
        attn_ref[:, cols] = jnp.where(first, halves[0], halves[1])
    lse_ref[...] = lse
    z1, inverse = normalize(x_ref[...] + nn(attn_ref[...].astype(BF), wo_ref[...]) + bo_ref[...])
    z1_ref[...] = z1
    inverse_ref[...] = jnp.broadcast_to(inverse, (rows, 128))
    y1 = z1 * gain_ref[0:1, :] + off_ref[0:1, :]
    y1_low = y1.astype(BF)
    ydf_ref[:, :D] = y1_low
    r2 = y1 + bd_ref[...]
    for cols in parts:
        u = nn(y1_low, up_ref[:, cols]) + bu_ref[:, cols]
        phi, slope = gelu_parts(u)
        slope_ref[:, cols] = slope
        r2 = r2 + nn((u * phi).astype(BF), down_ref[cols, :])
    z2, inverse2 = normalize(r2)
    result_ref[...] = (z2 * gain_ref[1:2, :] + off_ref[1:2, :]).astype(BF)
    cot = cot_ref[...].astype(F32)
    dr2 = normalize_back(z2, inverse2, cot * gain_ref[1:2, :])
    ydf_ref[:, D:] = dr2.astype(BF)
    dr2_ref[...] = dr2
    z2_sum_ref[...] = total(cot * z2)
    moved.wait()


def backward_kernel(
    starts, chips,
    z1_ref, inverse_ref, dr2_ref, slope_ref, z2_sum_ref, attn_ref, cot_ref, hot_ref, lse_ref,
    wo_ref, up_ref, down_ref, gain_ref, ydf_ref,
    packed_ref, dr1_out, docs_out, hot_out, *refs,
):
    ado_outs, ados = refs[:chips], refs[-chips - 1 : -1]
    dr1_ref, docs_ref, sums_ref = refs[chips : chips + 3]
    sems = refs[-1]
    rows = z1_ref.shape[0]
    moved = [copy(hot_ref, hot_out, sems, 0)]
    if chips > 1:
        moved += copies([(ydf_ref, one.at[:, : 2 * D]) for one in ado_outs], sems, 3 + chips)
        ado_outs = [one.at[:, 2 * D :] for one in ado_outs]
    z1 = z1_ref[...]
    dr2 = dr2_ref[...]
    df_low = dr2.astype(BF)
    dy1 = dr2
    width = D
    for at in range(FF // width):
        cols = slice(at * width, (at + 1) * width)
        du_low = (nt(df_low, down_ref[cols, :]) * slope_ref[:, cols]).astype(BF)
        sums_ref[6 + at : 7 + at, :] = total(du_low.astype(F32))
        dy1 = dy1 + nt(du_low, up_ref[:, cols])
    dr1 = normalize_back(z1, inverse_ref[:, 0:1], dy1 * gain_ref[0:1, :])
    dr1_ref[...] = dr1
    moved.append(copy(dr1_ref, dr1_out, sems, 1))
    do_low = dr1.astype(BF)
    da = nt(do_low, wo_ref[...]).astype(BF)
    attn = attn_ref[...]
    to_heads = (
        lax.broadcasted_iota(jnp.int32, (D, 128), 0) // HD
        == lax.broadcasted_iota(jnp.int32, (D, 128), 1)
    ).astype(BF)
    high, middle, low = split3(da.astype(F32) * attn)
    delta = nn(high, to_heads) + nn(middle, to_heads) + nn(low, to_heads)
    lse_first, delta_first = lse_ref[...].T, delta.T
    cot = cot_ref[...].astype(F32)
    sums_ref[0:1, :] = total(dy1 * z1)
    sums_ref[1:2, :] = z2_sum_ref[...]
    sums_ref[2:3, :] = total(dy1)
    sums_ref[3:4, :] = total(cot)
    sums_ref[4:5, :] = total(do_low.astype(F32))
    sums_ref[5:6, :] = total(df_low.astype(F32))
    sums_ref[6 + FF // width :, :] = jnp.zeros((SUMS - 6 - FF // width, D), F32)
    share = D // len(starts)
    for at, start in enumerate(starts):
        packed_ref[at, :rows, :] = da[:, start : start + PAIR]
        head = start // HD
        lines = [lse_first[head : head + 2], delta_first[head : head + 2]]
        if chips > 1:
            mine = sums_ref[:6, at * share : (at + 1) * share]
            lines.append(jnp.concatenate([mine, jnp.zeros((6, 128 - share), F32)], axis=1))
            for part in range(3):
                first = at * 4 * share + part * 128
                lines.append(sums_ref[6 + first // D : 7 + first // D, first % D : first % D + 128])
        used = sum(one.shape[0] for one in lines)
        lines.append(jnp.zeros((SUMS - used, 128), F32))
        lines = jnp.concatenate(lines, axis=0)
        parts = jnp.concatenate([one.astype(F32) for one in split3(lines)], axis=0).astype(BF)
        packed_ref[at, rows:, :] = parts
    hot = hot_ref[:, at_lanes(lax.axis_index("seq"), rows)]
    high, middle, low = split3(dr1)
    docs_ref[...] = nn(hot, high) + nn(hot, middle) + nn(hot, low)
    moved.append(copy(docs_ref, docs_out, sems, 2))
    attn = attn.astype(BF)
    if chips == 1:
        high, low = split2(sums_ref[...])
        ados[0][:rows, :D] = attn
        ados[0][:rows, D:] = do_low
        ados[0][rows:, :D] = high
        ados[0][rows:, D:] = low
    else:
        near, across = lax.axis_index("seq") % 2, lax.axis_index("rows") // 2
        shares = [
            jnp.concatenate(
                [attn[:, (2 * z + y) * 96 : (2 * z + y + 1) * 96] for z in range(4)], axis=1
            )
            for y in range(2)
        ]
        sides = do_low[:, : D // 2], do_low[:, D // 2 :]
        for to, ref in enumerate(ados):
            swapped, over = to // 2, to % 2
            ref[:, : D // 2] = jnp.where(near == swapped, shares[0], shares[1])
            ref[:, D // 2 :] = jnp.where(across == over, sides[0], sides[1])
    moved += copies(zip(ados, ado_outs), sems, 3)
    wait(moved)


def heads_kernel(share, x_in, qkv_in, bias_ref, *refs):
    q_out, k_out, v_out, w_out, x_ref, q_ref, k_ref, v_ref, w_ref, wide_ref, sems = refs
    length = x_ref.shape[0]
    base, back = head_window(share)
    windows = copies(
        [
            (qkv_in.at[:, pl.ds(pl.multiple_of(base + kind * D, PAIR), 2 * PAIR)], wide_ref.at[kind])
            for kind in range(3)
        ],
        sems,
        0,
    )
    step = 256
    pieces = [slice(at * step, (at + 1) * step) for at in range(length // step)]
    loads = copies([(x_in.at[one, :], x_ref.at[one, :]) for one in pieces], sems, 3)
    biases = []
    for kind in range(3):
        windows[kind].wait()
        turned = pltpu.roll(wide_ref[kind].astype(F32), back, 1)[:, :PAIR]
        w_ref[:, kind * PAIR : (kind + 1) * PAIR] = turned.astype(BF)
        if kind == 1:
            biases.append(jnp.zeros((1, PAIR), F32))
        else:
            cols = pl.ds(pl.multiple_of(base + (kind // 2) * D, PAIR), 2 * PAIR)
            bias = jnp.broadcast_to(bias_ref[:, cols], (8, 2 * PAIR))
            biases.append(pltpu.roll(bias, back, 1)[:1, :PAIR])
    first = 3 + len(pieces)
    moved = [copy(w_ref, w_out, sems, first)]
    for at, piece in enumerate(pieces):
        loads[at].wait()
        three = nn(x_ref[piece, :], w_ref[...])
        q_ref[piece, :] = (
            (three[:, :PAIR] + biases[0]).astype(BF).astype(F32) * (HD**-0.5)
        ).astype(BF)
        k_ref[piece, :] = three[:, PAIR : 2 * PAIR].astype(BF)
        v_ref[piece, :] = (three[:, 2 * PAIR :] + biases[2]).astype(BF)
    moved += copies(((q_ref, q_out), (k_ref, k_out), (v_ref, v_out)), sems, first + 1)
    wait(moved)


def head_grad_kernel(step, share, *refs):
    w_in, q_in, k_in, v_in, hot_in, docs_in, da_ref = refs[:7]
    back_ref, heads_out, bias_ref, sums_ref = refs[7:11]
    refs = refs[1:]
    w_ref, q_ref, k_ref, v_ref, hot_ref, docs_ref = refs[10:16]
    dq_ref, dk_ref, dv_ref, heads_ref, sems = refs[16:]
    length = q_ref.shape[0]
    rows = length // (D // share)
    seq = lax.axis_index("seq")
    loads = copies(
        (
            (hot_in, hot_ref), (v_in, v_ref), (k_in, k_ref), (q_in, q_ref),
            (w_in, w_ref), (docs_in, docs_ref),
        ),
        sems,
        0,
    )
    wait(loads[:4])
    first = lax.broadcasted_iota(jnp.int32, (step, PAIR), 1) < HD
    each = step // rows
    sums = jnp.zeros((SUMS, rows), F32)
    for at in range(D // share):
        lines = da_ref[at, rows:, :].astype(F32)
        sums = sums + (lines[:SUMS] + lines[SUMS : 2 * SUMS] + lines[2 * SUMS :])
    sums_ref[...] = sums
    dk_ref[...] = jnp.zeros((length, PAIR), F32)
    dv_ref[...] = jnp.zeros((length, PAIR), F32)

    @functools.partial(loop, length // step)
    def _(at):
        piece = at_rows(at, step)
        blocks = [at * each + one for one in range(each)]
        da_all = jnp.concatenate([da_ref[one, :rows, :] for one in blocks], axis=0)
        stats = jnp.concatenate(
            [da_ref[one, rows:, :].astype(F32) for one in blocks], axis=1
        )
        stats = stats[:SUMS] + stats[SUMS : 2 * SUMS] + stats[2 * SUMS :]
        mask = (tn(hot_ref[...], hot_ref[:, at_lanes(at, step)]) - 1.0) * -MASKED
        halves = []
        for half in range(2):
            here = first if half == 0 else ~first
            q = jnp.where(here, q_ref[piece, :], jnp.zeros((step, PAIR), BF))
            da = jnp.where(here, da_all, jnp.zeros((step, PAIR), BF))
            probs = jnp.exp(nt(k_ref[...], q) + (mask - stats[half : half + 1]))
            ds = (probs * (nt(v_ref[...], da) - stats[2 + half : 3 + half])).astype(BF)
            halves.append(tn(ds, k_ref[...]))
            dk_ref[...] += nn(ds, q)
            dv_ref[...] += nn(probs.astype(BF), da)
        dq_ref[piece, :] = jnp.where(first, halves[0], halves[1]) * (HD**-0.5)

    wait(loads[4:])
    offset = seq * share - head_start(seq, share)
    left = (PAIR - offset) % PAIR
    for at in range(length // step):
        piece = slice(at * step, (at + 1) * step)
        heads_ref[piece, :] = jnp.concatenate(
            [pltpu.roll(ref[piece, :], left, 1)[:, :share] for ref in (dq_ref, dk_ref, dv_ref)],
            axis=1,
        ).astype(BF)
    moved = copy(heads_ref, heads_out, sems, 6)
    doc_sums = nn(hot_ref[...], heads_ref[...])
    bias_ref[...] = total(doc_sums)
    docs = docs_ref[...]
    for kind in range(3):
        piece = doc_sums[:, kind * share : (kind + 1) * share]
        piece = jnp.concatenate([piece, jnp.zeros((DOCS, PAIR - share), F32)], axis=1)
        parts = jnp.concatenate(split3(pltpu.roll(piece, offset, 1)), axis=0)
        product = nt(parts, w_ref[:, kind * PAIR : (kind + 1) * PAIR])
        docs = docs + (product[:DOCS] + product[DOCS : 2 * DOCS] + product[2 * DOCS :])
    docs = docs.astype(BF)
    extra = back_ref.shape[1] - 6 * DOCS
    full = 3 * share // PAIR
    rest = 3 * share % PAIR
    group = rows * rest // PAIR
    for at in range(D // share):
        for part in range(full):
            back_ref[at, part * rows : (part + 1) * rows, :] = heads_ref[
                at * rows : (at + 1) * rows, part * PAIR : (part + 1) * PAIR
            ]
        back_ref[at, full * rows : extra, :] = jnp.concatenate(
            [
                heads_ref[first : first + group, full * PAIR :]
                for first in range(at * rows, (at + 1) * rows, group)
            ],
            axis=1,
        )
        for col in range(PAIRS):
            back_ref[at, extra + col * DOCS : extra + (col + 1) * DOCS, :] = docs[
                :, col * PAIR : (col + 1) * PAIR
            ]
    moved.wait()


def head_weights_kernel(share, split, x_in, heads_in, bias_ref, *refs):
    outs, (x_ref, heads_ref, grad_ref, sems) = refs[:-4], refs[-4:]
    wait(copies(((heads_in, heads_ref), (x_in, x_ref)), sems, 0))
    if not split:
        outs[0][...] = tn(x_ref[...], heads_ref[...])
        return
    *sent, mine_ref = outs
    grad_ref[...] = tn(x_ref[...], heads_ref[...])
    rank = lax.axis_index("rows")
    part = share // split
    high, low = split2(jnp.broadcast_to(bias_ref[...], (8, 3 * share)))
    row = lax.broadcasted_iota(jnp.int32, (8, 3 * share), 0)
    tail = jnp.where(row == 0, high.astype(F32), jnp.where(row == 1, low.astype(F32), 0.0))
    for to, ref in enumerate([mine_ref] + list(sent)):
        for at in range(D // share):
            here = pl.ds(pl.multiple_of(at * share + (rank ^ to) * part, 8), part)
            ref[at, :part, :] = grad_ref[here, :].astype(ref.dtype)
            ref[at, part:, :] = tail.astype(ref.dtype)


def head_grad(apart, da, share):
    length = apart[1].shape[0]
    count = D // share
    rows = length // count
    outs = [((count, rows * 3 * share // PAIR + 6 * DOCS, PAIR), BF)]
    outs += [((length, 3 * share), BF, FAR), ((1, 3 * share), F32), ((SUMS, rows), F32)]
    scratch = [(one.shape, one.dtype) for one in apart] + [((length, PAIR), F32)] * 3
    scratch += [((length, 3 * share), BF)]
    return call(
        functools.partial(head_grad_kernel, 512, share),
        "head_grad",
        (*(far(one) for one in apart), da),
        outs,
        scratch,
        20 if length <= 1024 else 40,
        7,
    )


def head_weights(x_low, heads, bias, share, split):
    block = (D // share, share // split + 8, 3 * share) if split else (D, 3 * share)
    return call(
        functools.partial(head_weights_kernel, share, split),
        "head_weights",
        (far(x_low), far(heads), bias),
        [(block, BF)] * (split - 1) + [(block, F32)] if split else [(block, F32)],
        [(x_low.shape, BF), (heads.shape, BF), ((D, 3 * share), F32)],
        16,
        2,
    )


def input_grad_kernel(
    share, back_ref, dr1_in, qkv_in, sums_ref, grad_ref, docs_ref, dr1_ref, qkv_ref, sems
):
    loads = copies(
        [(qkv_in.at[:, c], qkv_ref.at[:, c]) for c in [slice(i * D, i * D + D) for i in range(3)]],
        sems,
        0,
    )
    loads.append(copy(dr1_in, dr1_ref, sems, 3))
    rows = dr1_ref.shape[0]
    count = D // share
    extra = back_ref.shape[1] - 6 * DOCS
    full = 3 * share // PAIR
    rest = 3 * share % PAIR
    kinds = [[], [], []]
    for at in range(count):
        here = [back_ref[at, part * rows : (part + 1) * rows, :] for part in range(full)]
        last = back_ref[at, full * rows : extra, :]
        here.append(
            jnp.concatenate([last[:, c : c + rest] for c in range(0, PAIR, rest)], axis=0)
        )
        here = jnp.concatenate(here, axis=1)
        for kind in range(3):
            kinds[kind].append(here[:, kind * share : (kind + 1) * share])
    docs = jnp.zeros((6 * DOCS, PAIR), F32)
    for at in range(count):
        docs = docs + back_ref[at, extra:, :].astype(F32)
    docs_ref[:DOCS, :] = jnp.concatenate(
        [docs[at * DOCS : (at + 1) * DOCS] for at in range(PAIRS)], axis=1
    )
    docs_ref[DOCS:, :128] = sums_ref[...]
    docs_ref[DOCS:, 128:] = jnp.zeros((SUMS, D - 128), F32)
    loads[3].wait()
    result = dr1_ref[...]
    for kind in range(3):
        cols = slice(kind * D, (kind + 1) * D)
        loads[kind].wait()
        result = result + nt(jnp.concatenate(kinds[kind], axis=1), qkv_ref[:, cols])
    grad_ref[...] = result


def unit_share(at):
    return 2 * (at % 4) + at // 4


def part_weights_kernel(up_near, bu_ref, up_out, bu_out, up_ref, sems):
    back = (384 - lax.axis_index("rows") * 96) % 384
    ups, biases = [], []
    for at in range(8):
        cols = slice(unit_share(at) * 384, (unit_share(at) + 1) * 384)
        ups.append(pltpu.roll(up_near[:, cols].astype(F32), back, 1)[:, :96].astype(BF))
        bias = jnp.broadcast_to(bu_ref[:, cols], (8, 384))
        biases.append(pltpu.roll(bias, back, 1)[:1, :96])
    up_ref[...] = jnp.concatenate(ups, axis=1)
    moved = copy(up_ref, up_out, sems, 0)
    bu_out[...] = jnp.concatenate(biases, axis=1)
    moved.wait()


def feed_grad_kernel(*refs):
    pieces = refs[:8]
    up_in, bu_ref, down_in, up_own_ref, up_sent_ref, down_own_ref, down_sent_ref = refs[8:15]
    y1_ref, df_ref, up_ref, down_ref, g_ref, du_ref, attn_ref, do_ref = refs[15:23]
    up_grad_ref, down_grad_ref, out_grad_ref, sems = refs[23:]
    seq, rank = lax.axis_index("seq"), lax.axis_index("rows")
    near, z = seq % 2, seq // 2
    rows = pieces[0].shape[0]
    here = [slice(at * rows, (at + 1) * rows) for at in range(8)]
    loads = [copy(up_in, up_ref, sems, 16)]
    loads += copies([(piece.at[:, :D], y1_ref.at[r, :]) for piece, r in zip(pieces, here)], sems, 0)
    first = rank * 96
    downs = copies(
        [
            (
                down_in.at[pl.ds(pl.multiple_of(unit_share(at) * 384 + first, 32), 96), :],
                down_ref.at[at * 96 : (at + 1) * 96, :],
            )
            for at in range(8)
        ],
        sems,
        17,
    )
    grads = copies([(piece.at[:, D : 2 * D], df_ref.at[r, :]) for piece, r in zip(pieces, here)], sems, 8)
    base = pl.multiple_of(2 * D + D // 2 + (rank % 2) * 128, 128)
    attns = slice(2 * D, 2 * D + D // 2)
    outs = copies([(piece.at[:, attns], attn_ref.at[r, :]) for piece, r in zip(pieces, here)], sems, 25)
    outs += copies(
        [(piece.at[:, pl.ds(base, 256)], do_ref.at[r, :]) for piece, r in zip(pieces, here)], sems, 33
    )
    step = 2 * rows
    wait(loads)
    wait(downs)
    wait(grads)

    @functools.partial(loop, 4)
    def _(at):
        piece = at_rows(at, step)
        u = nn(y1_ref[piece, :], up_ref[...]) + bu_ref[...]
        phi, slope = gelu_parts(u)
        g_ref[piece, :] = (u * phi).astype(BF)
        du_ref[piece, :] = (nt(df_ref[piece, :], down_ref[...]) * slope).astype(BF)

    down_grad_ref[...] = tn(g_ref[:, at_lanes(near, 384)], df_ref[...])
    up_grad_ref[...] = tn(y1_ref[...], du_ref[...])
    wait(outs)
    back = (256 - (rank % 2) * 64) % 256
    out_grad_ref[...] = pltpu.roll(tn(attn_ref[...], do_ref[...]), back, 1)
    for to in range(4):
        up_rows = pl.ds(pl.multiple_of((2 * (z ^ to) + near) * 96, 8), 96)
        down_rows = pl.ds(pl.multiple_of((z ^ to) * 96, 8), 96)
        ref = up_own_ref.at[to // 2] if to % 2 == 0 else up_sent_ref.at[to // 2]
        ref[:96, :] = up_grad_ref[up_rows, :].astype(ref.dtype)
        out = out_grad_ref[down_rows, :192]
        ref[96:, :] = jnp.concatenate(
            [out[part * 24 : (part + 1) * 24] for part in range(4)], axis=1
        ).astype(ref.dtype)
        ref = down_own_ref.at[to % 2] if to < 2 else down_sent_ref.at[to % 2]
        ref[...] = down_grad_ref[down_rows, :].astype(ref.dtype)


def feed_grad(pieces, up, bias, down):
    tokens = 8 * pieces[0].shape[0]
    blocks = (2, 120, D), (2, 96, D)
    wide = ((tokens, D), BF)
    return call(
        feed_grad_kernel,
        "feed_grad",
        (*(far(one) for one in pieces), far(up), bias, far(down)),
        [(block, dtype) for block in blocks for dtype in (F32, BF)],
        [
            wide, wide, ((D, D), BF), ((D, D), BF), wide, wide, ((tokens, D // 2), BF),
            ((tokens, 256), BF), ((D, D), F32), ((384, D), F32), ((384, 256), F32),
        ],
        26,
        41,
    )


def combine_half_kernel(*refs):
    for own_ref, got_ref, mine_ref, sent_ref in (refs[0::2], refs[1::2]):
        mine_ref[...] = own_ref[0] + got_ref[0].astype(F32)
        sent_ref[...] = (own_ref[1] + got_ref[1].astype(F32)).astype(BF)


def combine_all_kernel(up_ref, down_ref, up_got_ref, down_got_ref, out_ref):
    out_ref[:120, :] = (up_ref[...] + up_got_ref[...].astype(F32)).astype(BF)
    out_ref[120:, :] = (down_ref[...] + down_got_ref[...].astype(F32)).astype(BF)


def finish_all_kernel(a_ref, b_ref, c_ref, d_ref, up_ref, down_ref, out_ref, held_ref):
    rank = lax.axis_index("rows")
    for at, ref in enumerate((a_ref, b_ref, c_ref, d_ref)):
        held_ref[rank ^ at] = ref[:120, :].astype(F32)
        down_ref[pl.ds(pl.multiple_of((rank ^ at) * 96, 8), 96), :] = ref[120:, :].astype(F32)
    for share in range(8):
        at = (share // 2) + 4 * (share % 2)
        up_ref[:, share * 384 : (share + 1) * 384] = jnp.concatenate(
            [held_ref[r, :96, at * 96 : (at + 1) * 96] for r in range(4)], axis=1
        )
    for at in range(4):
        out_ref[at * 24 : (at + 1) * 24, :] = jnp.concatenate(
            [held_ref[r, 96:, at * 192 : (at + 1) * 192] for r in range(4)], axis=1
        )


def time_grad_kernel(*refs):
    features, docs, (out_ref, norm_ref, bias_ref, up_ref, left_ref, sems) = refs[:4], refs[4:8], refs[8:]
    seq = lax.axis_index("seq")
    wait(
        copies([(ref, left_ref.at[at * DOCS : (at + 1) * DOCS]) for at, ref in enumerate(features)], sems, 0)
    )
    left = left_ref[...].astype(F32)
    left = pltpu.roll(left, (D - seq * 96) % D, 1)[:, :96].astype(BF)
    high, middle, low = split3(jnp.concatenate([ref[:DOCS, :] for ref in docs], axis=0))
    out_ref[...] = tn(left, high) + tn(left, middle) + tn(left, low)
    sums = jnp.zeros((SUMS, 128), F32)
    for ref in docs:
        sums = sums + ref[DOCS:, :128]
    norm_ref[...] = sums[4:8, :96]
    bias_ref[...] = sums[8:10, :96]
    up_ref[...] = jnp.concatenate([sums[at : at + 1] for at in range(10, 13)], axis=1)


def finish_heads_kernel(a_ref, b_ref, c_ref, d_ref, out_ref, bias_ref):
    rank = lax.axis_index("rows")
    order = [(kind, at) for kind in range(3) for at in range(8)]
    for to, ref in enumerate((a_ref, b_ref, c_ref, d_ref)):
        value = jnp.concatenate(
            [ref[at, :24, kind * 96 : (kind + 1) * 96].astype(F32) for kind, at in order], axis=1
        )
        out_ref[pl.ds(pl.multiple_of((rank ^ to) * 24, 8), 24), :] = value
    tail = jnp.concatenate(
        [a_ref[at, 24:, kind * 96 : (kind + 1) * 96].astype(F32) for kind, at in order], axis=1
    )
    sums = tail[0:1] + tail[1:2]
    sums = jnp.concatenate([sums[:, :D], sums[:, 2 * D :]], axis=1)
    back = (2 * D - lax.axis_index("seq") * 192) % (2 * D)
    bias_ref[...] = pltpu.roll(jnp.broadcast_to(sums, (8, 2 * D)), back, 1)[:1, :192]


def combine_kernel(tail, own_ref, a_ref, b_ref, c_ref, out_ref):
    value = own_ref[...]
    for ref in (a_ref, b_ref, c_ref):
        value = value + ref[...].astype(F32)
    if tail:
        count, rows, wide = value.shape
        out_ref[:, : rows - 8, :] = value[:, : rows - 8].astype(out_ref.dtype)
        row = lax.broadcasted_iota(jnp.int32, (8, wide), 0)
        for at in range(count):
            last = value[at, rows - 8 :]
            high, low = split2(jnp.broadcast_to(last[0:1] + last[1:2], (8, wide)))
            out_ref[at, rows - 8 :, :] = jnp.where(
                row == 0, high.astype(F32), jnp.where(row == 1, low.astype(F32), 0.0)
            ).astype(out_ref.dtype)
    else:
        out_ref[...] = value.astype(out_ref.dtype)


def combine(blocks, dtype, tail=False):
    return call(
        functools.partial(combine_kernel, tail), "combine", blocks, [(blocks[0].shape, dtype)]
    )[0]


def after(value, *others):
    return lax.optimization_barrier((value,) + others)[0]


def after_all(values, *others):
    return list(lax.optimization_barrier((tuple(values), others))[0])


def gates(order):
    known = {}

    def gate(name, value):
        held = [known[one] for one in order.get(name, ()) if one in known]
        return lax.optimization_barrier((value, held))[0] if held else value

    return known, gate


def from_chips(own, over, near, both):
    pairs = [((s * 4 + r), ((s ^ 1) * 4 + (r ^ 2))) for s in range(8) for r in range(4)]
    across = lax.ppermute(both, ("seq", "rows"), pairs)
    return [own, swap(over, "rows", 2), swap(near, "seq", 1), across]


def with_twin(blocks):
    return blocks + [swap(one, "rows", 1) for one in blocks]


def spread_rows(block):
    across = swap(block, "rows", 2)
    return block, swap(block, "rows", 1), across, swap(across, "rows", 1)


def pick(blocks, index, axis=0):
    return lax.dynamic_index_in_dim(blocks, index, axis, keepdims=False)


def reduce_rows(blocks, place):
    bit = 1
    while blocks.shape[0] > 1:
        pairs = blocks.reshape((blocks.shape[0] // 2, 2) + blocks.shape[1:])
        mine = (place // bit) % 2
        sent = swap(pick(pairs, 1 - mine, 1).astype(BF), "rows", bit)
        blocks = pick(pairs, mine, 1).astype(F32) + sent.astype(F32)
        bit *= 2
    return blocks[0]


def gather_rows(block, place):
    count = lax.axis_size("rows")
    found = block[None]
    bit = count // 2
    while bit >= 1:
        other = swap(found, "rows", bit)
        mine = (place // bit) % 2
        low, high = jnp.where(mine == 0, found, other), jnp.where(mine == 0, other, found)
        if bit == count // 2:
            found = jnp.concatenate([low, high], axis=0)
        else:
            found = jnp.stack([low, high], axis=1).reshape((-1,) + block.shape)
        bit //= 2
    return found


def general_grads(ydf, ado, grad_heads, head_sums, up_weight, up_bias, down_weight):
    seqs, ranks = lax.axis_size("seq"), lax.axis_size("rows")
    seq, rank = lax.axis_index("seq"), lax.axis_index("rows")
    inner = seqs // Z_STEPS
    near = seq % inner
    share = D // seqs
    ff_share = FF // seqs
    ff_part = ff_share // ranks
    rows = ydf.shape[0]

    part = share // ranks
    grad_heads = grad_heads.reshape(seqs, ranks, part, 3 * share)
    mine = reduce_rows(jnp.moveaxis(grad_heads, 1, 0), rank)
    spread = lax.all_to_all(mine.astype(BF), "seq", 0, 0, tiled=True)
    columns = [
        spread[i, :, kind * share : (kind + 1) * share] for kind in range(3) for i in range(seqs)
    ]
    quarter = jnp.concatenate(columns, axis=1)
    grad_qkv = gather_rows(quarter, rank).reshape(share, 3 * D).astype(F32)

    def gather_near(block):
        found = [block]
        bit = 2
        while bit < ranks:
            found = found + [swap(one, "rows", bit) for one in found]
            bit *= 2
        for step in range(1, inner):
            found = found + [swap(one, "seq", step) for one in found[: len(found) // step]]
        mine = jnp.concatenate(found, axis=0)
        return jnp.concatenate([mine, swap(mine, "rows", 1)], axis=0)

    ydf_all = gather_near(ydf)
    y1_all, df_all = ydf_all[:, :D], ydf_all[:, D:]
    order = [far * inner + i for i in range(inner) for far in range(Z_STEPS)]
    ff_starts = [i * ff_share + rank * ff_part for i in order]
    take = lambda array, axis: jnp.concatenate(
        [lax.dynamic_slice_in_dim(array, a, ff_part, axis) for a in ff_starts], axis=axis
    )
    up_mine, down_mine, bias_mine = take(up_weight, 1), take(down_weight, 0), take(up_bias, 0)
    u = nn(y1_all, up_mine) + bias_mine
    phi, slope = gelu_parts(u)
    du_all = (nt(df_all, down_mine) * slope).astype(BF)
    g_all = (u * phi).astype(BF)
    group = Z_STEPS * ff_part
    g_near = lax.dynamic_slice_in_dim(g_all, near * group, group, 1)
    grad_down = tn(g_near, df_all).reshape(Z_STEPS, ff_part, D)
    grad_up = pick(tn(y1_all, du_all).reshape(Z_STEPS, inner, share, seqs * ff_part), near, 1)
    ado, grad_up, grad_down = lax.optimization_barrier((ado, grad_up, grad_down))
    ado_all = gather_near(ado[:rows])
    attn_all, do_all = ado_all[:, :D], ado_all[:, D:]
    out_part = D // ranks
    do_mine = lax.dynamic_slice_in_dim(do_all, rank * out_part, out_part, 1)
    grad_out = pick(tn(attn_all, do_mine).reshape(Z_STEPS, inner, share, out_part), near, 1)

    def reduce_far(blocks):
        blocks = blocks.astype(BF)
        far = seq // inner
        summed = pick(blocks, far).astype(F32)
        for step in range(1, Z_STEPS):
            summed = summed + swap(pick(blocks, far ^ step), "seq", step * inner).astype(F32)
        return gather_rows(summed.astype(BF), rank)

    grad_down = reduce_far(grad_down).reshape(ff_share, D).astype(F32)
    grad_up = reduce_far(grad_up).reshape(ranks, share, inner, Z_STEPS, ff_part)
    grad_up = jnp.transpose(grad_up, (1, 3, 2, 0, 4)).reshape(share, FF).astype(F32)
    grad_out = jnp.transpose(reduce_far(grad_out), (1, 0, 2)).reshape(share, D).astype(F32)

    sums = ado[rows:, :D].astype(F32) + ado[rows:, D:].astype(F32)
    placed = lambda kind: lax.dynamic_update_slice_in_dim(
        jnp.zeros((D,), F32), head_sums[0, kind * share : (kind + 1) * share], seq * share, 0
    )
    sums = sums.at[10].set(placed(0)).at[11].set(placed(2))
    for axis, count in (("rows", ranks), ("seq", seqs)):
        bit = 1
        while bit < count:
            sums = sums + swap(sums, axis, bit)
            bit *= 2
    return grad_qkv, sums[10:12].reshape(-1), grad_out, grad_up, grad_down, sums


def body(
    hidden, cotangent, segment_ids, timesteps, qkv_weight, qv_bias, out_weight, out_bias,
    up_weight, up_bias, down_weight, down_bias, norm_gain, norm_bias, time_weight,
):
    assert hidden.shape[0] == 1
    rows = hidden.shape[1]
    seqs, ranks = lax.axis_size("seq"), lax.axis_size("rows")
    length = seqs * rows
    seq, rank = lax.axis_index("seq"), lax.axis_index("rows")
    share = D // seqs
    inner = seqs // Z_STEPS
    fast = seqs == 8 and ranks == 4
    starts = [min(i * share // HD, H - 2) * HD for i in range(seqs)]

    ids = jnp.pad(segment_ids.astype(BF), ((0, 7), (0, D - rows)))
    known, gate = gates(ORDER if fast else {})
    shards = gather_seq(jnp.concatenate([hidden[0], ids], axis=0), known, gate)

    features = time_features(timesteps[0]).astype(BF)
    embed = nn(features, time_weight)
    if fast:
        all_features = spread_rows(gate("feat", features))
        known["feat"] = all_features[1:]
    else:
        all_features = gather_rows(features, rank)
        all_features = lax.dynamic_slice_in_dim(all_features, seq * share, share, 2)
    qv_row, up_row = qv_bias.reshape(1, -1), up_bias.reshape(1, -1)
    tile = ((rows, D), BF)
    tile32 = ((rows, D), F32)
    narrow32 = ((rows, 128), F32)
    wide = ((length, D), BF)
    weights = [((D, 3 * D), BF), ((D, D), BF), ((D, FF), BF), ((FF, D), BF)]
    qkv_near, out_near, up_near, down_near = call(
        fetch_kernel,
        "fetch",
        (far(gate("fetch", qkv_weight)), far(out_weight), far(up_weight), far(down_weight)),
        [(*one, NEAR) for one in weights],
        (),
        2,
        4,
    )
    out_row, down_row = out_bias.reshape(1, -1), down_bias.reshape(1, -1)
    known["fetch"] = out_near
    if fast:
        up_part, bias_part = call(
            part_weights_kernel,
            "part_weights",
            (up_near, gate("part", up_row)),
            [((D, D), BF, FAR), ((1, D), F32)],
            [((D, D), BF)],
            14,
            1,
        )
        known["part"] = bias_part
        embed = after(embed, bias_part, all_features)
    x_low, lse, attn, hot, z1, inverse1, result, ydf, dr2, slope, z2_sum = call(
        functools.partial(forward_kernel, seqs),
        "forward",
        (
            *shards, embed, qkv_near, qv_row, out_near, out_row, norm_gain,
            norm_bias, cotangent[0], up_near, up_row, down_near, down_row,
        ),
        [
            (*wide, FAR), narrow32,
            tile32, ((DOCS, length), BF), tile32, narrow32,
            tile, ((rows, 2 * D), BF), tile32, ((rows, FF), F32), ((1, D), F32),
        ],
        [((rows, length), F32), tile32, wide, wide, wide, tile],
        16 if fast else 28,
        1,
    )
    known["forward"] = z1
    if fast:
        ados = [((rows, 3 * D), BF)] * 4
    else:
        ados = [((rows + SUMS, 2 * D), BF)]
    hots = ((DOCS, length), BF)
    docs_shape = ((DOCS, D), F32)
    packed, dr1, docs, hot, *ado = call(
        functools.partial(backward_kernel, starts, len(ados)),
        "backward",
        (
            gate("backward", z1), inverse1, dr2, slope, z2_sum, attn, cotangent[0], hot, lse,
            out_near, up_near, down_near, norm_gain, ydf,
        ),
        [
            ((seqs, rows + 3 * SUMS, PAIR), BF), (*tile32, FAR), (*docs_shape, FAR), (*hots, FAR),
            *((*one, FAR) for one in ados),
        ],
        [tile32, docs_shape, ((SUMS, D), F32), *([tile] * 4 if fast else ados)],
        8,
        3 + 2 * len(ados),
    )
    known["backward"] = packed

    arrived = lax.all_to_all(gate("DA", packed), "seq", 0, 0, tiled=True)
    known["DA"] = arrived
    pair = ((length, PAIR), BF)
    head_shape = ((D, 3 * PAIR), BF)
    q_two, k_two, v_two, head_weight = call(
        functools.partial(heads_kernel, share),
        "heads",
        (far(x_low), far(qkv_weight), gate("heads", qv_row)),
        [(*one, FAR) for one in (pair, pair, pair, head_shape)],
        [wide, pair, pair, pair, head_shape, ((3, D, 2 * PAIR), BF)],
        16,
        7 + length // 256,
    )
    known["heads"] = q_two
    if fast:
        near_all = from_chips(*gate("E", ado))
        known["E"] = near_all[1:]
    back, heads, head_sums, sums = head_grad(
        (head_weight, q_two, k_two, v_two, hot, docs), gate("head", arrived), share
    )
    back, heads, head_sums, sums = gate("headend", (back, heads, head_sums, sums))
    known["head"] = back
    if fast:
        near_all = with_twin(gate("Etwin", near_all))
        known["Etwin"] = near_all[4:]
        up_own, up_sent, down_own, down_sent = feed_grad(
            near_all, up_part, gate("feed", bias_part), down_weight
        )
        known["feed"] = up_own
        up_sent, down_sent = gate("RS1", (up_sent, down_sent))
        up_got, down_got = swap(up_sent, "seq", 2), swap(down_sent, "seq", 4)
        known["RS1"] = (up_got, down_got)
    back = lax.all_to_all(gate("BACK", back), "seq", 0, 0, tiled=True)
    known["BACK"] = back
    if fast:
        up_got, down_got = gate("half", (up_got, down_got))
        up_mine, down_mine, up_sent, down_sent = call(
            combine_half_kernel, "combine_half", (up_own, down_own, up_got, down_got),
            [((120, D), F32), ((96, D), F32), ((120, D), BF), ((96, D), BF)],
        )
        known["half"] = up_mine
        up_sent, down_sent = gate("RS2", (up_sent, down_sent))
        up_got, down_got = swap(up_sent, "seq", 4), swap(down_sent, "seq", 2)
        known["RS2"] = (up_got, down_got)
    grads = head_weights(x_low, heads, gate("hw", head_sums), share, 4 if fast else 0)
    known["hw"] = grads
    if fast:
        *sent, own = gate("GRS", grads)
        sent = [swap(block, "rows", to + 1) for to, block in enumerate(sent)]
        known["GRS"] = sent
        mine = combine((own, *gate("gc", sent)), BF, True)
        known["gc"] = mine
        spread = lax.all_to_all(gate("GA2A", mine), "seq", 0, 0, tiled=True)
        known["GA2A"] = spread
    input_grad, doc_grad = call(
        functools.partial(input_grad_kernel, share),
        "input_grad",
        (gate("in", back), far(dr1), far(qkv_weight), sums),
        [tile32, ((DOCS + SUMS, D), F32)],
        [tile32, ((D, 3 * D), BF)],
        10,
        4,
    )
    known["in"] = input_grad
    if fast:
        docs_all = spread_rows(gate("DOCS", doc_grad))
        known["DOCS"] = docs_all[1:]
        up_got, down_got = gate("all", (up_got, down_got))
        merged = call(
            combine_all_kernel, "combine_all", (up_mine, down_mine, up_got, down_got),
            [((216, D), BF)],
        )[0]
        known["all"] = merged
        feed_all = spread_rows(gate("AGF", merged))
        known["AGF"] = feed_all[1:]
        heads_all = spread_rows(gate("AGG", spread))
        known["AGG"] = heads_all[1:]
        grad_time_weight, norm_sums, bias_sums, grad_up_bias = call(
            time_grad_kernel, "time_grad",
            (*(far(one) for one in all_features), *gate("time", docs_all)),
            [((share, D), F32), ((4, 96), F32), ((2, 96), F32), ((1, 384), F32)],
            [((4 * DOCS, D), BF)],
            8,
            4,
        )
        known["time"] = grad_time_weight
        grad_up_weight, grad_down_weight, grad_out_weight = call(
            finish_all_kernel, "finish_all", gate("finf", feed_all),
            [((share, FF), F32), ((FF // seqs, D), F32), ((share, D), F32)],
            [((4, 120, D), F32)],
        )
        known["finf"] = grad_out_weight
        grad_qkv_weight, grad_qv_bias = call(
            finish_heads_kernel, "finish_heads", gate("finh", heads_all),
            [((share, 3 * D), F32), ((1, 192), F32)],
        )
        grad_qv_bias, grad_up_bias = grad_qv_bias[0], grad_up_bias[0]
        grad_out_bias, grad_down_bias = bias_sums[0], bias_sums[1]
        grad_norm_gain, grad_norm_bias = norm_sums[:2], norm_sums[2:]
    else:
        doc_grad = gather_rows(doc_grad[:DOCS], rank).reshape(ranks * DOCS, D)
        grad_time_weight = lax.dot_general(
            all_features.reshape(ranks * DOCS, share).astype(F32),
            doc_grad,
            (((0,), (0,)), ((), ())),
            precision=precise,
        )
        grad_qkv_weight, qv_sums, grad_out_weight, grad_up_weight, grad_down_weight, totals = (
            general_grads(ydf, ado[0], grads[0], head_sums, up_weight, up_bias, down_weight)
        )

        def part_of(vector, axis=0):
            size = vector.shape[axis] // seqs
            return lax.dynamic_slice_in_dim(vector, seq * size, size, axis)

        grad_qv_bias, grad_out_bias = part_of(qv_sums), part_of(totals[4])
        grad_up_bias = part_of(totals[6 : 6 + FF // D].reshape(-1))
        grad_down_bias = part_of(totals[5])
        grad_norm_gain, grad_norm_bias = part_of(totals[0:2], 1), part_of(totals[2:4], 1)

    return (
        result[None],
        input_grad[None],
        grad_qkv_weight,
        grad_qv_bias,
        grad_out_weight,
        grad_out_bias,
        grad_up_weight,
        grad_up_bias,
        grad_down_weight,
        grad_down_bias,
        grad_norm_gain,
        grad_norm_bias,
        grad_time_weight,
    )


def solution(mesh):
    tokens = P("rows", "seq", None)
    whole = P()
    return jax.shard_map(
        body,
        mesh=mesh,
        in_specs=(tokens, tokens, P("rows", "seq"), P("rows", None)) + (whole,) * 11,
        out_specs=(
            tokens,
            tokens,
            P("seq", None),
            P("seq"),
            P("seq", None),
            P("seq"),
            P("seq", None),
            P("seq"),
            P("seq", None),
            P("seq"),
            P(None, "seq"),
            P(None, "seq"),
            P("seq", None),
        ),
        check_vma=False,
    )
```

```python
import functools
import math

import jax
import jax.numpy as jnp
from jax import lax
from jax.experimental import pallas as pl
from jax.experimental.pallas import tpu as pltpu
from jax.sharding import PartitionSpec as P

D = 768
H = 12
HD = 64
FF = 3072
DOCS = 16
PAIR = 2 * HD
PAIRS = D // PAIR
Z_STEPS = 4
SUMS = 16

EPS = 1e-05
MASKED = -1e30
BF = jnp.bfloat16
F32 = jnp.float32
precise = lax.Precision.HIGHEST
VMEM = pl.BlockSpec(memory_space=pltpu.VMEM)


def swap(block, axis, bit):
    return lax.ppermute(block, axis, [(i, i ^ bit) for i in range(lax.axis_size(axis))])


def dot(a, b, dims):
    return lax.dot_general(a, b, (dims, ((), ())), preferred_element_type=F32)


def nn(a, b):
    return dot(a, b, ((1,), (0,)))


def nt(a, b):
    return dot(a, b, ((1,), (1,)))


def tn(a, b):
    return dot(a, b, ((0,), (0,)))


APART = pl.BlockSpec(memory_space=pltpu.HBM)
FAR = "far"
NEAR = "near"


def far(value):
    return FAR, value


def call(kernel, name, ins, outs, scratch=(), vmem=8, copies=0):
    specs = [APART if isinstance(one, tuple) else VMEM for one in ins]
    values = [
        pltpu.with_memory_space_constraint(one[1], pltpu.HBM) if isinstance(one, tuple) else one
        for one in ins
    ]
    held = [pltpu.VMEM(*one) for one in scratch]
    if copies:
        held.append(pltpu.SemaphoreType.DMA((copies,)))
    return pl.pallas_call(
        kernel,
        out_shape=tuple(
            (pltpu.HBM if FAR in one else pltpu.VMEM)(*one[:2])
            if one[2:]
            else jax.ShapeDtypeStruct(*one)
            for one in outs
        ),
        in_specs=specs,
        out_specs=tuple(APART if FAR in one else VMEM for one in outs),
        scratch_shapes=held,
        compiler_params=pltpu.CompilerParams(vmem_limit_bytes=vmem << 20),
        cost_estimate=pl.CostEstimate(flops=int(COSTS[name] * 1e9), transcendentals=0, bytes_accessed=0),
        name=name,
    )(*values)


def copy(source, target, sems, at):
    moved = pltpu.make_async_copy(source, target, sems.at[at])
    moved.start()
    return moved


def copies(pairs, sems, first):
    return [copy(one, to, sems, first + at) for at, (one, to) in enumerate(pairs)]


def wait(moved):
    for one in moved:
        one.wait()


def loop(count, step):
    def body(at, carry):
        step(at)
        return carry

    lax.fori_loop(0, count, body, 0)


def at_rows(index, size):
    return pl.ds(pl.multiple_of(index * size, 8), size)


def at_lanes(index, size):
    return pl.ds(pl.multiple_of(index * size, 128), size)


def time_features(timesteps):
    half_width = D // 2
    frequency = jnp.exp(
        jnp.arange(half_width, dtype=F32) * (-math.log(10000.0) / half_width)
    )
    phases = timesteps.astype(F32)[..., None] * frequency
    return jnp.concatenate([jnp.sin(phases), jnp.cos(phases)], axis=-1)


def gather_seq(block, known, gate, meanwhile):
    size = lax.axis_size("seq")
    inner = size // Z_STEPS
    found = [None] * size
    found[0] = block
    for far in range(1, Z_STEPS):
        name = "Z%d" % far
        found[far * inner] = swap(gate(name, block), "seq", far * inner)
        known[name] = found[far * inner]
    for far in range(Z_STEPS):
        if far == 2:
            meanwhile()
        name = "Y%d" % far
        held = gate(name, found[far * inner])
        for near in range(1, inner):
            found[far * inner + near] = swap(held, "seq", near)
        known[name] = found[far * inner + inner - 1]
    return found


ORDER = {
    "Etwin": ("part", ),
    "RS1": ("feed", "part", ),
    "all": ("AGG", "time", ),
    "backward": ("Y3", "forward", ),
    "fetch": ("Y0", ),
    "finf": ("finh", ),
    "forward": ("Y3", ),
    "half": ("DOCS", "in", ),
    "head": ("heads", ),
    "part": ("E0", "head", ),
}
COSTS = {
    "fetch": 7, "forward": 12, "backward": 5, "heads": 3, "part_weights": 3, "feed_grad": 8,
    "head_grad": 12, "input_grad": 5, "combine_half": 1,
    "combine_all": 1, "finish_all": 2, "finish_heads": 1, "time_grad": 1,
}


def split2(value):
    high = value.astype(BF)
    return high, (value - high.astype(F32)).astype(BF)


def split3(value):
    high = value.astype(BF)
    rest = value - high.astype(F32)
    middle = rest.astype(BF)
    low = (rest - middle.astype(F32)).astype(BF)
    return high, middle, low


def head_start(seq, share):
    return jnp.minimum(seq * share // HD, H - 2) * HD


def head_window(share):
    start = head_start(lax.axis_index("seq"), share)
    base = jnp.minimum(start // PAIR, PAIRS - 2) * PAIR
    return base, (2 * PAIR - (start - base)) % (2 * PAIR)


def normalize(value):
    centered = value - jnp.mean(value, axis=-1, keepdims=True)
    inverse = lax.rsqrt(jnp.mean(centered * centered, axis=-1, keepdims=True) + EPS)
    return centered * inverse, inverse


def normalize_back(z, inverse, grad):
    return inverse * (
        grad
        - jnp.mean(grad, axis=-1, keepdims=True)
        - z * jnp.mean(grad * z, axis=-1, keepdims=True)
    )


def total(value):
    return jnp.sum(value, axis=0, keepdims=True)


def gelu_parts(u):
    phi = 0.5 * (1.0 + lax.erf(u * math.sqrt(0.5)))
    return phi, phi + u * (jnp.exp(-0.5 * u * u) * (1.0 / math.sqrt(2.0 * math.pi)))


def fetch_kernel(*refs):
    count = (len(refs) - 1) // 2
    wait(copies(zip(refs[:count], refs[count:-1]), refs[-1], 0))


def forward_kernel(count, *refs):
    shards = refs[:count]
    embed_ref, qkv_ref, bias_ref, wo_ref, bo_ref, gain_ref, off_ref = refs[count : count + 7]
    cot_ref, up_ref, bu_ref, down_ref, bd_ref = refs[count + 7 : count + 12]
    refs = refs[count + 12 :]
    xlow_out, lse_ref, attn_ref, hot_ref, z1_ref, inverse_ref = refs[:6]
    result_ref, ydf_ref, dr2_ref, slope_ref, z2_sum_ref = refs[6:11]
    mask_ref, x_ref, xlow_ref, k_ref, v_ref, q_ref, sems = refs[11:]
    seq = lax.axis_index("seq")
    rows = attn_ref.shape[0]
    width = D
    parts = [slice(at * width, (at + 1) * width) for at in range(FF // width)]
    embed = jnp.concatenate(split3(embed_ref[...]), axis=0)
    places = lax.broadcasted_iota(jnp.int32, (DOCS, rows), 0).astype(F32)
    hot_own = None
    for at in range(count):
        ids = shards[at][rows : rows + 8, :rows].astype(F32)[:1]
        hot = (places == ids).astype(BF)
        hot_ref[:, at_lanes(seq ^ at, rows)] = hot
        x = shards[at][:rows, :].astype(F32) + tn(jnp.concatenate([hot] * 3, axis=0), embed)
        if at == 0:
            hot_own = hot
            x_ref[...] = x
            own = x.astype(BF)
        xlow_ref[at_rows(seq ^ at, rows), :] = x.astype(BF)
    moved = copy(xlow_ref, xlow_out, sems, 0)
    q_ref[...] = (
        (nn(own, qkv_ref[:, :D]) + bias_ref[:, :D]).astype(BF).astype(F32) * (HD**-0.5)
    ).astype(BF)
    step = 2 * rows
    for at in range(count * rows // step):
        piece = slice(at * step, (at + 1) * step)
        every = xlow_ref[piece, :]
        k_ref[piece, :] = nn(every, qkv_ref[:, D : 2 * D]).astype(BF)
        v_ref[piece, :] = (nn(every, qkv_ref[:, 2 * D :]) + bias_ref[:, D:]).astype(BF)
    mask_ref[...] = (tn(hot_own, hot_ref[...]) - 1.0) * -MASKED
    first = lax.broadcasted_iota(jnp.int32, (rows, PAIR), 1) < HD
    lane = lax.broadcasted_iota(jnp.int32, (rows, 128), 1)
    lse = jnp.zeros((rows, 128), F32)
    for pair in range(PAIRS):
        cols = slice(pair * PAIR, (pair + 1) * PAIR)
        q = q_ref[:, cols]
        halves = []
        for half in range(2):
            q_one = jnp.where(first if half == 0 else ~first, q, jnp.zeros_like(q))
            scores = nt(q_one, k_ref[:, cols]) + mask_ref[...]
            top = jnp.max(scores, axis=-1, keepdims=True)
            weights = jnp.exp(scores - top)
            summed = jnp.sum(weights, axis=-1, keepdims=True)
            halves.append(nn(weights.astype(BF), v_ref[:, cols]) / summed)
            lse = jnp.where(lane == 2 * pair + half, top + jnp.log(summed), lse)
        attn_ref[:, cols] = jnp.where(first, halves[0], halves[1])
    lse_ref[...] = lse
    z1, inverse = normalize(x_ref[...] + nn(attn_ref[...].astype(BF), wo_ref[...]) + bo_ref[...])
    z1_ref[...] = z1
    inverse_ref[...] = jnp.broadcast_to(inverse, (rows, 128))
    y1 = z1 * gain_ref[0:1, :] + off_ref[0:1, :]
    y1_low = y1.astype(BF)
    ydf_ref[:, :D] = y1_low
    r2 = y1 + bd_ref[...]
    for cols in parts:
        u = nn(y1_low, up_ref[:, cols]) + bu_ref[:, cols]
        phi, slope = gelu_parts(u)
        slope_ref[:, cols] = slope
        r2 = r2 + nn((u * phi).astype(BF), down_ref[cols, :])
    z2, inverse2 = normalize(r2)
    result_ref[...] = (z2 * gain_ref[1:2, :] + off_ref[1:2, :]).astype(BF)
    cot = cot_ref[...].astype(F32)
    dr2 = normalize_back(z2, inverse2, cot * gain_ref[1:2, :])
    ydf_ref[:, D:] = dr2.astype(BF)
    dr2_ref[...] = dr2
    z2_sum_ref[...] = total(cot * z2)
    moved.wait()


def backward_kernel(
    starts, chips,
    z1_ref, inverse_ref, dr2_ref, slope_ref, z2_sum_ref, attn_ref, cot_ref, hot_ref, lse_ref,
    wo_ref, up_ref, down_ref, gain_ref, ydf_ref,
    packed_ref, dr1_out, docs_out, hot_out, *refs,
):
    ado_outs, ados = refs[:chips], refs[-chips - 1 : -1]
    dr1_ref, docs_ref, sums_ref = refs[chips : chips + 3]
    sems = refs[-1]
    rows = z1_ref.shape[0]
    moved = [copy(hot_ref, hot_out, sems, 0)]
    if chips > 1:
        moved += copies([(ydf_ref, one.at[:, : 2 * D]) for one in ado_outs], sems, 3 + chips)
        ado_outs = [one.at[:, 2 * D :] for one in ado_outs]
    z1 = z1_ref[...]
    dr2 = dr2_ref[...]
    df_low = dr2.astype(BF)
    dy1 = dr2
    width = D
    for at in range(FF // width):
        cols = slice(at * width, (at + 1) * width)
        du_low = (nt(df_low, down_ref[cols, :]) * slope_ref[:, cols]).astype(BF)
        sums_ref[6 + at : 7 + at, :] = total(du_low.astype(F32))
        dy1 = dy1 + nt(du_low, up_ref[:, cols])
    dr1 = normalize_back(z1, inverse_ref[:, 0:1], dy1 * gain_ref[0:1, :])
    dr1_ref[...] = dr1
    moved.append(copy(dr1_ref, dr1_out, sems, 1))
    do_low = dr1.astype(BF)
    da = nt(do_low, wo_ref[...]).astype(BF)
    attn = attn_ref[...]
    to_heads = (
        lax.broadcasted_iota(jnp.int32, (D, 128), 0) // HD
        == lax.broadcasted_iota(jnp.int32, (D, 128), 1)
    ).astype(BF)
    high, middle, low = split3(da.astype(F32) * attn)
    delta = nn(high, to_heads) + nn(middle, to_heads) + nn(low, to_heads)
    lse_first, delta_first = lse_ref[...].T, delta.T
    cot = cot_ref[...].astype(F32)
    sums_ref[0:1, :] = total(dy1 * z1)
    sums_ref[1:2, :] = z2_sum_ref[...]
    sums_ref[2:3, :] = total(dy1)
    sums_ref[3:4, :] = total(cot)
    sums_ref[4:5, :] = total(do_low.astype(F32))
    sums_ref[5:6, :] = total(df_low.astype(F32))
    sums_ref[6 + FF // width :, :] = jnp.zeros((SUMS - 6 - FF // width, D), F32)
    share = D // len(starts)
    for at, start in enumerate(starts):
        packed_ref[at, :rows, :] = da[:, start : start + PAIR]
        head = start // HD
        lines = [lse_first[head : head + 2], delta_first[head : head + 2]]
        if chips > 1:
            mine = sums_ref[:6, at * share : (at + 1) * share]
            lines.append(jnp.concatenate([mine, jnp.zeros((6, 128 - share), F32)], axis=1))
            for part in range(3):
                first = at * 4 * share + part * 128
                lines.append(sums_ref[6 + first // D : 7 + first // D, first % D : first % D + 128])
        used = sum(one.shape[0] for one in lines)
        lines.append(jnp.zeros((SUMS - used, 128), F32))
        lines = jnp.concatenate(lines, axis=0)
        parts = jnp.concatenate([one.astype(F32) for one in split3(lines)], axis=0).astype(BF)
        packed_ref[at, rows:, :] = parts
    hot = hot_ref[:, at_lanes(lax.axis_index("seq"), rows)]
    high, middle, low = split3(dr1)
    docs_ref[...] = nn(hot, high) + nn(hot, middle) + nn(hot, low)
    moved.append(copy(docs_ref, docs_out, sems, 2))
    attn = attn.astype(BF)
    if chips == 1:
        high, low = split2(sums_ref[...])
        ados[0][:rows, :D] = attn
        ados[0][:rows, D:] = do_low
        ados[0][rows:, :D] = high
        ados[0][rows:, D:] = low
    else:
        near, across = lax.axis_index("seq") % 2, lax.axis_index("rows") // 2
        shares = [
            jnp.concatenate(
                [attn[:, (2 * z + y) * 96 : (2 * z + y + 1) * 96] for z in range(4)], axis=1
            )
            for y in range(2)
        ]
        sides = do_low[:, : D // 2], do_low[:, D // 2 :]
        for to, ref in enumerate(ados):
            swapped, over = to // 2, to % 2
            ref[:, : D // 2] = jnp.where(near == swapped, shares[0], shares[1])
            ref[:, D // 2 :] = jnp.where(across == over, sides[0], sides[1])
    moved += copies(zip(ados, ado_outs), sems, 3)
    wait(moved)


def heads_kernel(share, x_in, qkv_in, bias_ref, *refs):
    q_out, k_out, v_out, w_out, x_ref, q_ref, k_ref, v_ref, w_ref, wide_ref, sems = refs
    length = x_ref.shape[0]
    base, back = head_window(share)
    windows = copies(
        [
            (qkv_in.at[:, pl.ds(pl.multiple_of(base + kind * D, PAIR), 2 * PAIR)], wide_ref.at[kind])
            for kind in range(3)
        ],
        sems,
        0,
    )
    step = 256
    pieces = [slice(at * step, (at + 1) * step) for at in range(length // step)]
    loads = copies([(x_in.at[one, :], x_ref.at[one, :]) for one in pieces], sems, 3)
    biases = []
    for kind in range(3):
        windows[kind].wait()
        turned = pltpu.roll(wide_ref[kind].astype(F32), back, 1)[:, :PAIR]
        w_ref[:, kind * PAIR : (kind + 1) * PAIR] = turned.astype(BF)
        if kind == 1:
            biases.append(jnp.zeros((1, PAIR), F32))
        else:
            cols = pl.ds(pl.multiple_of(base + (kind // 2) * D, PAIR), 2 * PAIR)
            bias = jnp.broadcast_to(bias_ref[:, cols], (8, 2 * PAIR))
            biases.append(pltpu.roll(bias, back, 1)[:1, :PAIR])
    first = 3 + len(pieces)
    moved = [copy(w_ref, w_out, sems, first)]
    for at, piece in enumerate(pieces):
        loads[at].wait()
        three = nn(x_ref[piece, :], w_ref[...])
        q_ref[piece, :] = (
            (three[:, :PAIR] + biases[0]).astype(BF).astype(F32) * (HD**-0.5)
        ).astype(BF)
        k_ref[piece, :] = three[:, PAIR : 2 * PAIR].astype(BF)
        v_ref[piece, :] = (three[:, 2 * PAIR :] + biases[2]).astype(BF)
    moved += copies(((q_ref, q_out), (k_ref, k_out), (v_ref, v_out)), sems, first + 1)
    wait(moved)


def head_grad_kernel(step, share, split, *refs):
    w_in, q_in, k_in, v_in, hot_in, docs_in, x_in, da_ref, back_ref, sums_ref = refs[:10]
    w_ref, q_ref, k_ref, v_ref, hot_ref, docs_ref, x_ref = refs[-13:-6]
    dq_ref, dk_ref, dv_ref, heads_ref, grad_ref, sems = refs[-6:]
    outs = refs[10:-13]
    if split:
        *outs, own_ref = outs
    length = q_ref.shape[0]
    rows = length // (D // share)
    seq = lax.axis_index("seq")
    loads = copies(
        (
            (hot_in, hot_ref), (v_in, v_ref), (k_in, k_ref), (q_in, q_ref),
            (w_in, w_ref), (docs_in, docs_ref), (x_in, x_ref),
        ),
        sems,
        0,
    )
    wait(loads[:4])
    first = lax.broadcasted_iota(jnp.int32, (step, PAIR), 1) < HD
    each = step // rows
    sums = jnp.zeros((SUMS, rows), F32)
    for at in range(D // share):
        lines = da_ref[at, rows:, :].astype(F32)
        sums = sums + (lines[:SUMS] + lines[SUMS : 2 * SUMS] + lines[2 * SUMS :])
    sums_ref[...] = sums
    dk_ref[...] = jnp.zeros((length, PAIR), F32)
    dv_ref[...] = jnp.zeros((length, PAIR), F32)

    @functools.partial(loop, length // step)
    def _(at):
        piece = at_rows(at, step)
        blocks = [at * each + one for one in range(each)]
        da_all = jnp.concatenate([da_ref[one, :rows, :] for one in blocks], axis=0)
        stats = jnp.concatenate(
            [da_ref[one, rows:, :].astype(F32) for one in blocks], axis=1
        )
        stats = stats[:SUMS] + stats[SUMS : 2 * SUMS] + stats[2 * SUMS :]
        mask = (tn(hot_ref[...], hot_ref[:, at_lanes(at, step)]) - 1.0) * -MASKED
        halves = []
        for half in range(2):
            here = first if half == 0 else ~first
            q = jnp.where(here, q_ref[piece, :], jnp.zeros((step, PAIR), BF))
            da = jnp.where(here, da_all, jnp.zeros((step, PAIR), BF))
            probs = jnp.exp(nt(k_ref[...], q) + (mask - stats[half : half + 1]))
            ds = (probs * (nt(v_ref[...], da) - stats[2 + half : 3 + half])).astype(BF)
            halves.append(tn(ds, k_ref[...]))
            dk_ref[...] += nn(ds, q)
            dv_ref[...] += nn(probs.astype(BF), da)
        dq_ref[piece, :] = jnp.where(first, halves[0], halves[1]) * (HD**-0.5)

    wait(loads[4:])
    offset = seq * share - head_start(seq, share)
    left = (PAIR - offset) % PAIR
    for at in range(length // step):
        piece = slice(at * step, (at + 1) * step)
        heads_ref[piece, :] = jnp.concatenate(
            [pltpu.roll(ref[piece, :], left, 1)[:, :share] for ref in (dq_ref, dk_ref, dv_ref)],
            axis=1,
        ).astype(BF)
    doc_sums = nn(hot_ref[...], heads_ref[...])
    docs = docs_ref[...]
    for kind in range(3):
        piece = doc_sums[:, kind * share : (kind + 1) * share]
        piece = jnp.concatenate([piece, jnp.zeros((DOCS, PAIR - share), F32)], axis=1)
        parts = jnp.concatenate(split3(pltpu.roll(piece, offset, 1)), axis=0)
        product = nt(parts, w_ref[:, kind * PAIR : (kind + 1) * PAIR])
        docs = docs + (product[:DOCS] + product[DOCS : 2 * DOCS] + product[2 * DOCS :])
    docs = docs.astype(BF)
    extra = back_ref.shape[1] - 6 * DOCS
    full = 3 * share // PAIR
    rest = 3 * share % PAIR
    group = rows * rest // PAIR
    for at in range(D // share):
        for part in range(full):
            back_ref[at, part * rows : (part + 1) * rows, :] = heads_ref[
                at * rows : (at + 1) * rows, part * PAIR : (part + 1) * PAIR
            ]
        back_ref[at, full * rows : extra, :] = jnp.concatenate(
            [
                heads_ref[first : first + group, full * PAIR :]
                for first in range(at * rows, (at + 1) * rows, group)
            ],
            axis=1,
        )
        for col in range(PAIRS):
            back_ref[at, extra + col * DOCS : extra + (col + 1) * DOCS, :] = docs[
                :, col * PAIR : (col + 1) * PAIR
            ]
    if not split:
        outs[0][...] = tn(x_ref[...], heads_ref[...])
        outs[1][...] = total(doc_sums)
        return
    *sent, mine_out = outs
    grad_ref[...] = tn(x_ref[...], heads_ref[...])
    rank = lax.axis_index("rows")
    part = share // split
    high, low = split2(jnp.broadcast_to(total(doc_sums), (8, 3 * share)))
    row = lax.broadcasted_iota(jnp.int32, (8, 3 * share), 0)
    tail = jnp.where(row == 0, high.astype(F32), jnp.where(row == 1, low.astype(F32), 0.0))
    for to, ref in enumerate([own_ref] + list(sent)):
        for at in range(D // share):
            here = pl.ds(pl.multiple_of(at * share + (rank ^ to) * part, 8), part)
            ref[at, :part, :] = grad_ref[here, :].astype(ref.dtype)
            ref[at, part:, :] = tail.astype(ref.dtype)
        if to == 0:
            moved = copy(own_ref, mine_out, sems, 7)
    moved.wait()


def head_grad(apart, da, share, split):
    length = apart[1].shape[0]
    count = D // share
    rows = length // count
    outs = [((count, rows * 3 * share // PAIR + 6 * DOCS, PAIR), BF), ((SUMS, rows), F32)]
    if split:
        block = (count, share // split + 8, 3 * share)
        outs += [(block, BF)] * (split - 1) + [(block, F32, FAR)]
    else:
        outs += [((D, 3 * share), F32), ((1, 3 * share), F32)]
    scratch = [(block, F32)] if split else []
    scratch += [(one.shape, one.dtype) for one in apart] + [((length, PAIR), F32)] * 3
    scratch += [((length, 3 * share), BF), ((D, 3 * share), F32)]
    return call(
        functools.partial(head_grad_kernel, 512, share, split),
        "head_grad",
        (*(far(one) for one in apart), da),
        outs,
        scratch,
        24 if length <= 1024 else 44,
        8,
    )


def combine(blocks, out_ref):
    value = blocks[0][...]
    for ref in blocks[1:]:
        value = value + ref[...].astype(F32)
    count, rows, wide = value.shape
    out_ref[:, : rows - 8, :] = value[:, : rows - 8].astype(out_ref.dtype)
    row = lax.broadcasted_iota(jnp.int32, (8, wide), 0)
    for at in range(count):
        last = value[at, rows - 8 :]
        high, low = split2(jnp.broadcast_to(last[0:1] + last[1:2], (8, wide)))
        out_ref[at, rows - 8 :, :] = jnp.where(
            row == 0, high.astype(F32), jnp.where(row == 1, low.astype(F32), 0.0)
        ).astype(out_ref.dtype)


def input_grad_kernel(share, back_ref, dr1_in, qkv_in, sums_ref, *refs):
    blocks = ()
    if len(refs) > 5:
        blocks, held, refs = refs[:4], refs[-5:-1], refs[4:-5] + refs[-1:]
    grad_ref, docs_ref, *mine_ref, dr1_ref, qkv_ref, sems = refs
    blocks = copies(zip(blocks, held), sems, 4) if blocks else ()
    loads = copies(
        [(qkv_in.at[:, c], qkv_ref.at[:, c]) for c in [slice(i * D, i * D + D) for i in range(3)]],
        sems,
        0,
    )
    loads.append(copy(dr1_in, dr1_ref, sems, 3))
    rows = dr1_ref.shape[0]
    count = D // share
    extra = back_ref.shape[1] - 6 * DOCS
    full = 3 * share // PAIR
    rest = 3 * share % PAIR
    kinds = [[], [], []]
    for at in range(count):
        here = [back_ref[at, part * rows : (part + 1) * rows, :] for part in range(full)]
        last = back_ref[at, full * rows : extra, :]
        here.append(
            jnp.concatenate([last[:, c : c + rest] for c in range(0, PAIR, rest)], axis=0)
        )
        here = jnp.concatenate(here, axis=1)
        for kind in range(3):
            kinds[kind].append(here[:, kind * share : (kind + 1) * share])
    docs = jnp.zeros((6 * DOCS, PAIR), F32)
    for at in range(count):
        docs = docs + back_ref[at, extra:, :].astype(F32)
    docs_ref[:DOCS, :] = jnp.concatenate(
        [docs[at * DOCS : (at + 1) * DOCS] for at in range(PAIRS)], axis=1
    )
    docs_ref[DOCS:, :128] = sums_ref[...]
    docs_ref[DOCS:, 128:] = jnp.zeros((SUMS, D - 128), F32)
    loads[3].wait()
    result = dr1_ref[...]
    for kind in range(3):
        cols = slice(kind * D, (kind + 1) * D)
        loads[kind].wait()
        result = result + nt(jnp.concatenate(kinds[kind], axis=1), qkv_ref[:, cols])
    grad_ref[...] = result
    if blocks:
        wait(blocks)
        combine(held, mine_ref[0])


def unit_share(at):
    return 2 * (at % 4) + at // 4


def part_weights_kernel(up_in, bu_ref, up_out, bu_out, held_ref, up_ref, sems):
    back = (384 - lax.axis_index("rows") * 96) % 384
    loads = copies(
        [
            (up_in.at[:, unit_share(at) * 384 : (unit_share(at) + 1) * 384], held_ref.at[at])
            for at in range(8)
        ],
        sems,
        0,
    )
    ups, biases = [], []
    for at in range(8):
        cols = slice(unit_share(at) * 384, (unit_share(at) + 1) * 384)
        loads[at].wait()
        ups.append(pltpu.roll(held_ref[at].astype(F32), back, 1)[:, :96].astype(BF))
        bias = jnp.broadcast_to(bu_ref[:, cols], (8, 384))
        biases.append(pltpu.roll(bias, back, 1)[:1, :96])
    up_ref[...] = jnp.concatenate(ups, axis=1)
    moved = copy(up_ref, up_out, sems, 8)
    bu_out[...] = jnp.concatenate(biases, axis=1)
    moved.wait()


def feed_grad_kernel(*refs):
    pieces = refs[:8]
    up_in, bu_ref, down_in, up_own_out, up_sent_ref, down_own_out, down_sent_ref = refs[8:15]
    all_ref, up_ref, down_ref, g_ref, du_ref = refs[15:20]
    up_grad_ref, down_grad_ref, out_grad_ref, up_own_ref, down_own_ref, sems = refs[20:]
    seq, rank = lax.axis_index("seq"), lax.axis_index("rows")
    near, z = seq % 2, seq // 2
    rows = pieces[0].shape[0]
    loads = [copy(up_in, up_ref, sems, 8)]
    loads += copies([(pieces[at], all_ref.at[at]) for at in range(2)], sems, 0)
    first = rank * 96
    downs = copies(
        [
            (
                down_in.at[pl.ds(pl.multiple_of(unit_share(at) * 384 + first, 32), 96), :],
                down_ref.at[at * 96 : (at + 1) * 96, :],
            )
            for at in range(8)
        ],
        sems,
        9,
    )
    loads += copies([(pieces[at], all_ref.at[at]) for at in range(2, 8)], sems, 2)
    loads[0].wait()
    step = 2 * rows
    for at in range(4):
        wait(loads[1 + 2 * at : 3 + 2 * at])
        piece = slice(at * step, (at + 1) * step)
        two = slice(2 * at, 2 * at + 2)
        u = nn(all_ref[two, :, :D].reshape(step, D), up_ref[...]) + bu_ref[...]
        phi, slope = gelu_parts(u)
        if at == 0:
            wait(downs)
        g_ref[piece, :] = (u * phi).astype(BF)
        df = all_ref[two, :, D : 2 * D].reshape(step, D)
        du_ref[piece, :] = (nt(df, down_ref[...]) * slope).astype(BF)

    tokens = 8 * rows
    df = all_ref[:, :, D : 2 * D].reshape(tokens, D)
    down_grad_ref[...] = tn(g_ref[:, at_lanes(near, 384)], df)
    up_grad_ref[...] = tn(all_ref[:, :, :D].reshape(tokens, D), du_ref[...])
    base = pl.multiple_of(2 * D + D // 2 + (rank % 2) * 128, 128)
    attn = all_ref[:, :, 2 * D : 2 * D + D // 2].reshape(tokens, D // 2)
    do = all_ref[:, :, pl.ds(base, 256)].reshape(tokens, 256)
    back = (256 - (rank % 2) * 64) % 256
    out_grad_ref[...] = pltpu.roll(tn(attn, do), back, 1)
    for to in range(4):
        up_rows = pl.ds(pl.multiple_of((2 * (z ^ to) + near) * 96, 8), 96)
        down_rows = pl.ds(pl.multiple_of((z ^ to) * 96, 8), 96)
        ref = up_own_ref.at[to // 2] if to % 2 == 0 else up_sent_ref.at[to // 2]
        ref[:96, :] = up_grad_ref[up_rows, :].astype(ref.dtype)
        out = out_grad_ref[down_rows, :192]
        ref[96:, :] = jnp.concatenate(
            [out[part * 24 : (part + 1) * 24] for part in range(4)], axis=1
        ).astype(ref.dtype)
        ref = down_own_ref.at[to % 2] if to < 2 else down_sent_ref.at[to % 2]
        ref[...] = down_grad_ref[down_rows, :].astype(ref.dtype)
    wait(copies(((up_own_ref, up_own_out), (down_own_ref, down_own_out)), sems, 17))


def feed_grad(pieces, up, bias, down):
    tokens = 8 * pieces[0].shape[0]
    blocks = (2, 120, D), (2, 96, D)
    wide = ((tokens, D), BF)
    return call(
        feed_grad_kernel,
        "feed_grad",
        (*(far(one) for one in pieces), far(up), bias, far(down)),
        [one for block in blocks for one in ((block, F32, FAR), (block, BF))],
        [
            ((8, tokens // 8, 3 * D), BF), ((D, D), BF), ((D, D), BF), wide, wide,
            ((D, D), F32), ((384, D), F32), ((384, 256), F32),
            *((block, F32) for block in blocks),
        ],
        28,
        19,
    )


def combine_half_kernel(up_in, down_in, up_got_in, down_got_in, up_ref, down_ref, *refs):
    *held, sems = refs
    loads = copies(zip((up_in, down_in, up_got_in, down_got_in), held), sems, 0)
    wait(loads)
    up_ref[...] = (held[0][1] + held[2][1].astype(F32)).astype(BF)
    down_ref[...] = (held[1][1] + held[3][1].astype(F32)).astype(BF)


def combine_all_kernel(up_in, down_in, up_got_in, down_got_in, up_last_ref, down_last_ref, out_ref, *refs):
    *held, sems = refs
    sources = [one.at[0] for one in (up_in, down_in, up_got_in, down_got_in)]
    wait(copies(zip(sources, held), sems, 0))
    up = held[0][...] + held[2][...].astype(F32) + up_last_ref[...].astype(F32)
    down = held[1][...] + held[3][...].astype(F32) + down_last_ref[...].astype(F32)
    out_ref[:120, :] = up.astype(BF)
    out_ref[120:, :] = down.astype(BF)


def finish_all_kernel(a_ref, b_ref, c_ref, d_ref, up_ref, down_ref, out_ref, held_ref):
    rank = lax.axis_index("rows")
    for at, ref in enumerate((a_ref, b_ref, c_ref, d_ref)):
        held_ref[rank ^ at] = ref[:120, :].astype(F32)
        down_ref[pl.ds(pl.multiple_of((rank ^ at) * 96, 8), 96), :] = ref[120:, :].astype(F32)
    for share in range(8):
        at = (share // 2) + 4 * (share % 2)
        up_ref[:, share * 384 : (share + 1) * 384] = jnp.concatenate(
            [held_ref[r, :96, at * 96 : (at + 1) * 96] for r in range(4)], axis=1
        )
    for at in range(4):
        out_ref[at * 24 : (at + 1) * 24, :] = jnp.concatenate(
            [held_ref[r, 96:, at * 192 : (at + 1) * 192] for r in range(4)], axis=1
        )


def time_grad_kernel(*refs):
    features, docs, (out_ref, norm_ref, bias_ref, up_ref, left_ref, sems) = refs[:4], refs[4:8], refs[8:]
    seq = lax.axis_index("seq")
    wait(
        copies([(ref, left_ref.at[at * DOCS : (at + 1) * DOCS]) for at, ref in enumerate(features)], sems, 0)
    )
    left = left_ref[...].astype(F32)
    left = pltpu.roll(left, (D - seq * 96) % D, 1)[:, :96].astype(BF)
    high, middle, low = split3(jnp.concatenate([ref[:DOCS, :] for ref in docs], axis=0))
    out_ref[...] = tn(left, high) + tn(left, middle) + tn(left, low)
    sums = jnp.zeros((SUMS, 128), F32)
    for ref in docs:
        sums = sums + ref[DOCS:, :128]
    norm_ref[...] = sums[4:8, :96]
    bias_ref[...] = sums[8:10, :96]
    up_ref[...] = jnp.concatenate([sums[at : at + 1] for at in range(10, 13)], axis=1)


def finish_heads_kernel(a_ref, b_ref, c_ref, d_ref, out_ref, bias_ref):
    rank = lax.axis_index("rows")
    order = [(kind, at) for kind in range(3) for at in range(8)]
    for to, ref in enumerate((a_ref, b_ref, c_ref, d_ref)):
        value = jnp.concatenate(
            [ref[at, :24, kind * 96 : (kind + 1) * 96].astype(F32) for kind, at in order], axis=1
        )
        out_ref[pl.ds(pl.multiple_of((rank ^ to) * 24, 8), 24), :] = value
    tail = jnp.concatenate(
        [a_ref[at, 24:, kind * 96 : (kind + 1) * 96].astype(F32) for kind, at in order], axis=1
    )
    sums = tail[0:1] + tail[1:2]
    sums = jnp.concatenate([sums[:, :D], sums[:, 2 * D :]], axis=1)
    back = (2 * D - lax.axis_index("seq") * 192) % (2 * D)
    bias_ref[...] = pltpu.roll(jnp.broadcast_to(sums, (8, 2 * D)), back, 1)[:1, :192]


def after(value, *others):
    return lax.optimization_barrier((value,) + others)[0]


def after_all(values, *others):
    return list(lax.optimization_barrier((tuple(values), others))[0])


def gates(order):
    known = {}

    def gate(name, value):
        held = [known[one] for one in order.get(name, ()) if one in known]
        return lax.optimization_barrier((value, held))[0] if held else value

    return known, gate


def from_chips(own, over, near, both):
    pairs = [((s * 4 + r), ((s ^ 1) * 4 + (r ^ 2))) for s in range(8) for r in range(4)]
    across = lax.ppermute(both, ("seq", "rows"), pairs)
    return [own, swap(over, "rows", 2), swap(near, "seq", 1), across]


def with_twin(blocks):
    return blocks + [swap(one, "rows", 1) for one in blocks]


def spread_rows(block):
    across = swap(block, "rows", 2)
    return block, swap(block, "rows", 1), across, swap(across, "rows", 1)


def pick(blocks, index, axis=0):
    return lax.dynamic_index_in_dim(blocks, index, axis, keepdims=False)


def reduce_rows(blocks, place):
    bit = 1
    while blocks.shape[0] > 1:
        pairs = blocks.reshape((blocks.shape[0] // 2, 2) + blocks.shape[1:])
        mine = (place // bit) % 2
        sent = swap(pick(pairs, 1 - mine, 1).astype(BF), "rows", bit)
        blocks = pick(pairs, mine, 1).astype(F32) + sent.astype(F32)
        bit *= 2
    return blocks[0]


def gather_rows(block, place):
    count = lax.axis_size("rows")
    found = block[None]
    bit = count // 2
    while bit >= 1:
        other = swap(found, "rows", bit)
        mine = (place // bit) % 2
        low, high = jnp.where(mine == 0, found, other), jnp.where(mine == 0, other, found)
        if bit == count // 2:
            found = jnp.concatenate([low, high], axis=0)
        else:
            found = jnp.stack([low, high], axis=1).reshape((-1,) + block.shape)
        bit //= 2
    return found


def general_grads(ydf, ado, grad_heads, head_sums, up_weight, up_bias, down_weight):
    seqs, ranks = lax.axis_size("seq"), lax.axis_size("rows")
    seq, rank = lax.axis_index("seq"), lax.axis_index("rows")
    inner = seqs // Z_STEPS
    near = seq % inner
    share = D // seqs
    ff_share = FF // seqs
    ff_part = ff_share // ranks
    rows = ydf.shape[0]

    part = share // ranks
    grad_heads = grad_heads.reshape(seqs, ranks, part, 3 * share)
    mine = reduce_rows(jnp.moveaxis(grad_heads, 1, 0), rank)
    spread = lax.all_to_all(mine.astype(BF), "seq", 0, 0, tiled=True)
    columns = [
        spread[i, :, kind * share : (kind + 1) * share] for kind in range(3) for i in range(seqs)
    ]
    quarter = jnp.concatenate(columns, axis=1)
    grad_qkv = gather_rows(quarter, rank).reshape(share, 3 * D).astype(F32)

    def gather_near(block):
        found = [block]
        bit = 2
        while bit < ranks:
            found = found + [swap(one, "rows", bit) for one in found]
            bit *= 2
        for step in range(1, inner):
            found = found + [swap(one, "seq", step) for one in found[: len(found) // step]]
        mine = jnp.concatenate(found, axis=0)
        return jnp.concatenate([mine, swap(mine, "rows", 1)], axis=0)

    ydf_all = gather_near(ydf)
    y1_all, df_all = ydf_all[:, :D], ydf_all[:, D:]
    order = [far * inner + i for i in range(inner) for far in range(Z_STEPS)]
    ff_starts = [i * ff_share + rank * ff_part for i in order]
    take = lambda array, axis: jnp.concatenate(
        [lax.dynamic_slice_in_dim(array, a, ff_part, axis) for a in ff_starts], axis=axis
    )
    up_mine, down_mine, bias_mine = take(up_weight, 1), take(down_weight, 0), take(up_bias, 0)
    u = nn(y1_all, up_mine) + bias_mine
    phi, slope = gelu_parts(u)
    du_all = (nt(df_all, down_mine) * slope).astype(BF)
    g_all = (u * phi).astype(BF)
    group = Z_STEPS * ff_part
    g_near = lax.dynamic_slice_in_dim(g_all, near * group, group, 1)
    grad_down = tn(g_near, df_all).reshape(Z_STEPS, ff_part, D)
    grad_up = pick(tn(y1_all, du_all).reshape(Z_STEPS, inner, share, seqs * ff_part), near, 1)
    ado, grad_up, grad_down = lax.optimization_barrier((ado, grad_up, grad_down))
    ado_all = gather_near(ado[:rows])
    attn_all, do_all = ado_all[:, :D], ado_all[:, D:]
    out_part = D // ranks
    do_mine = lax.dynamic_slice_in_dim(do_all, rank * out_part, out_part, 1)
    grad_out = pick(tn(attn_all, do_mine).reshape(Z_STEPS, inner, share, out_part), near, 1)

    def reduce_far(blocks):
        blocks = blocks.astype(BF)
        far = seq // inner
        summed = pick(blocks, far).astype(F32)
        for step in range(1, Z_STEPS):
            summed = summed + swap(pick(blocks, far ^ step), "seq", step * inner).astype(F32)
        return gather_rows(summed.astype(BF), rank)

    grad_down = reduce_far(grad_down).reshape(ff_share, D).astype(F32)
    grad_up = reduce_far(grad_up).reshape(ranks, share, inner, Z_STEPS, ff_part)
    grad_up = jnp.transpose(grad_up, (1, 3, 2, 0, 4)).reshape(share, FF).astype(F32)
    grad_out = jnp.transpose(reduce_far(grad_out), (1, 0, 2)).reshape(share, D).astype(F32)

    sums = ado[rows:, :D].astype(F32) + ado[rows:, D:].astype(F32)
    placed = lambda kind: lax.dynamic_update_slice_in_dim(
        jnp.zeros((D,), F32), head_sums[0, kind * share : (kind + 1) * share], seq * share, 0
    )
    sums = sums.at[10].set(placed(0)).at[11].set(placed(2))
    for axis, count in (("rows", ranks), ("seq", seqs)):
        bit = 1
        while bit < count:
            sums = sums + swap(sums, axis, bit)
            bit *= 2
    return grad_qkv, sums[10:12].reshape(-1), grad_out, grad_up, grad_down, sums


def body(
    hidden, cotangent, segment_ids, timesteps, qkv_weight, qv_bias, out_weight, out_bias,
    up_weight, up_bias, down_weight, down_bias, norm_gain, norm_bias, time_weight,
):
    assert hidden.shape[0] == 1
    rows = hidden.shape[1]
    seqs, ranks = lax.axis_size("seq"), lax.axis_size("rows")
    length = seqs * rows
    seq, rank = lax.axis_index("seq"), lax.axis_index("rows")
    share = D // seqs
    inner = seqs // Z_STEPS
    fast = seqs == 8 and ranks == 4
    starts = [min(i * share // HD, H - 2) * HD for i in range(seqs)]

    known, gate = gates(ORDER if fast else {})
    features = time_features(timesteps[0]).astype(BF)
    up_row = up_bias.reshape(1, -1)
    weights = [((D, 3 * D), BF), ((D, D), BF), ((D, FF), BF), ((FF, D), BF)]

    def meanwhile():
        known["weights"] = call(
            fetch_kernel,
            "fetch",
            (far(gate("fetch", qkv_weight)), far(out_weight), far(up_weight), far(down_weight)),
            [(*one, NEAR) for one in weights],
            (),
            2,
            4,
        )
        known["fetch"] = known["weights"][1]

    ids = jnp.pad(segment_ids.astype(BF), ((0, 7), (0, D - rows)))
    shards = gather_seq(jnp.concatenate([hidden[0], ids], axis=0), known, gate, meanwhile)
    qkv_near, out_near, up_near, down_near = known["weights"]
    embed = nn(features, time_weight)
    if not fast:
        all_features = gather_rows(features, rank)
        all_features = lax.dynamic_slice_in_dim(all_features, seq * share, share, 2)
    qv_row = qv_bias.reshape(1, -1)
    tile = ((rows, D), BF)
    tile32 = ((rows, D), F32)
    narrow32 = ((rows, 128), F32)
    wide = ((length, D), BF)
    out_row, down_row = out_bias.reshape(1, -1), down_bias.reshape(1, -1)
    x_low, lse, attn, hot, z1, inverse1, result, ydf, dr2, slope, z2_sum = call(
        functools.partial(forward_kernel, seqs),
        "forward",
        (
            *shards, embed, qkv_near, qv_row, out_near, out_row, norm_gain,
            norm_bias, cotangent[0], up_near, up_row, down_near, down_row,
        ),
        [
            (*wide, FAR), narrow32,
            tile32, ((DOCS, length), BF), tile32, narrow32,
            tile, ((rows, 2 * D), BF), tile32, ((rows, FF), F32), ((1, D), F32),
        ],
        [((rows, length), F32), tile32, wide, wide, wide, tile],
        16 if fast else 28,
        1,
    )
    known["forward"] = z1
    if fast:
        ados = [((rows, 3 * D), BF)] * 4
    else:
        ados = [((rows + SUMS, 2 * D), BF)]
    hots = ((DOCS, length), BF)
    docs_shape = ((DOCS, D), F32)
    packed, dr1, docs, hot, *ado = call(
        functools.partial(backward_kernel, starts, len(ados)),
        "backward",
        (
            gate("backward", z1), inverse1, dr2, slope, z2_sum, attn, cotangent[0], hot, lse,
            out_near, up_near, down_near, norm_gain, ydf,
        ),
        [
            ((seqs, rows + 3 * SUMS, PAIR), BF), (*tile32, FAR), (*docs_shape, FAR), (*hots, FAR),
            *((*one, FAR) for one in ados),
        ],
        [tile32, docs_shape, ((SUMS, D), F32), *([tile] * 4 if fast else ados)],
        8,
        3 + 2 * len(ados),
    )
    known["backward"] = packed

    pair = ((length, PAIR), BF)
    head_shape = ((D, 3 * PAIR), BF)
    q_two, k_two, v_two, head_weight = call(
        functools.partial(heads_kernel, share),
        "heads",
        (far(x_low), far(qkv_weight), gate("heads", qv_row)),
        [(*one, FAR) for one in (pair, pair, pair, head_shape)],
        [wide, pair, pair, pair, head_shape, ((3, D, 2 * PAIR), BF)],
        16,
        7 + length // 256,
    )
    known["heads"] = q_two
    if fast:
        near_all = from_chips(*gate("E", ado))
        known["E"] = near_all[1:]
        own_twin = swap(gate("E0", near_all[0]), "rows", 1)
        known["E0"] = own_twin
    arrived = lax.all_to_all(gate("DA", packed), "seq", 0, 0, tiled=True)
    known["DA"] = arrived
    back, sums, *grads = gate(
        "headend",
        head_grad(
            (head_weight, q_two, k_two, v_two, hot, docs, x_low), gate("head", arrived), share,
            4 if fast else 0,
        ),
    )
    known["head"] = back
    if fast:
        up_part, bias_part = call(
            part_weights_kernel,
            "part_weights",
            (far(up_weight), gate("part", up_row)),
            [((D, D), BF, FAR), ((1, D), F32)],
            [((8, D, 384), BF), ((D, D), BF)],
            14,
            9,
        )
        known["part"] = bias_part
        all_features = spread_rows(gate("feat", features))
        known["feat"] = all_features[1:]
        twins = with_twin(gate("Etwin", near_all[1:]))
        near_all = [near_all[0], own_twin, *twins]
        known["Etwin"] = twins[3:]
        up_own, up_sent, down_own, down_sent = feed_grad(
            near_all, up_part, gate("feed", bias_part), down_weight
        )
        known["feed"] = up_own
        up_sent, down_sent = gate("RS1", (up_sent, down_sent))
        up_got, down_got = swap(up_sent, "seq", 2), swap(down_sent, "seq", 4)
        known["RS1"] = (up_got, down_got)
    back = lax.all_to_all(gate("BACK", back), "seq", 0, 0, tiled=True)
    known["BACK"] = back
    blocks, mines = (), ()
    if fast:
        *sent, own = gate("GRS", grads)
        sent = [swap(block, "rows", to + 1) for to, block in enumerate(sent)]
        known["GRS"] = sent
        blocks, mines = (own, *sent), ((own.shape, BF),)
    input_grad, doc_grad, *mine = call(
        functools.partial(input_grad_kernel, share),
        "input_grad",
        (gate("in", back), far(dr1), far(qkv_weight), sums, *(far(one) for one in blocks)),
        [tile32, ((DOCS + SUMS, D), F32), *mines],
        [tile32, ((D, 3 * D), BF), *((one.shape, one.dtype) for one in blocks)],
        12,
        8,
    )
    known["in"] = input_grad
    if fast:
        spread = lax.all_to_all(gate("GA2A", mine[0]), "seq", 0, 0, tiled=True)
        known["GA2A"] = spread
        docs_all = spread_rows(gate("DOCS", doc_grad))
        known["DOCS"] = docs_all[1:]
        up_got, down_got = gate("half", (up_got, down_got))
        halves = [far(one) for one in (up_own, down_own, up_got, down_got)]
        up_sent, down_sent = call(
            combine_half_kernel, "combine_half", halves,
            [((120, D), BF), ((96, D), BF)],
            [(one[1].shape, one[1].dtype) for one in halves],
            8,
            4,
        )
        known["half"] = up_sent
        up_sent, down_sent = gate("RS2", (up_sent, down_sent))
        up_last, down_last = swap(up_sent, "seq", 4), swap(down_sent, "seq", 2)
        known["RS2"] = (up_last, down_last)
        grad_time_weight, norm_sums, bias_sums, grad_up_bias = call(
            time_grad_kernel, "time_grad",
            (*(far(one) for one in all_features), *gate("time", docs_all)),
            [((share, D), F32), ((4, 96), F32), ((2, 96), F32), ((1, 384), F32)],
            [((4 * DOCS, D), BF)],
            8,
            4,
        )
        known["time"] = grad_time_weight
        heads_all = spread_rows(gate("AGG", spread))
        known["AGG"] = heads_all[1:]
        up_last, down_last = gate("all", (up_last, down_last))
        merged = call(
            combine_all_kernel, "combine_all", (*halves, up_last, down_last),
            [((216, D), BF)],
            [(one[1].shape[1:], one[1].dtype) for one in halves],
            8,
            4,
        )[0]
        known["all"] = merged
        feed_all = spread_rows(gate("AGF", merged))
        known["AGF"] = feed_all[1:]
        grad_qkv_weight, grad_qv_bias = call(
            finish_heads_kernel, "finish_heads", gate("finh", heads_all),
            [((share, 3 * D), F32), ((1, 192), F32)],
        )
        known["finh"] = grad_qkv_weight
        grad_up_weight, grad_down_weight, grad_out_weight = call(
            finish_all_kernel, "finish_all", gate("finf", feed_all),
            [((share, FF), F32), ((FF // seqs, D), F32), ((share, D), F32)],
            [((4, 120, D), F32)],
        )
        known["finf"] = grad_out_weight
        grad_qv_bias, grad_up_bias = grad_qv_bias[0], grad_up_bias[0]
        grad_out_bias, grad_down_bias = bias_sums[0], bias_sums[1]
        grad_norm_gain, grad_norm_bias = norm_sums[:2], norm_sums[2:]
    else:
        doc_grad = gather_rows(doc_grad[:DOCS], rank).reshape(ranks * DOCS, D)
        grad_time_weight = lax.dot_general(
            all_features.reshape(ranks * DOCS, share).astype(F32),
            doc_grad,
            (((0,), (0,)), ((), ())),
            precision=precise,
        )
        grad_qkv_weight, qv_sums, grad_out_weight, grad_up_weight, grad_down_weight, totals = (
            general_grads(ydf, ado[0], grads[0], grads[1], up_weight, up_bias, down_weight)
        )

        def part_of(vector, axis=0):
            size = vector.shape[axis] // seqs
            return lax.dynamic_slice_in_dim(vector, seq * size, size, axis)

        grad_qv_bias, grad_out_bias = part_of(qv_sums), part_of(totals[4])
        grad_up_bias = part_of(totals[6 : 6 + FF // D].reshape(-1))
        grad_down_bias = part_of(totals[5])
        grad_norm_gain, grad_norm_bias = part_of(totals[0:2], 1), part_of(totals[2:4], 1)

    return (
        result[None],
        input_grad[None],
        grad_qkv_weight,
        grad_qv_bias,
        grad_out_weight,
        grad_out_bias,
        grad_up_weight,
        grad_up_bias,
        grad_down_weight,
        grad_down_bias,
        grad_norm_gain,
        grad_norm_bias,
        grad_time_weight,
    )


def solution(mesh):
    tokens = P("rows", "seq", None)
    whole = P()
    return jax.shard_map(
        body,
        mesh=mesh,
        in_specs=(tokens, tokens, P("rows", "seq"), P("rows", None)) + (whole,) * 11,
        out_specs=(
            tokens,
            tokens,
            P("seq", None),
            P("seq"),
            P("seq", None),
            P("seq"),
            P("seq", None),
            P("seq"),
            P("seq", None),
            P("seq"),
            P(None, "seq"),
            P(None, "seq"),
            P("seq", None),
        ),
        check_vma=False,
    )
```

```python
import functools
import math

import jax
import jax.numpy as jnp
from jax import lax
from jax.experimental import pallas as pl
from jax.experimental.pallas import tpu as pltpu
from jax.sharding import PartitionSpec as P

D = 768
H = 12
HD = 64
FF = 3072
DOCS = 16
PAIR = 2 * HD
PAIRS = D // PAIR
Z_STEPS = 4
SUMS = 16

EPS = 1e-05
MASKED = -1e30
BF = jnp.bfloat16
F32 = jnp.float32
precise = lax.Precision.HIGHEST
VMEM = pl.BlockSpec(memory_space=pltpu.VMEM)


def swap(block, axis, bit):
    return lax.ppermute(block, axis, [(i, i ^ bit) for i in range(lax.axis_size(axis))])


def dot(a, b, dims):
    return lax.dot_general(a, b, (dims, ((), ())), preferred_element_type=F32)


def nn(a, b):
    return dot(a, b, ((1,), (0,)))


def nt(a, b):
    return dot(a, b, ((1,), (1,)))


def tn(a, b):
    return dot(a, b, ((0,), (0,)))


APART = pl.BlockSpec(memory_space=pltpu.HBM)
FAR = "far"
NEAR = "near"


def far(value):
    return FAR, value


def call(kernel, name, ins, outs, scratch=(), vmem=8, copies=0):
    specs = [APART if isinstance(one, tuple) else VMEM for one in ins]
    values = [
        pltpu.with_memory_space_constraint(one[1], pltpu.HBM) if isinstance(one, tuple) else one
        for one in ins
    ]
    held = [pltpu.VMEM(*one) for one in scratch]
    if copies:
        held.append(pltpu.SemaphoreType.DMA((copies,)))
    return pl.pallas_call(
        kernel,
        out_shape=tuple(
            (pltpu.HBM if FAR in one else pltpu.VMEM)(*one[:2])
            if one[2:]
            else jax.ShapeDtypeStruct(*one)
            for one in outs
        ),
        in_specs=specs,
        out_specs=tuple(APART if FAR in one else VMEM for one in outs),
        scratch_shapes=held,
        compiler_params=pltpu.CompilerParams(vmem_limit_bytes=vmem << 20),
        cost_estimate=pl.CostEstimate(flops=int(COSTS[name] * 1e9), transcendentals=0, bytes_accessed=0),
        name=name,
    )(*values)


def copy(source, target, sems, at):
    moved = pltpu.make_async_copy(source, target, sems.at[at])
    moved.start()
    return moved


def copies(pairs, sems, first):
    return [copy(one, to, sems, first + at) for at, (one, to) in enumerate(pairs)]


def wait(moved):
    for one in moved:
        one.wait()


def loop(count, step):
    def body(at, carry):
        step(at)
        return carry

    lax.fori_loop(0, count, body, 0)


def at_rows(index, size):
    return pl.ds(pl.multiple_of(index * size, 8), size)


def at_lanes(index, size):
    return pl.ds(pl.multiple_of(index * size, 128), size)


def time_features(timesteps):
    half_width = D // 2
    frequency = jnp.exp(
        jnp.arange(half_width, dtype=F32) * (-math.log(10000.0) / half_width)
    )
    phases = timesteps.astype(F32)[..., None] * frequency
    return jnp.concatenate([jnp.sin(phases), jnp.cos(phases)], axis=-1)


def gather_seq(block, known, gate, meanwhile):
    size = lax.axis_size("seq")
    inner = size // Z_STEPS
    found = [None] * size
    found[0] = block
    for far in range(1, Z_STEPS):
        name = "Z%d" % far
        found[far * inner] = swap(gate(name, block), "seq", far * inner)
        known[name] = found[far * inner]
    for far in range(Z_STEPS):
        if far == 2:
            meanwhile()
        name = "Y%d" % far
        held = gate(name, found[far * inner])
        for near in range(1, inner):
            found[far * inner + near] = swap(held, "seq", near)
        known[name] = found[far * inner + inner - 1]
    return found


ORDER = {
    "Etwin": ("part", ),
    "RS1": ("feed", "part", ),
    "all": ("AGG", "time", ),
    "backward": ("Y3", "forward", ),
    "fetch": ("Y0", ),
    "finf": ("finh", ),
    "forward": ("Y3", ),
    "half": ("DOCS", "in", ),
    "head": ("heads", ),
    "part": ("E0", "head", ),
}
COSTS = {
    "fetch": 7, "forward": 12, "backward": 5, "heads": 3, "part_weights": 3, "feed_grad": 8,
    "head_grad": 12, "input_grad": 5, "combine_half": 1,
    "combine_all": 1, "finish_all": 2, "finish_heads": 1, "time_grad": 1,
}


def split2(value):
    high = value.astype(BF)
    return high, (value - high.astype(F32)).astype(BF)


def split3(value):
    high = value.astype(BF)
    rest = value - high.astype(F32)
    middle = rest.astype(BF)
    low = (rest - middle.astype(F32)).astype(BF)
    return high, middle, low


def head_start(seq, share):
    return jnp.minimum(seq * share // HD, H - 2) * HD


def head_window(share):
    start = head_start(lax.axis_index("seq"), share)
    base = jnp.minimum(start // PAIR, PAIRS - 2) * PAIR
    return base, (2 * PAIR - (start - base)) % (2 * PAIR)


def normalize(value):
    centered = value - jnp.mean(value, axis=-1, keepdims=True)
    inverse = lax.rsqrt(jnp.mean(centered * centered, axis=-1, keepdims=True) + EPS)
    return centered * inverse, inverse


def normalize_back(z, inverse, grad):
    return inverse * (
        grad
        - jnp.mean(grad, axis=-1, keepdims=True)
        - z * jnp.mean(grad * z, axis=-1, keepdims=True)
    )


def total(value):
    return jnp.sum(value, axis=0, keepdims=True)


def gelu_parts(u):
    phi = 0.5 * (1.0 + lax.erf(u * math.sqrt(0.5)))
    return phi, phi + u * (jnp.exp(-0.5 * u * u) * (1.0 / math.sqrt(2.0 * math.pi)))


def fetch_kernel(*refs):
    count = (len(refs) - 1) // 2
    wait(copies(zip(refs[:count], refs[count:-1]), refs[-1], 0))


def forward_kernel(count, *refs):
    shards = refs[:count]
    embed_ref, qkv_ref, bias_ref, wo_ref, bo_ref, gain_ref, off_ref = refs[count : count + 7]
    cot_ref, up_ref, bu_ref, down_ref, bd_ref = refs[count + 7 : count + 12]
    refs = refs[count + 12 :]
    xlow_out, lse_ref, attn_ref, hot_ref, z1_ref, inverse_ref = refs[:6]
    result_ref, ydf_ref, dr2_ref, slope_ref, z2_sum_ref = refs[6:11]
    mask_ref, x_ref, xlow_ref, k_ref, v_ref, q_ref, sems = refs[11:]
    seq = lax.axis_index("seq")
    rows = attn_ref.shape[0]
    width = D
    parts = [slice(at * width, (at + 1) * width) for at in range(FF // width)]
    embed = jnp.concatenate(split3(embed_ref[...]), axis=0)
    places = lax.broadcasted_iota(jnp.int32, (DOCS, rows), 0).astype(F32)
    hot_own = None
    for at in range(count):
        ids = shards[at][rows : rows + 8, :rows].astype(F32)[:1]
        hot = (places == ids).astype(BF)
        hot_ref[:, at_lanes(seq ^ at, rows)] = hot
        x = shards[at][:rows, :].astype(F32) + tn(jnp.concatenate([hot] * 3, axis=0), embed)
        if at == 0:
            hot_own = hot
            x_ref[...] = x
            own = x.astype(BF)
        xlow_ref[at_rows(seq ^ at, rows), :] = x.astype(BF)
    moved = copy(xlow_ref, xlow_out, sems, 0)
    q_ref[...] = (
        (nn(own, qkv_ref[:, :D]) + bias_ref[:, :D]).astype(BF).astype(F32) * (HD**-0.5)
    ).astype(BF)
    step = 2 * rows
    for at in range(count * rows // step):
        piece = slice(at * step, (at + 1) * step)
        every = xlow_ref[piece, :]
        k_ref[piece, :] = nn(every, qkv_ref[:, D : 2 * D]).astype(BF)
        v_ref[piece, :] = (nn(every, qkv_ref[:, 2 * D :]) + bias_ref[:, D:]).astype(BF)
    mask_ref[...] = (tn(hot_own, hot_ref[...]) - 1.0) * -MASKED
    first = lax.broadcasted_iota(jnp.int32, (rows, PAIR), 1) < HD
    lane = lax.broadcasted_iota(jnp.int32, (rows, 128), 1)
    lse = jnp.zeros((rows, 128), F32)
    for pair in range(PAIRS):
        cols = slice(pair * PAIR, (pair + 1) * PAIR)
        q = q_ref[:, cols]
        halves = []
        for half in range(2):
            q_one = jnp.where(first if half == 0 else ~first, q, jnp.zeros_like(q))
            scores = nt(q_one, k_ref[:, cols]) + mask_ref[...]
            top = jnp.max(scores, axis=-1, keepdims=True)
            weights = jnp.exp(scores - top)
            summed = jnp.sum(weights, axis=-1, keepdims=True)
            halves.append(nn(weights.astype(BF), v_ref[:, cols]) / summed)
            lse = jnp.where(lane == 2 * pair + half, top + jnp.log(summed), lse)
        attn_ref[:, cols] = jnp.where(first, halves[0], halves[1])
    lse_ref[...] = lse
    z1, inverse = normalize(x_ref[...] + nn(attn_ref[...].astype(BF), wo_ref[...]) + bo_ref[...])
    z1_ref[...] = z1
    inverse_ref[...] = jnp.broadcast_to(inverse, (rows, 128))
    y1 = z1 * gain_ref[0:1, :] + off_ref[0:1, :]
    y1_low = y1.astype(BF)
    ydf_ref[:, :D] = y1_low
    r2 = y1 + bd_ref[...]
    for cols in parts:
        u = nn(y1_low, up_ref[:, cols]) + bu_ref[:, cols]
        phi, slope = gelu_parts(u)
        slope_ref[:, cols] = slope
        r2 = r2 + nn((u * phi).astype(BF), down_ref[cols, :])
    z2, inverse2 = normalize(r2)
    result_ref[...] = (z2 * gain_ref[1:2, :] + off_ref[1:2, :]).astype(BF)
    cot = cot_ref[...].astype(F32)
    dr2 = normalize_back(z2, inverse2, cot * gain_ref[1:2, :])
    ydf_ref[:, D:] = dr2.astype(BF)
    dr2_ref[...] = dr2
    z2_sum_ref[...] = total(cot * z2)
    moved.wait()


def backward_kernel(
    starts, chips,
    z1_ref, inverse_ref, dr2_ref, slope_ref, z2_sum_ref, attn_ref, cot_ref, hot_ref, lse_ref,
    wo_ref, up_ref, down_ref, gain_ref, ydf_ref,
    packed_ref, dr1_out, docs_out, hot_out, *refs,
):
    ado_outs, ados = refs[:chips], refs[-chips - 1 : -1]
    dr1_ref, docs_ref, sums_ref = refs[chips : chips + 3]
    sems = refs[-1]
    rows = z1_ref.shape[0]
    moved = [copy(hot_ref, hot_out, sems, 0)]
    if chips > 1:
        moved += copies([(ydf_ref, one.at[:, : 2 * D]) for one in ado_outs], sems, 3 + chips)
        ado_outs = [one.at[:, 2 * D :] for one in ado_outs]
    z1 = z1_ref[...]
    dr2 = dr2_ref[...]
    df_low = dr2.astype(BF)
    dy1 = dr2
    width = D
    for at in range(FF // width):
        cols = slice(at * width, (at + 1) * width)
        du_low = (nt(df_low, down_ref[cols, :]) * slope_ref[:, cols]).astype(BF)
        sums_ref[6 + at : 7 + at, :] = total(du_low.astype(F32))
        dy1 = dy1 + nt(du_low, up_ref[:, cols])
    dr1 = normalize_back(z1, inverse_ref[:, 0:1], dy1 * gain_ref[0:1, :])
    dr1_ref[...] = dr1
    moved.append(copy(dr1_ref, dr1_out, sems, 1))
    do_low = dr1.astype(BF)
    da = nt(do_low, wo_ref[...]).astype(BF)
    attn = attn_ref[...]
    to_heads = (
        lax.broadcasted_iota(jnp.int32, (D, 128), 0) // HD
        == lax.broadcasted_iota(jnp.int32, (D, 128), 1)
    ).astype(BF)
    high, middle, low = split3(da.astype(F32) * attn)
    delta = nn(high, to_heads) + nn(middle, to_heads) + nn(low, to_heads)
    lse_first, delta_first = lse_ref[...].T, delta.T
    cot = cot_ref[...].astype(F32)
    sums_ref[0:1, :] = total(dy1 * z1)
    sums_ref[1:2, :] = z2_sum_ref[...]
    sums_ref[2:3, :] = total(dy1)
    sums_ref[3:4, :] = total(cot)
    sums_ref[4:5, :] = total(do_low.astype(F32))
    sums_ref[5:6, :] = total(df_low.astype(F32))
    sums_ref[6 + FF // width :, :] = jnp.zeros((SUMS - 6 - FF // width, D), F32)
    share = D // len(starts)
    for at, start in enumerate(starts):
        packed_ref[at, :rows, :] = da[:, start : start + PAIR]
        head = start // HD
        lines = [lse_first[head : head + 2], delta_first[head : head + 2]]
        if chips > 1:
            mine = sums_ref[:6, at * share : (at + 1) * share]
            lines.append(jnp.concatenate([mine, jnp.zeros((6, 128 - share), F32)], axis=1))
            for part in range(3):
                first = at * 4 * share + part * 128
                lines.append(sums_ref[6 + first // D : 7 + first // D, first % D : first % D + 128])
        used = sum(one.shape[0] for one in lines)
        lines.append(jnp.zeros((SUMS - used, 128), F32))
        lines = jnp.concatenate(lines, axis=0)
        parts = jnp.concatenate([one.astype(F32) for one in split3(lines)], axis=0).astype(BF)
        packed_ref[at, rows:, :] = parts
    hot = hot_ref[:, at_lanes(lax.axis_index("seq"), rows)]
    high, middle, low = split3(dr1)
    docs_ref[...] = nn(hot, high) + nn(hot, middle) + nn(hot, low)
    moved.append(copy(docs_ref, docs_out, sems, 2))
    attn = attn.astype(BF)
    if chips == 1:
        high, low = split2(sums_ref[...])
        ados[0][:rows, :D] = attn
        ados[0][:rows, D:] = do_low
        ados[0][rows:, :D] = high
        ados[0][rows:, D:] = low
    else:
        near, across = lax.axis_index("seq") % 2, lax.axis_index("rows") // 2
        shares = [
            jnp.concatenate(
                [attn[:, (2 * z + y) * 96 : (2 * z + y + 1) * 96] for z in range(4)], axis=1
            )
            for y in range(2)
        ]
        sides = do_low[:, : D // 2], do_low[:, D // 2 :]
        for to, ref in enumerate(ados):
            swapped, over = to // 2, to % 2
            ref[:, : D // 2] = jnp.where(near == swapped, shares[0], shares[1])
            ref[:, D // 2 :] = jnp.where(across == over, sides[0], sides[1])
    moved += copies(zip(ados, ado_outs), sems, 3)
    wait(moved)


def heads_kernel(share, x_in, qkv_in, bias_ref, *refs):
    q_out, k_out, v_out, w_out, x_ref, q_ref, k_ref, v_ref, w_ref, wide_ref, sems = refs
    length = x_ref.shape[0]
    base, back = head_window(share)
    windows = copies(
        [
            (qkv_in.at[:, pl.ds(pl.multiple_of(base + kind * D, PAIR), 2 * PAIR)], wide_ref.at[kind])
            for kind in range(3)
        ],
        sems,
        0,
    )
    step = 256
    pieces = [slice(at * step, (at + 1) * step) for at in range(length // step)]
    loads = copies([(x_in.at[one, :], x_ref.at[one, :]) for one in pieces], sems, 3)
    biases = []
    for kind in range(3):
        windows[kind].wait()
        turned = pltpu.roll(wide_ref[kind].astype(F32), back, 1)[:, :PAIR]
        w_ref[:, kind * PAIR : (kind + 1) * PAIR] = turned.astype(BF)
        if kind == 1:
            biases.append(jnp.zeros((1, PAIR), F32))
        else:
            cols = pl.ds(pl.multiple_of(base + (kind // 2) * D, PAIR), 2 * PAIR)
            bias = jnp.broadcast_to(bias_ref[:, cols], (8, 2 * PAIR))
            biases.append(pltpu.roll(bias, back, 1)[:1, :PAIR])
    first = 3 + len(pieces)
    moved = [copy(w_ref, w_out, sems, first)]
    for at, piece in enumerate(pieces):
        loads[at].wait()
        three = nn(x_ref[piece, :], w_ref[...])
        q_ref[piece, :] = (
            (three[:, :PAIR] + biases[0]).astype(BF).astype(F32) * (HD**-0.5)
        ).astype(BF)
        k_ref[piece, :] = three[:, PAIR : 2 * PAIR].astype(BF)
        v_ref[piece, :] = (three[:, 2 * PAIR :] + biases[2]).astype(BF)
    moved += copies(((q_ref, q_out), (k_ref, k_out), (v_ref, v_out)), sems, first + 1)
    wait(moved)


def head_grad_kernel(step, share, split, *refs):
    w_in, q_in, k_in, v_in, hot_in, docs_in, x_in, da_ref, back_ref, sums_ref = refs[:10]
    w_ref, q_ref, k_ref, v_ref, hot_ref, docs_ref, x_ref = refs[-13:-6]
    dq_ref, dk_ref, dv_ref, heads_ref, grad_ref, sems = refs[-6:]
    outs = refs[10:-13]
    if split:
        *outs, own_ref = outs
    length = q_ref.shape[0]
    rows = length // (D // share)
    seq = lax.axis_index("seq")
    loads = copies(
        (
            (hot_in, hot_ref), (v_in, v_ref), (k_in, k_ref), (q_in, q_ref),
            (w_in, w_ref), (docs_in, docs_ref), (x_in, x_ref),
        ),
        sems,
        0,
    )
    wait(loads[:4])
    first = lax.broadcasted_iota(jnp.int32, (step, PAIR), 1) < HD
    each = step // rows
    sums = jnp.zeros((SUMS, rows), F32)
    for at in range(D // share):
        lines = da_ref[at, rows:, :].astype(F32)
        sums = sums + (lines[:SUMS] + lines[SUMS : 2 * SUMS] + lines[2 * SUMS :])
    sums_ref[...] = sums
    dk_ref[...] = jnp.zeros((length, PAIR), F32)
    dv_ref[...] = jnp.zeros((length, PAIR), F32)

    @functools.partial(loop, length // step)
    def _(at):
        piece = at_rows(at, step)
        blocks = [at * each + one for one in range(each)]
        da_all = jnp.concatenate([da_ref[one, :rows, :] for one in blocks], axis=0)
        stats = jnp.concatenate(
            [da_ref[one, rows:, :].astype(F32) for one in blocks], axis=1
        )
        stats = stats[:SUMS] + stats[SUMS : 2 * SUMS] + stats[2 * SUMS :]
        mask = (tn(hot_ref[...], hot_ref[:, at_lanes(at, step)]) - 1.0) * -MASKED
        halves = []
        for half in range(2):
            here = first if half == 0 else ~first
            q = jnp.where(here, q_ref[piece, :], jnp.zeros((step, PAIR), BF))
            da = jnp.where(here, da_all, jnp.zeros((step, PAIR), BF))
            probs = jnp.exp(nt(k_ref[...], q) + (mask - stats[half : half + 1]))
            ds = (probs * (nt(v_ref[...], da) - stats[2 + half : 3 + half])).astype(BF)
            halves.append(tn(ds, k_ref[...]))
            dk_ref[...] += nn(ds, q)
            dv_ref[...] += nn(probs.astype(BF), da)
        dq_ref[piece, :] = jnp.where(first, halves[0], halves[1]) * (HD**-0.5)

    wait(loads[4:])
    offset = seq * share - head_start(seq, share)
    left = (PAIR - offset) % PAIR
    for at in range(length // step):
        piece = slice(at * step, (at + 1) * step)
        heads_ref[piece, :] = jnp.concatenate(
            [pltpu.roll(ref[piece, :], left, 1)[:, :share] for ref in (dq_ref, dk_ref, dv_ref)],
            axis=1,
        ).astype(BF)
    doc_sums = nn(hot_ref[...], heads_ref[...])
    docs = docs_ref[...]
    for kind in range(3):
        piece = doc_sums[:, kind * share : (kind + 1) * share]
        piece = jnp.concatenate([piece, jnp.zeros((DOCS, PAIR - share), F32)], axis=1)
        parts = jnp.concatenate(split3(pltpu.roll(piece, offset, 1)), axis=0)
        product = nt(parts, w_ref[:, kind * PAIR : (kind + 1) * PAIR])
        docs = docs + (product[:DOCS] + product[DOCS : 2 * DOCS] + product[2 * DOCS :])
    docs = docs.astype(BF)
    extra = back_ref.shape[1] - 6 * DOCS
    full = 3 * share // PAIR
    rest = 3 * share % PAIR
    group = rows * rest // PAIR
    for at in range(D // share):
        for part in range(full):
            back_ref[at, part * rows : (part + 1) * rows, :] = heads_ref[
                at * rows : (at + 1) * rows, part * PAIR : (part + 1) * PAIR
            ]
        back_ref[at, full * rows : extra, :] = jnp.concatenate(
            [
                heads_ref[first : first + group, full * PAIR :]
                for first in range(at * rows, (at + 1) * rows, group)
            ],
            axis=1,
        )
        for col in range(PAIRS):
            back_ref[at, extra + col * DOCS : extra + (col + 1) * DOCS, :] = docs[
                :, col * PAIR : (col + 1) * PAIR
            ]
    if not split:
        outs[0][...] = tn(x_ref[...], heads_ref[...])
        outs[1][...] = total(doc_sums)
        return
    *sent, mine_out = outs
    grad_ref[...] = tn(x_ref[...], heads_ref[...])
    rank = lax.axis_index("rows")
    part = share // split
    high, low = split2(jnp.broadcast_to(total(doc_sums), (8, 3 * share)))
    row = lax.broadcasted_iota(jnp.int32, (8, 3 * share), 0)
    tail = jnp.where(row == 0, high.astype(F32), jnp.where(row == 1, low.astype(F32), 0.0))
    for to, ref in enumerate([own_ref] + list(sent)):
        for at in range(D // share):
            here = pl.ds(pl.multiple_of(at * share + (rank ^ to) * part, 8), part)
            ref[at, :part, :] = grad_ref[here, :].astype(ref.dtype)
            ref[at, part:, :] = tail.astype(ref.dtype)
        if to == 0:
            moved = copy(own_ref, mine_out, sems, 7)
    moved.wait()


def head_grad(apart, da, share, split):
    length = apart[1].shape[0]
    count = D // share
    rows = length // count
    outs = [((count, rows * 3 * share // PAIR + 6 * DOCS, PAIR), BF), ((SUMS, rows), F32)]
    if split:
        block = (count, share // split + 8, 3 * share)
        outs += [(block, BF)] * (split - 1) + [(block, F32, FAR)]
    else:
        outs += [((D, 3 * share), F32), ((1, 3 * share), F32)]
    scratch = [(block, F32)] if split else []
    scratch += [(one.shape, one.dtype) for one in apart] + [((length, PAIR), F32)] * 3
    scratch += [((length, 3 * share), BF), ((D, 3 * share), F32)]
    return call(
        functools.partial(head_grad_kernel, 512, share, split),
        "head_grad",
        (*(far(one) for one in apart), da),
        outs,
        scratch,
        24 if length <= 1024 else 44,
        8,
    )


def combine(blocks, out_ref):
    value = blocks[0][...]
    for ref in blocks[1:]:
        value = value + ref[...].astype(F32)
    count, rows, wide = value.shape
    out_ref[:, : rows - 8, :] = value[:, : rows - 8].astype(out_ref.dtype)
    row = lax.broadcasted_iota(jnp.int32, (8, wide), 0)
    for at in range(count):
        last = value[at, rows - 8 :]
        high, low = split2(jnp.broadcast_to(last[0:1] + last[1:2], (8, wide)))
        out_ref[at, rows - 8 :, :] = jnp.where(
            row == 0, high.astype(F32), jnp.where(row == 1, low.astype(F32), 0.0)
        ).astype(out_ref.dtype)


def input_grad_kernel(share, back_ref, dr1_in, qkv_in, sums_ref, *refs):
    blocks = ()
    if len(refs) > 5:
        blocks, held, refs = refs[:4], refs[-5:-1], refs[4:-5] + refs[-1:]
    grad_ref, docs_ref, *mine_ref, dr1_ref, qkv_ref, sems = refs
    blocks = copies(zip(blocks, held), sems, 4) if blocks else ()
    loads = copies(
        [(qkv_in.at[:, c], qkv_ref.at[:, c]) for c in [slice(i * D, i * D + D) for i in range(3)]],
        sems,
        0,
    )
    loads.append(copy(dr1_in, dr1_ref, sems, 3))
    rows = dr1_ref.shape[0]
    count = D // share
    extra = back_ref.shape[1] - 6 * DOCS
    full = 3 * share // PAIR
    rest = 3 * share % PAIR
    kinds = [[], [], []]
    for at in range(count):
        here = [back_ref[at, part * rows : (part + 1) * rows, :] for part in range(full)]
        last = back_ref[at, full * rows : extra, :]
        here.append(
            jnp.concatenate([last[:, c : c + rest] for c in range(0, PAIR, rest)], axis=0)
        )
        here = jnp.concatenate(here, axis=1)
        for kind in range(3):
            kinds[kind].append(here[:, kind * share : (kind + 1) * share])
    docs = jnp.zeros((6 * DOCS, PAIR), F32)
    for at in range(count):
        docs = docs + back_ref[at, extra:, :].astype(F32)
    docs_ref[:DOCS, :] = jnp.concatenate(
        [docs[at * DOCS : (at + 1) * DOCS] for at in range(PAIRS)], axis=1
    )
    docs_ref[DOCS:, :128] = sums_ref[...]
    docs_ref[DOCS:, 128:] = jnp.zeros((SUMS, D - 128), F32)
    loads[3].wait()
    result = dr1_ref[...]
    for kind in range(3):
        cols = slice(kind * D, (kind + 1) * D)
        loads[kind].wait()
        result = result + nt(jnp.concatenate(kinds[kind], axis=1), qkv_ref[:, cols])
    grad_ref[...] = result
    if blocks:
        wait(blocks)
        combine(held, mine_ref[0])


def unit_share(at):
    return 2 * (at % 4) + at // 4


def part_weights_kernel(up_in, bu_ref, up_out, bu_out, held_ref, up_ref, sems):
    back = (384 - lax.axis_index("rows") * 96) % 384
    loads = copies(
        [
            (up_in.at[:, unit_share(at) * 384 : (unit_share(at) + 1) * 384], held_ref.at[at])
            for at in range(8)
        ],
        sems,
        0,
    )
    ups, biases = [], []
    for at in range(8):
        cols = slice(unit_share(at) * 384, (unit_share(at) + 1) * 384)
        loads[at].wait()
        ups.append(pltpu.roll(held_ref[at].astype(F32), back, 1)[:, :96].astype(BF))
        bias = jnp.broadcast_to(bu_ref[:, cols], (8, 384))
        biases.append(pltpu.roll(bias, back, 1)[:1, :96])
    up_ref[...] = jnp.concatenate(ups, axis=1)
    moved = copy(up_ref, up_out, sems, 8)
    bu_out[...] = jnp.concatenate(biases, axis=1)
    moved.wait()


def feed_grad_kernel(*refs):
    pieces = refs[:8]
    up_in, bu_ref, down_in, up_own_out, up_sent_ref, down_own_out, down_sent_ref = refs[8:15]
    all_ref, up_ref, down_ref, g_ref, du_ref = refs[15:20]
    up_grad_ref, down_grad_ref, out_grad_ref, up_own_ref, down_own_ref, sems = refs[20:]
    seq, rank = lax.axis_index("seq"), lax.axis_index("rows")
    near, z = seq % 2, seq // 2
    rows = pieces[0].shape[0]
    loads = [copy(up_in, up_ref, sems, 8)]
    loads += copies([(pieces[at], all_ref.at[at]) for at in range(2)], sems, 0)
    first = rank * 96
    downs = copies(
        [
            (
                down_in.at[pl.ds(pl.multiple_of(unit_share(at) * 384 + first, 32), 96), :],
                down_ref.at[at * 96 : (at + 1) * 96, :],
            )
            for at in range(8)
        ],
        sems,
        9,
    )
    loads += copies([(pieces[at], all_ref.at[at]) for at in range(2, 8)], sems, 2)
    loads[0].wait()
    step = 2 * rows
    for at in range(4):
        wait(loads[1 + 2 * at : 3 + 2 * at])
        piece = slice(at * step, (at + 1) * step)
        two = slice(2 * at, 2 * at + 2)
        u = nn(all_ref[two, :, :D].reshape(step, D), up_ref[...]) + bu_ref[...]
        phi, slope = gelu_parts(u)
        if at == 0:
            wait(downs)
        g_ref[piece, :] = (u * phi).astype(BF)
        df = all_ref[two, :, D : 2 * D].reshape(step, D)
        du_ref[piece, :] = (nt(df, down_ref[...]) * slope).astype(BF)

    tokens = 8 * rows
    df = all_ref[:, :, D : 2 * D].reshape(tokens, D)
    down_grad_ref[...] = tn(g_ref[:, at_lanes(near, 384)], df)
    up_grad_ref[...] = tn(all_ref[:, :, :D].reshape(tokens, D), du_ref[...])
    base = pl.multiple_of(2 * D + D // 2 + (rank % 2) * 128, 128)
    attn = all_ref[:, :, 2 * D : 2 * D + D // 2].reshape(tokens, D // 2)
    do = all_ref[:, :, pl.ds(base, 256)].reshape(tokens, 256)
    back = (256 - (rank % 2) * 64) % 256
    out_grad_ref[...] = pltpu.roll(tn(attn, do), back, 1)
    for to in range(4):
        up_rows = pl.ds(pl.multiple_of((2 * (z ^ to) + near) * 96, 8), 96)
        down_rows = pl.ds(pl.multiple_of((z ^ to) * 96, 8), 96)
        ref = up_own_ref.at[to // 2] if to % 2 == 0 else up_sent_ref.at[to // 2]
        ref[:96, :] = up_grad_ref[up_rows, :].astype(ref.dtype)
        out = out_grad_ref[down_rows, :192]
        ref[96:, :] = jnp.concatenate(
            [out[part * 24 : (part + 1) * 24] for part in range(4)], axis=1
        ).astype(ref.dtype)
        ref = down_own_ref.at[to % 2] if to < 2 else down_sent_ref.at[to % 2]
        ref[...] = down_grad_ref[down_rows, :].astype(ref.dtype)
    wait(copies(((up_own_ref, up_own_out), (down_own_ref, down_own_out)), sems, 17))


def feed_grad(pieces, up, bias, down):
    tokens = 8 * pieces[0].shape[0]
    blocks = (2, 120, D), (2, 96, D)
    wide = ((tokens, D), BF)
    return call(
        feed_grad_kernel,
        "feed_grad",
        (*(far(one) for one in pieces), far(up), bias, far(down)),
        [one for block in blocks for one in ((block, F32, FAR), (block, BF))],
        [
            ((8, tokens // 8, 3 * D), BF), ((D, D), BF), ((D, D), BF), wide, wide,
            ((D, D), F32), ((384, D), F32), ((384, 256), F32),
            *((block, F32) for block in blocks),
        ],
        28,
        19,
    )


def combine_half_kernel(up_in, down_in, up_got_in, down_got_in, up_ref, down_ref, *refs):
    *held, sems = refs
    loads = copies(zip((up_in, down_in, up_got_in, down_got_in), held), sems, 0)
    wait(loads)
    up_ref[...] = (held[0][1] + held[2][1].astype(F32)).astype(BF)
    down_ref[...] = (held[1][1] + held[3][1].astype(F32)).astype(BF)


def combine_all_kernel(up_in, down_in, up_got_in, down_got_in, up_last_ref, down_last_ref, out_ref, *refs):
    *held, sems = refs
    sources = [one.at[0] for one in (up_in, down_in, up_got_in, down_got_in)]
    wait(copies(zip(sources, held), sems, 0))
    up = held[0][...] + held[2][...].astype(F32) + up_last_ref[...].astype(F32)
    down = held[1][...] + held[3][...].astype(F32) + down_last_ref[...].astype(F32)
    out_ref[:120, :] = up.astype(BF)
    out_ref[120:, :] = down.astype(BF)


def finish_all_kernel(a_ref, b_ref, c_ref, d_ref, up_ref, down_ref, out_ref, held_ref):
    rank = lax.axis_index("rows")
    for at, ref in enumerate((a_ref, b_ref, c_ref, d_ref)):
        held_ref[rank ^ at] = ref[:120, :].astype(F32)
        down_ref[pl.ds(pl.multiple_of((rank ^ at) * 96, 8), 96), :] = ref[120:, :].astype(F32)
    for share in range(8):
        at = (share // 2) + 4 * (share % 2)
        up_ref[:, share * 384 : (share + 1) * 384] = jnp.concatenate(
            [held_ref[r, :96, at * 96 : (at + 1) * 96] for r in range(4)], axis=1
        )
    for at in range(4):
        out_ref[at * 24 : (at + 1) * 24, :] = jnp.concatenate(
            [held_ref[r, 96:, at * 192 : (at + 1) * 192] for r in range(4)], axis=1
        )


def time_grad_kernel(*refs):
    features, docs, (out_ref, norm_ref, bias_ref, up_ref, left_ref, sems) = refs[:4], refs[4:8], refs[8:]
    seq = lax.axis_index("seq")
    wait(
        copies([(ref, left_ref.at[at * DOCS : (at + 1) * DOCS]) for at, ref in enumerate(features)], sems, 0)
    )
    left = left_ref[...].astype(F32)
    left = pltpu.roll(left, (D - seq * 96) % D, 1)[:, :96].astype(BF)
    high, middle, low = split3(jnp.concatenate([ref[:DOCS, :] for ref in docs], axis=0))
    out_ref[...] = tn(left, high) + tn(left, middle) + tn(left, low)
    sums = jnp.zeros((SUMS, 128), F32)
    for ref in docs:
        sums = sums + ref[DOCS:, :128]
    norm_ref[...] = sums[4:8, :96]
    bias_ref[...] = sums[8:10, :96]
    up_ref[...] = jnp.concatenate([sums[at : at + 1] for at in range(10, 13)], axis=1)


def finish_heads_kernel(a_ref, b_ref, c_ref, d_ref, out_ref, bias_ref):
    rank = lax.axis_index("rows")
    order = [(kind, at) for kind in range(3) for at in range(8)]
    for to, ref in enumerate((a_ref, b_ref, c_ref, d_ref)):
        value = jnp.concatenate(
            [ref[at, :24, kind * 96 : (kind + 1) * 96].astype(F32) for kind, at in order], axis=1
        )
        out_ref[pl.ds(pl.multiple_of((rank ^ to) * 24, 8), 24), :] = value
    tail = jnp.concatenate(
        [a_ref[at, 24:, kind * 96 : (kind + 1) * 96].astype(F32) for kind, at in order], axis=1
    )
    sums = tail[0:1] + tail[1:2]
    sums = jnp.concatenate([sums[:, :D], sums[:, 2 * D :]], axis=1)
    back = (2 * D - lax.axis_index("seq") * 192) % (2 * D)
    bias_ref[...] = pltpu.roll(jnp.broadcast_to(sums, (8, 2 * D)), back, 1)[:1, :192]


def after(value, *others):
    return lax.optimization_barrier((value,) + others)[0]


def after_all(values, *others):
    return list(lax.optimization_barrier((tuple(values), others))[0])


def gates(order):
    known = {}

    def gate(name, value):
        held = [known[one] for one in order.get(name, ()) if one in known]
        return lax.optimization_barrier((value, held))[0] if held else value

    return known, gate


def from_chips(own, over, near, both):
    pairs = [((s * 4 + r), ((s ^ 1) * 4 + (r ^ 2))) for s in range(8) for r in range(4)]
    across = lax.ppermute(both, ("seq", "rows"), pairs)
    return [own, swap(over, "rows", 2), swap(near, "seq", 1), across]


def with_twin(blocks):
    return blocks + [swap(one, "rows", 1) for one in blocks]


def spread_rows(block):
    across = swap(block, "rows", 2)
    return block, swap(block, "rows", 1), across, swap(across, "rows", 1)


def pick(blocks, index, axis=0):
    return lax.dynamic_index_in_dim(blocks, index, axis, keepdims=False)


def reduce_rows(blocks, place):
    bit = 1
    while blocks.shape[0] > 1:
        pairs = blocks.reshape((blocks.shape[0] // 2, 2) + blocks.shape[1:])
        mine = (place // bit) % 2
        sent = swap(pick(pairs, 1 - mine, 1).astype(BF), "rows", bit)
        blocks = pick(pairs, mine, 1).astype(F32) + sent.astype(F32)
        bit *= 2
    return blocks[0]


def gather_rows(block, place):
    count = lax.axis_size("rows")
    found = block[None]
    bit = count // 2
    while bit >= 1:
        other = swap(found, "rows", bit)
        mine = (place // bit) % 2
        low, high = jnp.where(mine == 0, found, other), jnp.where(mine == 0, other, found)
        if bit == count // 2:
            found = jnp.concatenate([low, high], axis=0)
        else:
            found = jnp.stack([low, high], axis=1).reshape((-1,) + block.shape)
        bit //= 2
    return found


def general_grads(ydf, ado, grad_heads, head_sums, up_weight, up_bias, down_weight):
    seqs, ranks = lax.axis_size("seq"), lax.axis_size("rows")
    seq, rank = lax.axis_index("seq"), lax.axis_index("rows")
    inner = seqs // Z_STEPS
    near = seq % inner
    share = D // seqs
    ff_share = FF // seqs
    ff_part = ff_share // ranks
    rows = ydf.shape[0]

    part = share // ranks
    grad_heads = grad_heads.reshape(seqs, ranks, part, 3 * share)
    mine = reduce_rows(jnp.moveaxis(grad_heads, 1, 0), rank)
    spread = lax.all_to_all(mine.astype(BF), "seq", 0, 0, tiled=True)
    columns = [
        spread[i, :, kind * share : (kind + 1) * share] for kind in range(3) for i in range(seqs)
    ]
    quarter = jnp.concatenate(columns, axis=1)
    grad_qkv = gather_rows(quarter, rank).reshape(share, 3 * D).astype(F32)

    def gather_near(block):
        found = [block]
        bit = 2
        while bit < ranks:
            found = found + [swap(one, "rows", bit) for one in found]
            bit *= 2
        for step in range(1, inner):
            found = found + [swap(one, "seq", step) for one in found[: len(found) // step]]
        mine = jnp.concatenate(found, axis=0)
        return jnp.concatenate([mine, swap(mine, "rows", 1)], axis=0)

    ydf_all = gather_near(ydf)
    y1_all, df_all = ydf_all[:, :D], ydf_all[:, D:]
    order = [far * inner + i for i in range(inner) for far in range(Z_STEPS)]
    ff_starts = [i * ff_share + rank * ff_part for i in order]
    take = lambda array, axis: jnp.concatenate(
        [lax.dynamic_slice_in_dim(array, a, ff_part, axis) for a in ff_starts], axis=axis
    )
    up_mine, down_mine, bias_mine = take(up_weight, 1), take(down_weight, 0), take(up_bias, 0)
    u = nn(y1_all, up_mine) + bias_mine
    phi, slope = gelu_parts(u)
    du_all = (nt(df_all, down_mine) * slope).astype(BF)
    g_all = (u * phi).astype(BF)
    group = Z_STEPS * ff_part
    g_near = lax.dynamic_slice_in_dim(g_all, near * group, group, 1)
    grad_down = tn(g_near, df_all).reshape(Z_STEPS, ff_part, D)
    grad_up = pick(tn(y1_all, du_all).reshape(Z_STEPS, inner, share, seqs * ff_part), near, 1)
    ado, grad_up, grad_down = lax.optimization_barrier((ado, grad_up, grad_down))
    ado_all = gather_near(ado[:rows])
    attn_all, do_all = ado_all[:, :D], ado_all[:, D:]
    out_part = D // ranks
    do_mine = lax.dynamic_slice_in_dim(do_all, rank * out_part, out_part, 1)
    grad_out = pick(tn(attn_all, do_mine).reshape(Z_STEPS, inner, share, out_part), near, 1)

    def reduce_far(blocks):
        blocks = blocks.astype(BF)
        far = seq // inner
        summed = pick(blocks, far).astype(F32)
        for step in range(1, Z_STEPS):
            summed = summed + swap(pick(blocks, far ^ step), "seq", step * inner).astype(F32)
        return gather_rows(summed.astype(BF), rank)

    grad_down = reduce_far(grad_down).reshape(ff_share, D).astype(F32)
    grad_up = reduce_far(grad_up).reshape(ranks, share, inner, Z_STEPS, ff_part)
    grad_up = jnp.transpose(grad_up, (1, 3, 2, 0, 4)).reshape(share, FF).astype(F32)
    grad_out = jnp.transpose(reduce_far(grad_out), (1, 0, 2)).reshape(share, D).astype(F32)

    sums = ado[rows:, :D].astype(F32) + ado[rows:, D:].astype(F32)
    placed = lambda kind: lax.dynamic_update_slice_in_dim(
        jnp.zeros((D,), F32), head_sums[0, kind * share : (kind + 1) * share], seq * share, 0
    )
    sums = sums.at[10].set(placed(0)).at[11].set(placed(2))
    for axis, count in (("rows", ranks), ("seq", seqs)):
        bit = 1
        while bit < count:
            sums = sums + swap(sums, axis, bit)
            bit *= 2
    return grad_qkv, sums[10:12].reshape(-1), grad_out, grad_up, grad_down, sums


def body(
    hidden, cotangent, segment_ids, timesteps, qkv_weight, qv_bias, out_weight, out_bias,
    up_weight, up_bias, down_weight, down_bias, norm_gain, norm_bias, time_weight,
):
    assert hidden.shape[0] == 1
    rows = hidden.shape[1]
    seqs, ranks = lax.axis_size("seq"), lax.axis_size("rows")
    length = seqs * rows
    seq, rank = lax.axis_index("seq"), lax.axis_index("rows")
    share = D // seqs
    inner = seqs // Z_STEPS
    fast = seqs == 8 and ranks == 4
    starts = [min(i * share // HD, H - 2) * HD for i in range(seqs)]

    known, gate = gates(ORDER if fast else {})
    features = time_features(timesteps[0]).astype(BF)
    up_row = up_bias.reshape(1, -1)
    weights = [((D, 3 * D), BF), ((D, D), BF), ((D, FF), BF), ((FF, D), BF)]

    def meanwhile():
        known["weights"] = call(
            fetch_kernel,
            "fetch",
            (far(gate("fetch", qkv_weight)), far(out_weight), far(up_weight), far(down_weight)),
            [(*one, NEAR) for one in weights],
            (),
            2,
            4,
        )
        known["fetch"] = known["weights"][1]

    ids = jnp.pad(segment_ids.astype(BF), ((0, 7), (0, D - rows)))
    shards = gather_seq(jnp.concatenate([hidden[0], ids], axis=0), known, gate, meanwhile)
    qkv_near, out_near, up_near, down_near = known["weights"]
    embed = nn(features, time_weight)
    if not fast:
        all_features = gather_rows(features, rank)
        all_features = lax.dynamic_slice_in_dim(all_features, seq * share, share, 2)
    qv_row = qv_bias.reshape(1, -1)
    tile = ((rows, D), BF)
    tile32 = ((rows, D), F32)
    narrow32 = ((rows, 128), F32)
    wide = ((length, D), BF)
    out_row, down_row = out_bias.reshape(1, -1), down_bias.reshape(1, -1)
    x_low, lse, attn, hot, z1, inverse1, result, ydf, dr2, slope, z2_sum = call(
        functools.partial(forward_kernel, seqs),
        "forward",
        (
            *shards, embed, qkv_near, qv_row, out_near, out_row, norm_gain,
            norm_bias, cotangent[0], up_near, up_row, down_near, down_row,
        ),
        [
            (*wide, FAR), narrow32,
            tile32, ((DOCS, length), BF), tile32, narrow32,
            tile, ((rows, 2 * D), BF), tile32, ((rows, FF), F32), ((1, D), F32),
        ],
        [((rows, length), F32), tile32, wide, wide, wide, tile],
        16 if fast else 28,
        1,
    )
    known["forward"] = z1
    if fast:
        ados = [((rows, 3 * D), BF)] * 4
    else:
        ados = [((rows + SUMS, 2 * D), BF)]
    hots = ((DOCS, length), BF)
    docs_shape = ((DOCS, D), F32)
    packed, dr1, docs, hot, *ado = call(
        functools.partial(backward_kernel, starts, len(ados)),
        "backward",
        (
            gate("backward", z1), inverse1, dr2, slope, z2_sum, attn, cotangent[0], hot, lse,
            out_near, up_near, down_near, norm_gain, ydf,
        ),
        [
            ((seqs, rows + 3 * SUMS, PAIR), BF), (*tile32, FAR), (*docs_shape, FAR), (*hots, FAR),
            *((*one, FAR) for one in ados),
        ],
        [tile32, docs_shape, ((SUMS, D), F32), *([tile] * 4 if fast else ados)],
        8,
        3 + 2 * len(ados),
    )
    known["backward"] = packed

    pair = ((length, PAIR), BF)
    head_shape = ((D, 3 * PAIR), BF)
    q_two, k_two, v_two, head_weight = call(
        functools.partial(heads_kernel, share),
        "heads",
        (far(x_low), far(qkv_weight), gate("heads", qv_row)),
        [(*one, FAR) for one in (pair, pair, pair, head_shape)],
        [wide, pair, pair, pair, head_shape, ((3, D, 2 * PAIR), BF)],
        16,
        7 + length // 256,
    )
    known["heads"] = q_two
    if fast:
        near_all = from_chips(*gate("E", ado))
        known["E"] = near_all[1:]
        own_twin = swap(gate("E0", near_all[0]), "rows", 1)
        known["E0"] = own_twin
    arrived = lax.all_to_all(gate("DA", packed), "seq", 0, 0, tiled=True)
    known["DA"] = arrived
    back, sums, *grads = gate(
        "headend",
        head_grad(
            (head_weight, q_two, k_two, v_two, hot, docs, x_low), gate("head", arrived), share,
            4 if fast else 0,
        ),
    )
    known["head"] = back
    if fast:
        up_part, bias_part = call(
            part_weights_kernel,
            "part_weights",
            (far(up_weight), gate("part", up_row)),
            [((D, D), BF, FAR), ((1, D), F32)],
            [((8, D, 384), BF), ((D, D), BF)],
            14,
            9,
        )
        known["part"] = bias_part
        all_features = spread_rows(gate("feat", features))
        known["feat"] = all_features[1:]
        twins = with_twin(gate("Etwin", near_all[1:]))
        near_all = [near_all[0], own_twin, *twins]
        known["Etwin"] = twins[3:]
        up_own, up_sent, down_own, down_sent = feed_grad(
            near_all, up_part, gate("feed", bias_part), down_weight
        )
        known["feed"] = up_own
        up_sent, down_sent = gate("RS1", (up_sent, down_sent))
        up_got, down_got = swap(up_sent, "seq", 2), swap(down_sent, "seq", 4)
        known["RS1"] = (up_got, down_got)
    back = lax.all_to_all(gate("BACK", back), "seq", 0, 0, tiled=True)
    known["BACK"] = back
    blocks, mines = (), ()
    if fast:
        *sent, own = gate("GRS", grads)
        sent = [swap(block, "rows", to + 1) for to, block in enumerate(sent)]
        known["GRS"] = sent
        blocks, mines = (own, *sent), ((own.shape, BF),)
    input_grad, doc_grad, *mine = call(
        functools.partial(input_grad_kernel, share),
        "input_grad",
        (gate("in", back), far(dr1), far(qkv_weight), sums, *(far(one) for one in blocks)),
        [tile32, ((DOCS + SUMS, D), F32), *mines],
        [tile32, ((D, 3 * D), BF), *((one.shape, one.dtype) for one in blocks)],
        12,
        8,
    )
    known["in"] = input_grad
    if fast:
        spread = lax.all_to_all(gate("GA2A", mine[0]), "seq", 0, 0, tiled=True)
        known["GA2A"] = spread
        docs_all = spread_rows(gate("DOCS", doc_grad))
        known["DOCS"] = docs_all[1:]
        up_got, down_got = gate("half", (up_got, down_got))
        halves = [far(one) for one in (up_own, down_own, up_got, down_got)]
        up_sent, down_sent = call(
            combine_half_kernel, "combine_half", halves,
            [((120, D), BF), ((96, D), BF)],
            [(one[1].shape, one[1].dtype) for one in halves],
            8,
            4,
        )
        known["half"] = up_sent
        up_sent, down_sent = gate("RS2", (up_sent, down_sent))
        up_last, down_last = swap(up_sent, "seq", 4), swap(down_sent, "seq", 2)
        known["RS2"] = (up_last, down_last)
        grad_time_weight, norm_sums, bias_sums, grad_up_bias = call(
            time_grad_kernel, "time_grad",
            (*(far(one) for one in all_features), *gate("time", docs_all)),
            [((share, D), F32), ((4, 96), F32), ((2, 96), F32), ((1, 384), F32)],
            [((4 * DOCS, D), BF)],
            8,
            4,
        )
        known["time"] = grad_time_weight
        heads_all = spread_rows(gate("AGG", spread))
        known["AGG"] = heads_all[1:]
        up_last, down_last = gate("all", (up_last, down_last))
        merged = call(
            combine_all_kernel, "combine_all", (*halves, up_last, down_last),
            [((216, D), BF)],
            [(one[1].shape[1:], one[1].dtype) for one in halves],
            8,
            4,
        )[0]
        known["all"] = merged
        merged = gate("AGF", merged)
        across = swap(merged, "rows", 2)
        feed_all = [merged, swap(merged, "rows", 1), across]
        grad_qkv_weight, grad_qv_bias = call(
            finish_heads_kernel, "finish_heads", gate("finh", heads_all),
            [((share, 3 * D), F32), ((1, 192), F32)],
        )
        known["finh"] = grad_qkv_weight
        grad_qv_bias, grad_up_bias = grad_qv_bias[0], grad_up_bias[0]
        grad_out_bias, grad_down_bias = bias_sums[0], bias_sums[1]
        grad_norm_gain, grad_norm_bias = norm_sums[:2], norm_sums[2:]
        others = (
            grad_qkv_weight, grad_qv_bias, grad_up_bias, grad_out_bias, grad_down_bias,
            grad_norm_gain, grad_norm_bias,
        )
        others, held = lax.optimization_barrier((others, across))
        (
            grad_qkv_weight, grad_qv_bias, grad_up_bias, grad_out_bias, grad_down_bias,
            grad_norm_gain, grad_norm_bias,
        ) = others
        feed_all.append(swap(held, "rows", 1))
        grad_up_weight, grad_down_weight, grad_out_weight = call(
            finish_all_kernel, "finish_all", gate("finf", feed_all),
            [((share, FF), F32), ((FF // seqs, D), F32), ((share, D), F32)],
            [((4, 120, D), F32)],
        )
        known["finf"] = grad_out_weight
    else:
        doc_grad = gather_rows(doc_grad[:DOCS], rank).reshape(ranks * DOCS, D)
        grad_time_weight = lax.dot_general(
            all_features.reshape(ranks * DOCS, share).astype(F32),
            doc_grad,
            (((0,), (0,)), ((), ())),
            precision=precise,
        )
        grad_qkv_weight, qv_sums, grad_out_weight, grad_up_weight, grad_down_weight, totals = (
            general_grads(ydf, ado[0], grads[0], grads[1], up_weight, up_bias, down_weight)
        )

        def part_of(vector, axis=0):
            size = vector.shape[axis] // seqs
            return lax.dynamic_slice_in_dim(vector, seq * size, size, axis)

        grad_qv_bias, grad_out_bias = part_of(qv_sums), part_of(totals[4])
        grad_up_bias = part_of(totals[6 : 6 + FF // D].reshape(-1))
        grad_down_bias = part_of(totals[5])
        grad_norm_gain, grad_norm_bias = part_of(totals[0:2], 1), part_of(totals[2:4], 1)

    return (
        result[None],
        input_grad[None],
        grad_qkv_weight,
        grad_qv_bias,
        grad_out_weight,
        grad_out_bias,
        grad_up_weight,
        grad_up_bias,
        grad_down_weight,
        grad_down_bias,
        grad_norm_gain,
        grad_norm_bias,
        grad_time_weight,
    )


def solution(mesh):
    tokens = P("rows", "seq", None)
    whole = P()
    return jax.shard_map(
        body,
        mesh=mesh,
        in_specs=(tokens, tokens, P("rows", "seq"), P("rows", None)) + (whole,) * 11,
        out_specs=(
            tokens,
            tokens,
            P("seq", None),
            P("seq"),
            P("seq", None),
            P("seq"),
            P("seq", None),
            P("seq"),
            P("seq", None),
            P("seq"),
            P(None, "seq"),
            P(None, "seq"),
            P("seq", None),
        ),
        check_vma=False,
    )
```

```python
import functools
import math

import jax
import jax.numpy as jnp
from jax import lax
from jax.experimental import pallas as pl
from jax.experimental.pallas import tpu as pltpu
from jax.sharding import PartitionSpec as P

D = 768
H = 12
HD = 64
FF = 3072
DOCS = 16
PAIR = 2 * HD
PAIRS = D // PAIR
Z_STEPS = 4
SUMS = 16

EPS = 1e-05
MASKED = -1e30
BF = jnp.bfloat16
F32 = jnp.float32
precise = lax.Precision.HIGHEST
VMEM = pl.BlockSpec(memory_space=pltpu.VMEM)


def swap(block, axis, bit):
    return lax.ppermute(block, axis, [(i, i ^ bit) for i in range(lax.axis_size(axis))])


def dot(a, b, dims):
    return lax.dot_general(a, b, (dims, ((), ())), preferred_element_type=F32)


def nn(a, b):
    return dot(a, b, ((1,), (0,)))


def nt(a, b):
    return dot(a, b, ((1,), (1,)))


def tn(a, b):
    return dot(a, b, ((0,), (0,)))


APART = pl.BlockSpec(memory_space=pltpu.HBM)
FAR = "far"
NEAR = "near"


def far(value):
    return FAR, value


def call(kernel, name, ins, outs, scratch=(), vmem=8, copies=0):
    specs = [APART if isinstance(one, tuple) else VMEM for one in ins]
    values = [
        pltpu.with_memory_space_constraint(one[1], pltpu.HBM) if isinstance(one, tuple) else one
        for one in ins
    ]
    held = [pltpu.VMEM(*one) for one in scratch]
    if copies:
        held.append(pltpu.SemaphoreType.DMA((copies,)))
    return pl.pallas_call(
        kernel,
        out_shape=tuple(
            (pltpu.HBM if FAR in one else pltpu.VMEM)(*one[:2])
            if one[2:]
            else jax.ShapeDtypeStruct(*one)
            for one in outs
        ),
        in_specs=specs,
        out_specs=tuple(APART if FAR in one else VMEM for one in outs),
        scratch_shapes=held,
        compiler_params=pltpu.CompilerParams(vmem_limit_bytes=vmem << 20),
        cost_estimate=pl.CostEstimate(flops=int(COSTS[name] * 1e9), transcendentals=0, bytes_accessed=0),
        name=name,
    )(*values)


def copy(source, target, sems, at):
    moved = pltpu.make_async_copy(source, target, sems.at[at])
    moved.start()
    return moved


def copies(pairs, sems, first):
    return [copy(one, to, sems, first + at) for at, (one, to) in enumerate(pairs)]


def wait(moved):
    for one in moved:
        one.wait()


def loop(count, step):
    def body(at, carry):
        step(at)
        return carry

    lax.fori_loop(0, count, body, 0)


def at_rows(index, size):
    return pl.ds(pl.multiple_of(index * size, 8), size)


def at_lanes(index, size):
    return pl.ds(pl.multiple_of(index * size, 128), size)


def time_features(timesteps):
    half_width = D // 2
    frequency = jnp.exp(
        jnp.arange(half_width, dtype=F32) * (-math.log(10000.0) / half_width)
    )
    phases = timesteps.astype(F32)[..., None] * frequency
    return jnp.concatenate([jnp.sin(phases), jnp.cos(phases)], axis=-1)


def gather_seq(block, known, gate, meanwhile):
    size = lax.axis_size("seq")
    inner = size // Z_STEPS
    found = [None] * size
    found[0] = block
    for far in range(1, Z_STEPS):
        name = "Z%d" % far
        found[far * inner] = swap(gate(name, block), "seq", far * inner)
        known[name] = found[far * inner]
    for far in range(Z_STEPS):
        if far == 2:
            meanwhile()
        name = "Y%d" % far
        held = gate(name, found[far * inner])
        for near in range(1, inner):
            found[far * inner + near] = swap(held, "seq", near)
        known[name] = found[far * inner + inner - 1]
    return found


ORDER = {
    "Etwin": ("part", ),
    "RS1": ("feed", "part", ),
    "all": ("time", ),
    "backward": ("Y3", "forward", ),
    "fetch": ("Y0", ),
    "finf": ("finh", ),
    "forward": ("Y3", ),
    "half": ("DOCS", "in", ),
    "part": ("head", ),
}
COSTS = {
    "fetch": 7, "forward": 12, "backward": 5, "heads": 3, "part_weights": 3, "feed_grad": 8,
    "head_grad": 12, "input_grad": 5, "combine_half": 1,
    "combine_all": 1, "finish_all": 2, "finish_heads": 1, "time_grad": 1,
}


def split2(value):
    high = value.astype(BF)
    return high, (value - high.astype(F32)).astype(BF)


def split3(value):
    high = value.astype(BF)
    rest = value - high.astype(F32)
    middle = rest.astype(BF)
    low = (rest - middle.astype(F32)).astype(BF)
    return high, middle, low


def head_start(seq, share):
    return jnp.minimum(seq * share // HD, H - 2) * HD


def head_window(share):
    start = head_start(lax.axis_index("seq"), share)
    base = jnp.minimum(start // PAIR, PAIRS - 2) * PAIR
    return base, (2 * PAIR - (start - base)) % (2 * PAIR)


def normalize(value):
    centered = value - jnp.mean(value, axis=-1, keepdims=True)
    inverse = lax.rsqrt(jnp.mean(centered * centered, axis=-1, keepdims=True) + EPS)
    return centered * inverse, inverse


def normalize_back(z, inverse, grad):
    return inverse * (
        grad
        - jnp.mean(grad, axis=-1, keepdims=True)
        - z * jnp.mean(grad * z, axis=-1, keepdims=True)
    )


def total(value):
    return jnp.sum(value, axis=0, keepdims=True)


def gelu_parts(u):
    phi = 0.5 * (1.0 + lax.erf(u * math.sqrt(0.5)))
    return phi, phi + u * (jnp.exp(-0.5 * u * u) * (1.0 / math.sqrt(2.0 * math.pi)))


def fetch_kernel(*refs):
    count = (len(refs) - 1) // 2
    wait(copies(zip(refs[:count], refs[count:-1]), refs[-1], 0))


def forward_kernel(count, *refs):
    shards = refs[:count]
    embed_ref, qkv_ref, bias_ref, wo_ref, bo_ref, gain_ref, off_ref = refs[count : count + 7]
    cot_ref, up_ref, bu_ref, down_ref, bd_ref = refs[count + 7 : count + 12]
    refs = refs[count + 12 :]
    xlow_out, lse_ref, attn_ref, hot_ref, z1_ref, inverse_ref = refs[:6]
    result_ref, ydf_ref, dr2_ref, slope_ref, z2_sum_ref = refs[6:11]
    mask_ref, x_ref, xlow_ref, k_ref, v_ref, q_ref, sems = refs[11:]
    seq = lax.axis_index("seq")
    rows = attn_ref.shape[0]
    width = D
    parts = [slice(at * width, (at + 1) * width) for at in range(FF // width)]
    embed = jnp.concatenate(split3(embed_ref[...]), axis=0)
    places = lax.broadcasted_iota(jnp.int32, (DOCS, rows), 0).astype(F32)
    hot_own = None
    for at in range(count):
        ids = shards[at][rows : rows + 8, :rows].astype(F32)[:1]
        hot = (places == ids).astype(BF)
        hot_ref[:, at_lanes(seq ^ at, rows)] = hot
        x = shards[at][:rows, :].astype(F32) + tn(jnp.concatenate([hot] * 3, axis=0), embed)
        if at == 0:
            hot_own = hot
            x_ref[...] = x
            own = x.astype(BF)
        xlow_ref[at_rows(seq ^ at, rows), :] = x.astype(BF)
    moved = copy(xlow_ref, xlow_out, sems, 0)
    q_ref[...] = (
        (nn(own, qkv_ref[:, :D]) + bias_ref[:, :D]).astype(BF).astype(F32) * (HD**-0.5)
    ).astype(BF)
    step = 2 * rows
    for at in range(count * rows // step):
        piece = slice(at * step, (at + 1) * step)
        every = xlow_ref[piece, :]
        k_ref[piece, :] = nn(every, qkv_ref[:, D : 2 * D]).astype(BF)
        v_ref[piece, :] = (nn(every, qkv_ref[:, 2 * D :]) + bias_ref[:, D:]).astype(BF)
    mask_ref[...] = (tn(hot_own, hot_ref[...]) - 1.0) * -MASKED
    first = lax.broadcasted_iota(jnp.int32, (rows, PAIR), 1) < HD
    lane = lax.broadcasted_iota(jnp.int32, (rows, 128), 1)
    lse = jnp.zeros((rows, 128), F32)
    for pair in range(PAIRS):
        cols = slice(pair * PAIR, (pair + 1) * PAIR)
        q = q_ref[:, cols]
        halves = []
        for half in range(2):
            q_one = jnp.where(first if half == 0 else ~first, q, jnp.zeros_like(q))
            scores = nt(q_one, k_ref[:, cols]) + mask_ref[...]
            top = jnp.max(scores, axis=-1, keepdims=True)
            weights = jnp.exp(scores - top)
            summed = jnp.sum(weights, axis=-1, keepdims=True)
            halves.append(nn(weights.astype(BF), v_ref[:, cols]) / summed)
            lse = jnp.where(lane == 2 * pair + half, top + jnp.log(summed), lse)
        attn_ref[:, cols] = jnp.where(first, halves[0], halves[1])
    lse_ref[...] = lse
    z1, inverse = normalize(x_ref[...] + nn(attn_ref[...].astype(BF), wo_ref[...]) + bo_ref[...])
    z1_ref[...] = z1
    inverse_ref[...] = jnp.broadcast_to(inverse, (rows, 128))
    y1 = z1 * gain_ref[0:1, :] + off_ref[0:1, :]
    y1_low = y1.astype(BF)
    ydf_ref[:, :D] = y1_low
    r2 = y1 + bd_ref[...]
    for cols in parts:
        u = nn(y1_low, up_ref[:, cols]) + bu_ref[:, cols]
        phi, slope = gelu_parts(u)
        slope_ref[:, cols] = slope
        r2 = r2 + nn((u * phi).astype(BF), down_ref[cols, :])
    z2, inverse2 = normalize(r2)
    result_ref[...] = (z2 * gain_ref[1:2, :] + off_ref[1:2, :]).astype(BF)
    cot = cot_ref[...].astype(F32)
    dr2 = normalize_back(z2, inverse2, cot * gain_ref[1:2, :])
    ydf_ref[:, D:] = dr2.astype(BF)
    dr2_ref[...] = dr2
    z2_sum_ref[...] = total(cot * z2)
    moved.wait()


def backward_kernel(
    starts, chips,
    z1_ref, inverse_ref, dr2_ref, slope_ref, z2_sum_ref, attn_ref, cot_ref, hot_ref, lse_ref,
    wo_ref, up_ref, down_ref, gain_ref, ydf_ref,
    packed_ref, dr1_out, docs_out, hot_out, *refs,
):
    ado_outs, ados = refs[:chips], refs[-chips - 1 : -1]
    dr1_ref, docs_ref, sums_ref = refs[chips : chips + 3]
    sems = refs[-1]
    rows = z1_ref.shape[0]
    moved = [copy(hot_ref, hot_out, sems, 0)]
    if chips > 1:
        moved += copies([(ydf_ref, one.at[:, : 2 * D]) for one in ado_outs], sems, 3 + chips)
        ado_outs = [one.at[:, 2 * D :] for one in ado_outs]
    z1 = z1_ref[...]
    dr2 = dr2_ref[...]
    df_low = dr2.astype(BF)
    dy1 = dr2
    width = D
    for at in range(FF // width):
        cols = slice(at * width, (at + 1) * width)
        du_low = (nt(df_low, down_ref[cols, :]) * slope_ref[:, cols]).astype(BF)
        sums_ref[6 + at : 7 + at, :] = total(du_low.astype(F32))
        dy1 = dy1 + nt(du_low, up_ref[:, cols])
    dr1 = normalize_back(z1, inverse_ref[:, 0:1], dy1 * gain_ref[0:1, :])
    dr1_ref[...] = dr1
    moved.append(copy(dr1_ref, dr1_out, sems, 1))
    do_low = dr1.astype(BF)
    da = nt(do_low, wo_ref[...]).astype(BF)
    attn = attn_ref[...]
    to_heads = (
        lax.broadcasted_iota(jnp.int32, (D, 128), 0) // HD
        == lax.broadcasted_iota(jnp.int32, (D, 128), 1)
    ).astype(BF)
    high, middle, low = split3(da.astype(F32) * attn)
    delta = nn(high, to_heads) + nn(middle, to_heads) + nn(low, to_heads)
    lse_first, delta_first = lse_ref[...].T, delta.T
    cot = cot_ref[...].astype(F32)
    sums_ref[0:1, :] = total(dy1 * z1)
    sums_ref[1:2, :] = z2_sum_ref[...]
    sums_ref[2:3, :] = total(dy1)
    sums_ref[3:4, :] = total(cot)
    sums_ref[4:5, :] = total(do_low.astype(F32))
    sums_ref[5:6, :] = total(df_low.astype(F32))
    sums_ref[6 + FF // width :, :] = jnp.zeros((SUMS - 6 - FF // width, D), F32)
    share = D // len(starts)
    for at, start in enumerate(starts):
        packed_ref[at, :rows, :] = da[:, start : start + PAIR]
        head = start // HD
        lines = [lse_first[head : head + 2], delta_first[head : head + 2]]
        if chips > 1:
            mine = sums_ref[:6, at * share : (at + 1) * share]
            lines.append(jnp.concatenate([mine, jnp.zeros((6, 128 - share), F32)], axis=1))
            for part in range(3):
                first = at * 4 * share + part * 128
                lines.append(sums_ref[6 + first // D : 7 + first // D, first % D : first % D + 128])
        used = sum(one.shape[0] for one in lines)
        lines.append(jnp.zeros((SUMS - used, 128), F32))
        lines = jnp.concatenate(lines, axis=0)
        parts = jnp.concatenate([one.astype(F32) for one in split3(lines)], axis=0).astype(BF)
        packed_ref[at, rows:, :] = parts
    hot = hot_ref[:, at_lanes(lax.axis_index("seq"), rows)]
    high, middle, low = split3(dr1)
    docs_ref[...] = nn(hot, high) + nn(hot, middle) + nn(hot, low)
    moved.append(copy(docs_ref, docs_out, sems, 2))
    attn = attn.astype(BF)
    if chips == 1:
        high, low = split2(sums_ref[...])
        ados[0][:rows, :D] = attn
        ados[0][:rows, D:] = do_low
        ados[0][rows:, :D] = high
        ados[0][rows:, D:] = low
    else:
        near, across = lax.axis_index("seq") % 2, lax.axis_index("rows") // 2
        shares = [
            jnp.concatenate(
                [attn[:, (2 * z + y) * 96 : (2 * z + y + 1) * 96] for z in range(4)], axis=1
            )
            for y in range(2)
        ]
        sides = do_low[:, : D // 2], do_low[:, D // 2 :]
        for to, ref in enumerate(ados):
            swapped, over = to // 2, to % 2
            ref[:, : D // 2] = jnp.where(near == swapped, shares[0], shares[1])
            ref[:, D // 2 :] = jnp.where(across == over, sides[0], sides[1])
    moved += copies(zip(ados, ado_outs), sems, 3)
    wait(moved)


def heads_kernel(share, x_in, qkv_in, bias_ref, *refs):
    q_out, k_out, v_out, w_out, x_ref, q_ref, k_ref, v_ref, w_ref, wide_ref, sems = refs
    length = x_ref.shape[0]
    base, back = head_window(share)
    windows = copies(
        [
            (qkv_in.at[:, pl.ds(pl.multiple_of(base + kind * D, PAIR), 2 * PAIR)], wide_ref.at[kind])
            for kind in range(3)
        ],
        sems,
        0,
    )
    step = 256
    pieces = [slice(at * step, (at + 1) * step) for at in range(length // step)]
    loads = copies([(x_in.at[one, :], x_ref.at[one, :]) for one in pieces], sems, 3)
    biases = []
    for kind in range(3):
        windows[kind].wait()
        turned = pltpu.roll(wide_ref[kind].astype(F32), back, 1)[:, :PAIR]
        w_ref[:, kind * PAIR : (kind + 1) * PAIR] = turned.astype(BF)
        if kind == 1:
            biases.append(jnp.zeros((1, PAIR), F32))
        else:
            cols = pl.ds(pl.multiple_of(base + (kind // 2) * D, PAIR), 2 * PAIR)
            bias = jnp.broadcast_to(bias_ref[:, cols], (8, 2 * PAIR))
            biases.append(pltpu.roll(bias, back, 1)[:1, :PAIR])
    first = 3 + len(pieces)
    moved = [copy(w_ref, w_out, sems, first)]
    for at, piece in enumerate(pieces):
        loads[at].wait()
        three = nn(x_ref[piece, :], w_ref[...])
        q_ref[piece, :] = (
            (three[:, :PAIR] + biases[0]).astype(BF).astype(F32) * (HD**-0.5)
        ).astype(BF)
        k_ref[piece, :] = three[:, PAIR : 2 * PAIR].astype(BF)
        v_ref[piece, :] = (three[:, 2 * PAIR :] + biases[2]).astype(BF)
    moved += copies(((q_ref, q_out), (k_ref, k_out), (v_ref, v_out)), sems, first + 1)
    wait(moved)


def head_grad_kernel(step, share, split, *refs):
    w_in, q_in, k_in, v_in, hot_in, docs_in, x_in, da_ref, back_ref, sums_ref = refs[:10]
    w_ref, q_ref, k_ref, v_ref, hot_ref, docs_ref, x_ref = refs[-13:-6]
    dq_ref, dk_ref, dv_ref, heads_ref, grad_ref, sems = refs[-6:]
    outs = refs[10:-13]
    if split:
        *outs, own_ref = outs
    length = q_ref.shape[0]
    rows = length // (D // share)
    seq = lax.axis_index("seq")
    loads = copies(
        (
            (hot_in, hot_ref), (v_in, v_ref), (k_in, k_ref), (q_in, q_ref),
            (w_in, w_ref), (docs_in, docs_ref), (x_in, x_ref),
        ),
        sems,
        0,
    )
    wait(loads[:4])
    first = lax.broadcasted_iota(jnp.int32, (step, PAIR), 1) < HD
    each = step // rows
    sums = jnp.zeros((SUMS, rows), F32)
    for at in range(D // share):
        lines = da_ref[at, rows:, :].astype(F32)
        sums = sums + (lines[:SUMS] + lines[SUMS : 2 * SUMS] + lines[2 * SUMS :])
    sums_ref[...] = sums
    dk_ref[...] = jnp.zeros((length, PAIR), F32)
    dv_ref[...] = jnp.zeros((length, PAIR), F32)

    @functools.partial(loop, length // step)
    def _(at):
        piece = at_rows(at, step)
        blocks = [at * each + one for one in range(each)]
        da_all = jnp.concatenate([da_ref[one, :rows, :] for one in blocks], axis=0)
        stats = jnp.concatenate(
            [da_ref[one, rows:, :].astype(F32) for one in blocks], axis=1
        )
        stats = stats[:SUMS] + stats[SUMS : 2 * SUMS] + stats[2 * SUMS :]
        mask = (tn(hot_ref[...], hot_ref[:, at_lanes(at, step)]) - 1.0) * -MASKED
        halves = []
        for half in range(2):
            here = first if half == 0 else ~first
            q = jnp.where(here, q_ref[piece, :], jnp.zeros((step, PAIR), BF))
            da = jnp.where(here, da_all, jnp.zeros((step, PAIR), BF))
            probs = jnp.exp(nt(k_ref[...], q) + (mask - stats[half : half + 1]))
            ds = (probs * (nt(v_ref[...], da) - stats[2 + half : 3 + half])).astype(BF)
            halves.append(tn(ds, k_ref[...]))
            dk_ref[...] += nn(ds, q)
            dv_ref[...] += nn(probs.astype(BF), da)
        dq_ref[piece, :] = jnp.where(first, halves[0], halves[1]) * (HD**-0.5)

    wait(loads[4:])
    offset = seq * share - head_start(seq, share)
    left = (PAIR - offset) % PAIR
    for at in range(length // step):
        piece = slice(at * step, (at + 1) * step)
        heads_ref[piece, :] = jnp.concatenate(
            [pltpu.roll(ref[piece, :], left, 1)[:, :share] for ref in (dq_ref, dk_ref, dv_ref)],
            axis=1,
        ).astype(BF)
    doc_sums = nn(hot_ref[...], heads_ref[...])
    docs = docs_ref[...]
    for kind in range(3):
        piece = doc_sums[:, kind * share : (kind + 1) * share]
        piece = jnp.concatenate([piece, jnp.zeros((DOCS, PAIR - share), F32)], axis=1)
        parts = jnp.concatenate(split3(pltpu.roll(piece, offset, 1)), axis=0)
        product = nt(parts, w_ref[:, kind * PAIR : (kind + 1) * PAIR])
        docs = docs + (product[:DOCS] + product[DOCS : 2 * DOCS] + product[2 * DOCS :])
    docs = docs.astype(BF)
    extra = back_ref.shape[1] - 6 * DOCS
    full = 3 * share // PAIR
    rest = 3 * share % PAIR
    group = rows * rest // PAIR
    for at in range(D // share):
        for part in range(full):
            back_ref[at, part * rows : (part + 1) * rows, :] = heads_ref[
                at * rows : (at + 1) * rows, part * PAIR : (part + 1) * PAIR
            ]
        back_ref[at, full * rows : extra, :] = jnp.concatenate(
            [
                heads_ref[first : first + group, full * PAIR :]
                for first in range(at * rows, (at + 1) * rows, group)
            ],
            axis=1,
        )
        for col in range(PAIRS):
            back_ref[at, extra + col * DOCS : extra + (col + 1) * DOCS, :] = docs[
                :, col * PAIR : (col + 1) * PAIR
            ]
    if not split:
        outs[0][...] = tn(x_ref[...], heads_ref[...])
        outs[1][...] = total(doc_sums)
        return
    *sent, mine_out = outs
    grad_ref[...] = tn(x_ref[...], heads_ref[...])
    rank = lax.axis_index("rows")
    part = share // split
    high, low = split2(jnp.broadcast_to(total(doc_sums), (8, 3 * share)))
    row = lax.broadcasted_iota(jnp.int32, (8, 3 * share), 0)
    tail = jnp.where(row == 0, high.astype(F32), jnp.where(row == 1, low.astype(F32), 0.0))
    for to, ref in enumerate([own_ref] + list(sent)):
        for at in range(D // share):
            here = pl.ds(pl.multiple_of(at * share + (rank ^ to) * part, 8), part)
            ref[at, :part, :] = grad_ref[here, :].astype(ref.dtype)
            ref[at, part:, :] = tail.astype(ref.dtype)
        if to == 0:
            moved = copy(own_ref, mine_out, sems, 7)
    moved.wait()


def head_grad(apart, da, share, split):
    length = apart[1].shape[0]
    count = D // share
    rows = length // count
    outs = [((count, rows * 3 * share // PAIR + 6 * DOCS, PAIR), BF), ((SUMS, rows), F32)]
    if split:
        block = (count, share // split + 8, 3 * share)
        outs += [(block, BF)] * (split - 1) + [(block, F32, FAR)]
    else:
        outs += [((D, 3 * share), F32), ((1, 3 * share), F32)]
    scratch = [(block, F32)] if split else []
    scratch += [(one.shape, one.dtype) for one in apart] + [((length, PAIR), F32)] * 3
    scratch += [((length, 3 * share), BF), ((D, 3 * share), F32)]
    return call(
        functools.partial(head_grad_kernel, 512, share, split),
        "head_grad",
        (*(far(one) for one in apart), da),
        outs,
        scratch,
        24 if length <= 1024 else 44,
        8,
    )


def combine(blocks, out_ref):
    value = blocks[0][...]
    for ref in blocks[1:]:
        value = value + ref[...].astype(F32)
    count, rows, wide = value.shape
    out_ref[:, : rows - 8, :] = value[:, : rows - 8].astype(out_ref.dtype)
    row = lax.broadcasted_iota(jnp.int32, (8, wide), 0)
    for at in range(count):
        last = value[at, rows - 8 :]
        high, low = split2(jnp.broadcast_to(last[0:1] + last[1:2], (8, wide)))
        out_ref[at, rows - 8 :, :] = jnp.where(
            row == 0, high.astype(F32), jnp.where(row == 1, low.astype(F32), 0.0)
        ).astype(out_ref.dtype)


def input_grad_kernel(share, back_ref, dr1_in, qkv_in, sums_ref, *refs):
    blocks = ()
    if len(refs) > 5:
        blocks, held, refs = refs[:4], refs[-5:-1], refs[4:-5] + refs[-1:]
    grad_ref, docs_ref, *mine_ref, dr1_ref, qkv_ref, sems = refs
    blocks = copies(zip(blocks, held), sems, 4) if blocks else ()
    loads = copies(
        [(qkv_in.at[:, c], qkv_ref.at[:, c]) for c in [slice(i * D, i * D + D) for i in range(3)]],
        sems,
        0,
    )
    loads.append(copy(dr1_in, dr1_ref, sems, 3))
    rows = dr1_ref.shape[0]
    count = D // share
    extra = back_ref.shape[1] - 6 * DOCS
    full = 3 * share // PAIR
    rest = 3 * share % PAIR
    kinds = [[], [], []]
    for at in range(count):
        here = [back_ref[at, part * rows : (part + 1) * rows, :] for part in range(full)]
        last = back_ref[at, full * rows : extra, :]
        here.append(
            jnp.concatenate([last[:, c : c + rest] for c in range(0, PAIR, rest)], axis=0)
        )
        here = jnp.concatenate(here, axis=1)
        for kind in range(3):
            kinds[kind].append(here[:, kind * share : (kind + 1) * share])
    docs = jnp.zeros((6 * DOCS, PAIR), F32)
    for at in range(count):
        docs = docs + back_ref[at, extra:, :].astype(F32)
    docs_ref[:DOCS, :] = jnp.concatenate(
        [docs[at * DOCS : (at + 1) * DOCS] for at in range(PAIRS)], axis=1
    )
    docs_ref[DOCS:, :128] = sums_ref[...]
    docs_ref[DOCS:, 128:] = jnp.zeros((SUMS, D - 128), F32)
    loads[3].wait()
    result = dr1_ref[...]
    for kind in range(3):
        cols = slice(kind * D, (kind + 1) * D)
        loads[kind].wait()
        result = result + nt(jnp.concatenate(kinds[kind], axis=1), qkv_ref[:, cols])
    grad_ref[...] = result
    if blocks:
        wait(blocks)
        combine(held, mine_ref[0])


def unit_share(at):
    return 2 * (at % 4) + at // 4


def part_weights_kernel(up_in, bu_ref, up_out, bu_out, held_ref, up_ref, sems):
    back = (384 - lax.axis_index("rows") * 96) % 384
    loads = copies(
        [
            (up_in.at[:, unit_share(at) * 384 : (unit_share(at) + 1) * 384], held_ref.at[at])
            for at in range(8)
        ],
        sems,
        0,
    )
    ups, biases = [], []
    for at in range(8):
        cols = slice(unit_share(at) * 384, (unit_share(at) + 1) * 384)
        loads[at].wait()
        ups.append(pltpu.roll(held_ref[at].astype(F32), back, 1)[:, :96].astype(BF))
        bias = jnp.broadcast_to(bu_ref[:, cols], (8, 384))
        biases.append(pltpu.roll(bias, back, 1)[:1, :96])
    up_ref[...] = jnp.concatenate(ups, axis=1)
    moved = copy(up_ref, up_out, sems, 8)
    bu_out[...] = jnp.concatenate(biases, axis=1)
    moved.wait()


def feed_grad_kernel(*refs):
    pieces = refs[:8]
    up_in, bu_ref, down_in, up_own_out, up_sent_ref, down_own_out, down_sent_ref = refs[8:15]
    all_ref, up_ref, down_ref, g_ref, du_ref = refs[15:20]
    up_grad_ref, down_grad_ref, out_grad_ref, up_own_ref, down_own_ref, sems = refs[20:]
    seq, rank = lax.axis_index("seq"), lax.axis_index("rows")
    near, z = seq % 2, seq // 2
    rows = pieces[0].shape[0]
    loads = [copy(up_in, up_ref, sems, 8)]
    loads += copies([(pieces[at], all_ref.at[at]) for at in range(2)], sems, 0)
    first = rank * 96
    downs = copies(
        [
            (
                down_in.at[pl.ds(pl.multiple_of(unit_share(at) * 384 + first, 32), 96), :],
                down_ref.at[at * 96 : (at + 1) * 96, :],
            )
            for at in range(8)
        ],
        sems,
        9,
    )
    loads += copies([(pieces[at], all_ref.at[at]) for at in range(2, 8)], sems, 2)
    loads[0].wait()
    step = 2 * rows
    for at in range(4):
        wait(loads[1 + 2 * at : 3 + 2 * at])
        piece = slice(at * step, (at + 1) * step)
        two = slice(2 * at, 2 * at + 2)
        u = nn(all_ref[two, :, :D].reshape(step, D), up_ref[...]) + bu_ref[...]
        phi, slope = gelu_parts(u)
        if at == 0:
            wait(downs)
        g_ref[piece, :] = (u * phi).astype(BF)
        df = all_ref[two, :, D : 2 * D].reshape(step, D)
        du_ref[piece, :] = (nt(df, down_ref[...]) * slope).astype(BF)

    tokens = 8 * rows
    df = all_ref[:, :, D : 2 * D].reshape(tokens, D)
    down_grad_ref[...] = tn(g_ref[:, at_lanes(near, 384)], df)
    up_grad_ref[...] = tn(all_ref[:, :, :D].reshape(tokens, D), du_ref[...])
    base = pl.multiple_of(2 * D + D // 2 + (rank % 2) * 128, 128)
    attn = all_ref[:, :, 2 * D : 2 * D + D // 2].reshape(tokens, D // 2)
    do = all_ref[:, :, pl.ds(base, 256)].reshape(tokens, 256)
    back = (256 - (rank % 2) * 64) % 256
    out_grad_ref[...] = pltpu.roll(tn(attn, do), back, 1)
    for to in range(4):
        up_rows = pl.ds(pl.multiple_of((2 * (z ^ to) + near) * 96, 8), 96)
        down_rows = pl.ds(pl.multiple_of((z ^ to) * 96, 8), 96)
        ref = up_own_ref.at[to // 2] if to % 2 == 0 else up_sent_ref.at[to // 2]
        ref[:96, :] = up_grad_ref[up_rows, :].astype(ref.dtype)
        out = out_grad_ref[down_rows, :192]
        ref[96:, :] = jnp.concatenate(
            [out[part * 24 : (part + 1) * 24] for part in range(4)], axis=1
        ).astype(ref.dtype)
        ref = down_own_ref.at[to % 2] if to < 2 else down_sent_ref.at[to % 2]
        ref[...] = down_grad_ref[down_rows, :].astype(ref.dtype)
    wait(copies(((up_own_ref, up_own_out), (down_own_ref, down_own_out)), sems, 17))


def feed_grad(pieces, up, bias, down):
    tokens = 8 * pieces[0].shape[0]
    blocks = (2, 120, D), (2, 96, D)
    wide = ((tokens, D), BF)
    return call(
        feed_grad_kernel,
        "feed_grad",
        (*(far(one) for one in pieces), far(up), bias, far(down)),
        [one for block in blocks for one in ((block, F32, FAR), (block, BF))],
        [
            ((8, tokens // 8, 3 * D), BF), ((D, D), BF), ((D, D), BF), wide, wide,
            ((D, D), F32), ((384, D), F32), ((384, 256), F32),
            *((block, F32) for block in blocks),
        ],
        28,
        19,
    )


def combine_half_kernel(up_in, down_in, up_got_in, down_got_in, up_ref, down_ref, *refs):
    *held, sems = refs
    loads = copies(zip((up_in, down_in, up_got_in, down_got_in), held), sems, 0)
    wait(loads)
    up_ref[...] = (held[0][1] + held[2][1].astype(F32)).astype(BF)
    down_ref[...] = (held[1][1] + held[3][1].astype(F32)).astype(BF)


def combine_all_kernel(up_in, down_in, up_got_in, down_got_in, up_last_ref, down_last_ref, out_ref, *refs):
    *held, sems = refs
    sources = [one.at[0] for one in (up_in, down_in, up_got_in, down_got_in)]
    wait(copies(zip(sources, held), sems, 0))
    up = held[0][...] + held[2][...].astype(F32) + up_last_ref[...].astype(F32)
    down = held[1][...] + held[3][...].astype(F32) + down_last_ref[...].astype(F32)
    out_ref[:120, :] = up.astype(BF)
    out_ref[120:, :] = down.astype(BF)


def finish_all_kernel(a_ref, b_ref, c_ref, d_ref, up_ref, down_ref, out_ref, held_ref):
    rank = lax.axis_index("rows")
    for at, ref in enumerate((a_ref, b_ref, c_ref, d_ref)):
        held_ref[rank ^ at] = ref[:120, :].astype(F32)
        down_ref[pl.ds(pl.multiple_of((rank ^ at) * 96, 8), 96), :] = ref[120:, :].astype(F32)
    for share in range(8):
        at = (share // 2) + 4 * (share % 2)
        up_ref[:, share * 384 : (share + 1) * 384] = jnp.concatenate(
            [held_ref[r, :96, at * 96 : (at + 1) * 96] for r in range(4)], axis=1
        )
    for at in range(4):
        out_ref[at * 24 : (at + 1) * 24, :] = jnp.concatenate(
            [held_ref[r, 96:, at * 192 : (at + 1) * 192] for r in range(4)], axis=1
        )


def time_grad_kernel(*refs):
    features, docs, (out_ref, norm_ref, bias_ref, up_ref, left_ref, sems) = refs[:4], refs[4:8], refs[8:]
    seq = lax.axis_index("seq")
    wait(
        copies([(ref, left_ref.at[at * DOCS : (at + 1) * DOCS]) for at, ref in enumerate(features)], sems, 0)
    )
    left = left_ref[...].astype(F32)
    left = pltpu.roll(left, (D - seq * 96) % D, 1)[:, :96].astype(BF)
    high, middle, low = split3(jnp.concatenate([ref[:DOCS, :] for ref in docs], axis=0))
    out_ref[...] = tn(left, high) + tn(left, middle) + tn(left, low)
    sums = jnp.zeros((SUMS, 128), F32)
    for ref in docs:
        sums = sums + ref[DOCS:, :128]
    norm_ref[...] = sums[4:8, :96]
    bias_ref[...] = sums[8:10, :96]
    up_ref[...] = jnp.concatenate([sums[at : at + 1] for at in range(10, 13)], axis=1)


def finish_heads_kernel(a_ref, b_ref, c_ref, d_ref, out_ref, bias_ref):
    rank = lax.axis_index("rows")
    order = [(kind, at) for kind in range(3) for at in range(8)]
    for to, ref in enumerate((a_ref, b_ref, c_ref, d_ref)):
        value = jnp.concatenate(
            [ref[at, :24, kind * 96 : (kind + 1) * 96].astype(F32) for kind, at in order], axis=1
        )
        out_ref[pl.ds(pl.multiple_of((rank ^ to) * 24, 8), 24), :] = value
    tail = jnp.concatenate(
        [a_ref[at, 24:, kind * 96 : (kind + 1) * 96].astype(F32) for kind, at in order], axis=1
    )
    sums = tail[0:1] + tail[1:2]
    sums = jnp.concatenate([sums[:, :D], sums[:, 2 * D :]], axis=1)
    back = (2 * D - lax.axis_index("seq") * 192) % (2 * D)
    bias_ref[...] = pltpu.roll(jnp.broadcast_to(sums, (8, 2 * D)), back, 1)[:1, :192]


def after(value, *others):
    return lax.optimization_barrier((value,) + others)[0]


def after_all(values, *others):
    return list(lax.optimization_barrier((tuple(values), others))[0])


def gates(order):
    known = {}

    def gate(name, value):
        held = [known[one] for one in order.get(name, ()) if one in known]
        return lax.optimization_barrier((value, held))[0] if held else value

    return known, gate


def from_chips(own, over, near, both):
    pairs = [((s * 4 + r), ((s ^ 1) * 4 + (r ^ 2))) for s in range(8) for r in range(4)]
    across = lax.ppermute(both, ("seq", "rows"), pairs)
    return [own, swap(over, "rows", 2), swap(near, "seq", 1), across]


def with_twin(blocks):
    return blocks + [swap(one, "rows", 1) for one in blocks]


def spread_rows(block):
    across = swap(block, "rows", 2)
    return block, swap(block, "rows", 1), across, swap(across, "rows", 1)


def pick(blocks, index, axis=0):
    return lax.dynamic_index_in_dim(blocks, index, axis, keepdims=False)


def reduce_rows(blocks, place):
    bit = 1
    while blocks.shape[0] > 1:
        pairs = blocks.reshape((blocks.shape[0] // 2, 2) + blocks.shape[1:])
        mine = (place // bit) % 2
        sent = swap(pick(pairs, 1 - mine, 1).astype(BF), "rows", bit)
        blocks = pick(pairs, mine, 1).astype(F32) + sent.astype(F32)
        bit *= 2
    return blocks[0]


def gather_rows(block, place):
    count = lax.axis_size("rows")
    found = block[None]
    bit = count // 2
    while bit >= 1:
        other = swap(found, "rows", bit)
        mine = (place // bit) % 2
        low, high = jnp.where(mine == 0, found, other), jnp.where(mine == 0, other, found)
        if bit == count // 2:
            found = jnp.concatenate([low, high], axis=0)
        else:
            found = jnp.stack([low, high], axis=1).reshape((-1,) + block.shape)
        bit //= 2
    return found


def general_grads(ydf, ado, grad_heads, head_sums, up_weight, up_bias, down_weight):
    seqs, ranks = lax.axis_size("seq"), lax.axis_size("rows")
    seq, rank = lax.axis_index("seq"), lax.axis_index("rows")
    inner = seqs // Z_STEPS
    near = seq % inner
    share = D // seqs
    ff_share = FF // seqs
    ff_part = ff_share // ranks
    rows = ydf.shape[0]

    part = share // ranks
    grad_heads = grad_heads.reshape(seqs, ranks, part, 3 * share)
    mine = reduce_rows(jnp.moveaxis(grad_heads, 1, 0), rank)
    spread = lax.all_to_all(mine.astype(BF), "seq", 0, 0, tiled=True)
    columns = [
        spread[i, :, kind * share : (kind + 1) * share] for kind in range(3) for i in range(seqs)
    ]
    quarter = jnp.concatenate(columns, axis=1)
    grad_qkv = gather_rows(quarter, rank).reshape(share, 3 * D).astype(F32)

    def gather_near(block):
        found = [block]
        bit = 2
        while bit < ranks:
            found = found + [swap(one, "rows", bit) for one in found]
            bit *= 2
        for step in range(1, inner):
            found = found + [swap(one, "seq", step) for one in found[: len(found) // step]]
        mine = jnp.concatenate(found, axis=0)
        return jnp.concatenate([mine, swap(mine, "rows", 1)], axis=0)

    ydf_all = gather_near(ydf)
    y1_all, df_all = ydf_all[:, :D], ydf_all[:, D:]
    order = [far * inner + i for i in range(inner) for far in range(Z_STEPS)]
    ff_starts = [i * ff_share + rank * ff_part for i in order]
    take = lambda array, axis: jnp.concatenate(
        [lax.dynamic_slice_in_dim(array, a, ff_part, axis) for a in ff_starts], axis=axis
    )
    up_mine, down_mine, bias_mine = take(up_weight, 1), take(down_weight, 0), take(up_bias, 0)
    u = nn(y1_all, up_mine) + bias_mine
    phi, slope = gelu_parts(u)
    du_all = (nt(df_all, down_mine) * slope).astype(BF)
    g_all = (u * phi).astype(BF)
    group = Z_STEPS * ff_part
    g_near = lax.dynamic_slice_in_dim(g_all, near * group, group, 1)
    grad_down = tn(g_near, df_all).reshape(Z_STEPS, ff_part, D)
    grad_up = pick(tn(y1_all, du_all).reshape(Z_STEPS, inner, share, seqs * ff_part), near, 1)
    ado, grad_up, grad_down = lax.optimization_barrier((ado, grad_up, grad_down))
    ado_all = gather_near(ado[:rows])
    attn_all, do_all = ado_all[:, :D], ado_all[:, D:]
    out_part = D // ranks
    do_mine = lax.dynamic_slice_in_dim(do_all, rank * out_part, out_part, 1)
    grad_out = pick(tn(attn_all, do_mine).reshape(Z_STEPS, inner, share, out_part), near, 1)

    def reduce_far(blocks):
        blocks = blocks.astype(BF)
        far = seq // inner
        summed = pick(blocks, far).astype(F32)
        for step in range(1, Z_STEPS):
            summed = summed + swap(pick(blocks, far ^ step), "seq", step * inner).astype(F32)
        return gather_rows(summed.astype(BF), rank)

    grad_down = reduce_far(grad_down).reshape(ff_share, D).astype(F32)
    grad_up = reduce_far(grad_up).reshape(ranks, share, inner, Z_STEPS, ff_part)
    grad_up = jnp.transpose(grad_up, (1, 3, 2, 0, 4)).reshape(share, FF).astype(F32)
    grad_out = jnp.transpose(reduce_far(grad_out), (1, 0, 2)).reshape(share, D).astype(F32)

    sums = ado[rows:, :D].astype(F32) + ado[rows:, D:].astype(F32)
    placed = lambda kind: lax.dynamic_update_slice_in_dim(
        jnp.zeros((D,), F32), head_sums[0, kind * share : (kind + 1) * share], seq * share, 0
    )
    sums = sums.at[10].set(placed(0)).at[11].set(placed(2))
    for axis, count in (("rows", ranks), ("seq", seqs)):
        bit = 1
        while bit < count:
            sums = sums + swap(sums, axis, bit)
            bit *= 2
    return grad_qkv, sums[10:12].reshape(-1), grad_out, grad_up, grad_down, sums


def body(
    hidden, cotangent, segment_ids, timesteps, qkv_weight, qv_bias, out_weight, out_bias,
    up_weight, up_bias, down_weight, down_bias, norm_gain, norm_bias, time_weight,
):
    assert hidden.shape[0] == 1
    rows = hidden.shape[1]
    seqs, ranks = lax.axis_size("seq"), lax.axis_size("rows")
    length = seqs * rows
    seq, rank = lax.axis_index("seq"), lax.axis_index("rows")
    share = D // seqs
    inner = seqs // Z_STEPS
    fast = seqs == 8 and ranks == 4
    starts = [min(i * share // HD, H - 2) * HD for i in range(seqs)]

    known, gate = gates(ORDER if fast else {})
    features = time_features(timesteps[0]).astype(BF)
    up_row = up_bias.reshape(1, -1)
    weights = [((D, 3 * D), BF), ((D, D), BF), ((D, FF), BF), ((FF, D), BF)]

    def meanwhile():
        known["weights"] = call(
            fetch_kernel,
            "fetch",
            (far(gate("fetch", qkv_weight)), far(out_weight), far(up_weight), far(down_weight)),
            [(*one, NEAR) for one in weights],
            (),
            2,
            4,
        )
        known["fetch"] = known["weights"][1]

    ids = jnp.pad(segment_ids.astype(BF), ((0, 7), (0, D - rows)))
    shards = gather_seq(jnp.concatenate([hidden[0], ids], axis=0), known, gate, meanwhile)
    qkv_near, out_near, up_near, down_near = known["weights"]
    embed = nn(features, time_weight)
    if not fast:
        all_features = gather_rows(features, rank)
        all_features = lax.dynamic_slice_in_dim(all_features, seq * share, share, 2)
    qv_row = qv_bias.reshape(1, -1)
    tile = ((rows, D), BF)
    tile32 = ((rows, D), F32)
    narrow32 = ((rows, 128), F32)
    wide = ((length, D), BF)
    out_row, down_row = out_bias.reshape(1, -1), down_bias.reshape(1, -1)
    x_low, lse, attn, hot, z1, inverse1, result, ydf, dr2, slope, z2_sum = call(
        functools.partial(forward_kernel, seqs),
        "forward",
        (
            *shards, embed, qkv_near, qv_row, out_near, out_row, norm_gain,
            norm_bias, cotangent[0], up_near, up_row, down_near, down_row,
        ),
        [
            (*wide, FAR), narrow32,
            tile32, ((DOCS, length), BF), tile32, narrow32,
            tile, ((rows, 2 * D), BF), tile32, ((rows, FF), F32), ((1, D), F32),
        ],
        [((rows, length), F32), tile32, wide, wide, wide, tile],
        16 if fast else 28,
        1,
    )
    known["forward"] = z1
    if fast:
        ados = [((rows, 3 * D), BF)] * 4
    else:
        ados = [((rows + SUMS, 2 * D), BF)]
    hots = ((DOCS, length), BF)
    docs_shape = ((DOCS, D), F32)
    packed, dr1, docs, hot, *ado = call(
        functools.partial(backward_kernel, starts, len(ados)),
        "backward",
        (
            gate("backward", z1), inverse1, dr2, slope, z2_sum, attn, cotangent[0], hot, lse,
            out_near, up_near, down_near, norm_gain, ydf,
        ),
        [
            ((seqs, rows + 3 * SUMS, PAIR), BF), (*tile32, FAR), (*docs_shape, FAR), (*hots, FAR),
            *((*one, FAR) for one in ados),
        ],
        [tile32, docs_shape, ((SUMS, D), F32), *([tile] * 4 if fast else ados)],
        8,
        3 + 2 * len(ados),
    )
    known["backward"] = packed

    pair = ((length, PAIR), BF)
    head_shape = ((D, 3 * PAIR), BF)
    q_two, k_two, v_two, head_weight = call(
        functools.partial(heads_kernel, share),
        "heads",
        (far(x_low), far(qkv_weight), gate("heads", qv_row)),
        [(*one, FAR) for one in (pair, pair, pair, head_shape)],
        [wide, pair, pair, pair, head_shape, ((3, D, 2 * PAIR), BF)],
        16,
        7 + length // 256,
    )
    known["heads"] = q_two
    if fast:
        near_all = from_chips(*gate("E", ado))
        known["E"] = near_all[1:]
        own_twin = swap(gate("E0", near_all[0]), "rows", 1)
        known["E0"] = own_twin
    arrived = lax.all_to_all(gate("DA", packed), "seq", 0, 0, tiled=True)
    known["DA"] = arrived
    back, sums, *grads = gate(
        "headend",
        head_grad(
            (head_weight, q_two, k_two, v_two, hot, docs, x_low), gate("head", arrived), share,
            4 if fast else 0,
        ),
    )
    known["head"] = back
    if fast:
        up_part, bias_part = call(
            part_weights_kernel,
            "part_weights",
            (far(up_weight), gate("part", up_row)),
            [((D, D), BF, FAR), ((1, D), F32)],
            [((8, D, 384), BF), ((D, D), BF)],
            14,
            9,
        )
        known["part"] = bias_part
        all_features = spread_rows(gate("feat", features))
        known["feat"] = all_features[1:]
        twins = with_twin(gate("Etwin", near_all[1:]))
        near_all = [near_all[0], own_twin, *twins]
        known["Etwin"] = twins[3:]
        up_own, up_sent, down_own, down_sent = feed_grad(
            near_all, up_part, gate("feed", bias_part), down_weight
        )
        known["feed"] = up_own
        up_sent, down_sent = gate("RS1", (up_sent, down_sent))
        up_got, down_got = swap(up_sent, "seq", 2), swap(down_sent, "seq", 4)
        known["RS1"] = (up_got, down_got)
    back = lax.all_to_all(gate("BACK", back), "seq", 0, 0, tiled=True)
    known["BACK"] = back
    blocks, mines = (), ()
    if fast:
        *sent, own = gate("GRS", grads)
        sent = [swap(block, "rows", to + 1) for to, block in enumerate(sent)]
        known["GRS"] = sent
        blocks, mines = (own, *sent), ((own.shape, BF),)
    input_grad, doc_grad, *mine = call(
        functools.partial(input_grad_kernel, share),
        "input_grad",
        (gate("in", back), far(dr1), far(qkv_weight), sums, *(far(one) for one in blocks)),
        [tile32, ((DOCS + SUMS, D), F32), *mines],
        [tile32, ((D, 3 * D), BF), *((one.shape, one.dtype) for one in blocks)],
        12,
        8,
    )
    known["in"] = input_grad
    if fast:
        spread = lax.all_to_all(gate("GA2A", mine[0]), "seq", 0, 0, tiled=True)
        known["GA2A"] = spread
        docs_all = spread_rows(gate("DOCS", doc_grad))
        known["DOCS"] = docs_all[1:]
        up_got, down_got = gate("half", (up_got, down_got))
        halves = [far(one) for one in (up_own, down_own, up_got, down_got)]
        up_sent, down_sent = call(
            combine_half_kernel, "combine_half", halves,
            [((120, D), BF), ((96, D), BF)],
            [(one[1].shape, one[1].dtype) for one in halves],
            8,
            4,
        )
        known["half"] = up_sent
        up_sent, down_sent = gate("RS2", (up_sent, down_sent))
        up_last, down_last = swap(up_sent, "seq", 4), swap(down_sent, "seq", 2)
        known["RS2"] = (up_last, down_last)
        grad_time_weight, norm_sums, bias_sums, grad_up_bias = call(
            time_grad_kernel, "time_grad",
            (*(far(one) for one in all_features), *gate("time", docs_all)),
            [((share, D), F32), ((4, 96), F32), ((2, 96), F32), ((1, 384), F32)],
            [((4 * DOCS, D), BF)],
            8,
            4,
        )
        known["time"] = grad_time_weight
        heads_all = spread_rows(gate("AGG", spread))
        known["AGG"] = heads_all[1:]
        up_last, down_last = gate("all", (up_last, down_last))
        merged = call(
            combine_all_kernel, "combine_all", (*halves, up_last, down_last),
            [((216, D), BF)],
            [(one[1].shape[1:], one[1].dtype) for one in halves],
            8,
            4,
        )[0]
        known["all"] = merged
        merged = gate("AGF", merged)
        across = swap(merged, "rows", 2)
        feed_all = [merged, swap(merged, "rows", 1), across]
        grad_qkv_weight, grad_qv_bias = call(
            finish_heads_kernel, "finish_heads", gate("finh", heads_all),
            [((share, 3 * D), F32), ((1, 192), F32)],
        )
        known["finh"] = grad_qkv_weight
        grad_qv_bias, grad_up_bias = grad_qv_bias[0], grad_up_bias[0]
        grad_out_bias, grad_down_bias = bias_sums[0], bias_sums[1]
        grad_norm_gain, grad_norm_bias = norm_sums[:2], norm_sums[2:]
        others = (
            grad_qkv_weight, grad_qv_bias, grad_up_bias, grad_out_bias, grad_down_bias,
            grad_norm_gain, grad_norm_bias,
        )
        others, held = lax.optimization_barrier((others, across))
        (
            grad_qkv_weight, grad_qv_bias, grad_up_bias, grad_out_bias, grad_down_bias,
            grad_norm_gain, grad_norm_bias,
        ) = others
        feed_all.append(swap(held, "rows", 1))
        grad_up_weight, grad_down_weight, grad_out_weight = call(
            finish_all_kernel, "finish_all", gate("finf", feed_all),
            [((share, FF), F32), ((FF // seqs, D), F32), ((share, D), F32)],
            [((4, 120, D), F32)],
        )
        known["finf"] = grad_out_weight
    else:
        doc_grad = gather_rows(doc_grad[:DOCS], rank).reshape(ranks * DOCS, D)
        grad_time_weight = lax.dot_general(
            all_features.reshape(ranks * DOCS, share).astype(F32),
            doc_grad,
            (((0,), (0,)), ((), ())),
            precision=precise,
        )
        grad_qkv_weight, qv_sums, grad_out_weight, grad_up_weight, grad_down_weight, totals = (
            general_grads(ydf, ado[0], grads[0], grads[1], up_weight, up_bias, down_weight)
        )

        def part_of(vector, axis=0):
            size = vector.shape[axis] // seqs
            return lax.dynamic_slice_in_dim(vector, seq * size, size, axis)

        grad_qv_bias, grad_out_bias = part_of(qv_sums), part_of(totals[4])
        grad_up_bias = part_of(totals[6 : 6 + FF // D].reshape(-1))
        grad_down_bias = part_of(totals[5])
        grad_norm_gain, grad_norm_bias = part_of(totals[0:2], 1), part_of(totals[2:4], 1)

    return (
        result[None],
        input_grad[None],
        grad_qkv_weight,
        grad_qv_bias,
        grad_out_weight,
        grad_out_bias,
        grad_up_weight,
        grad_up_bias,
        grad_down_weight,
        grad_down_bias,
        grad_norm_gain,
        grad_norm_bias,
        grad_time_weight,
    )


def solution(mesh):
    tokens = P("rows", "seq", None)
    whole = P()
    return jax.shard_map(
        body,
        mesh=mesh,
        in_specs=(tokens, tokens, P("rows", "seq"), P("rows", None)) + (whole,) * 11,
        out_specs=(
            tokens,
            tokens,
            P("seq", None),
            P("seq"),
            P("seq", None),
            P("seq"),
            P("seq", None),
            P("seq"),
            P("seq", None),
            P("seq"),
            P(None, "seq"),
            P(None, "seq"),
            P("seq", None),
        ),
        check_vma=False,
    )
```

```python
import functools
import math

import jax
import jax.numpy as jnp
from jax import lax
from jax.experimental import pallas as pl
from jax.experimental.pallas import tpu as pltpu
from jax.sharding import PartitionSpec as P

D = 768
H = 12
HD = 64
FF = 3072
DOCS = 16
PAIR = 2 * HD
PAIRS = D // PAIR
Z_STEPS = 4
SUMS = 16

EPS = 1e-05
MASKED = -1e30
BF = jnp.bfloat16
F32 = jnp.float32
precise = lax.Precision.HIGHEST
VMEM = pl.BlockSpec(memory_space=pltpu.VMEM)


def swap(block, axis, bit):
    return lax.ppermute(block, axis, [(i, i ^ bit) for i in range(lax.axis_size(axis))])


def dot(a, b, dims):
    return lax.dot_general(a, b, (dims, ((), ())), preferred_element_type=F32)


def nn(a, b):
    return dot(a, b, ((1,), (0,)))


def nt(a, b):
    return dot(a, b, ((1,), (1,)))


def tn(a, b):
    return dot(a, b, ((0,), (0,)))


APART = pl.BlockSpec(memory_space=pltpu.HBM)
FAR = "far"
NEAR = "near"


def far(value):
    return FAR, value


def call(kernel, name, ins, outs, scratch=(), vmem=8, copies=0):
    specs = [APART if isinstance(one, tuple) else VMEM for one in ins]
    values = [
        pltpu.with_memory_space_constraint(one[1], pltpu.HBM) if isinstance(one, tuple) else one
        for one in ins
    ]
    held = [pltpu.VMEM(*one) for one in scratch]
    if copies:
        held.append(pltpu.SemaphoreType.DMA((copies,)))
    return pl.pallas_call(
        kernel,
        out_shape=tuple(
            (pltpu.HBM if FAR in one else pltpu.VMEM)(*one[:2])
            if one[2:]
            else jax.ShapeDtypeStruct(*one)
            for one in outs
        ),
        in_specs=specs,
        out_specs=tuple(APART if FAR in one else VMEM for one in outs),
        scratch_shapes=held,
        compiler_params=pltpu.CompilerParams(vmem_limit_bytes=vmem << 20),
        cost_estimate=pl.CostEstimate(flops=int(COSTS[name] * 1e9), transcendentals=0, bytes_accessed=0),
        name=name,
    )(*values)


def copy(source, target, sems, at):
    moved = pltpu.make_async_copy(source, target, sems.at[at])
    moved.start()
    return moved


def copies(pairs, sems, first):
    return [copy(one, to, sems, first + at) for at, (one, to) in enumerate(pairs)]


def wait(moved):
    for one in moved:
        one.wait()


def loop(count, step):
    def body(at, carry):
        step(at)
        return carry

    lax.fori_loop(0, count, body, 0)


def at_rows(index, size):
    return pl.ds(pl.multiple_of(index * size, 8), size)


def at_lanes(index, size):
    return pl.ds(pl.multiple_of(index * size, 128), size)


def time_features(timesteps):
    half_width = D // 2
    frequency = jnp.exp(
        jnp.arange(half_width, dtype=F32) * (-math.log(10000.0) / half_width)
    )
    phases = timesteps.astype(F32)[..., None] * frequency
    return jnp.concatenate([jnp.sin(phases), jnp.cos(phases)], axis=-1)


def gather_seq(block, known, gate, meanwhile):
    size = lax.axis_size("seq")
    inner = size // Z_STEPS
    found = [None] * size
    found[0] = block
    for far in range(1, Z_STEPS):
        name = "Z%d" % far
        found[far * inner] = swap(gate(name, block), "seq", far * inner)
        known[name] = found[far * inner]
    for far in range(Z_STEPS):
        if far == 2:
            meanwhile()
        name = "Y%d" % far
        held = gate(name, found[far * inner])
        for near in range(1, inner):
            found[far * inner + near] = swap(held, "seq", near)
        known[name] = found[far * inner + inner - 1]
    return found


ORDER = {
    "Etwin": ("part", ),
    "RS1": ("feed", "part", ),
    "all": ("time", ),
    "backward": ("Y3", "forward", ),
    "fetch": ("Y0", ),
    "finf": ("finh", ),
    "forward": ("Y3", ),
    "half": ("DOCS", "in", ),
    "part": ("head", ),
}
COSTS = {
    "fetch": 7, "forward": 12, "backward": 5, "heads": 3, "part_weights": 3, "feed_grad": 8,
    "head_grad": 12, "input_grad": 5, "combine_half": 1,
    "combine_all": 1, "finish_all": 2, "finish_heads": 1, "time_grad": 1,
}


def split2(value):
    high = value.astype(BF)
    return high, (value - high.astype(F32)).astype(BF)


def split3(value):
    high = value.astype(BF)
    rest = value - high.astype(F32)
    middle = rest.astype(BF)
    low = (rest - middle.astype(F32)).astype(BF)
    return high, middle, low


def head_start(seq, share):
    return jnp.minimum(seq * share // HD, H - 2) * HD


def head_window(share):
    start = head_start(lax.axis_index("seq"), share)
    base = jnp.minimum(start // PAIR, PAIRS - 2) * PAIR
    return base, (2 * PAIR - (start - base)) % (2 * PAIR)


def normalize(value):
    centered = value - jnp.mean(value, axis=-1, keepdims=True)
    inverse = lax.rsqrt(jnp.mean(centered * centered, axis=-1, keepdims=True) + EPS)
    return centered * inverse, inverse


def normalize_back(z, inverse, grad):
    return inverse * (
        grad
        - jnp.mean(grad, axis=-1, keepdims=True)
        - z * jnp.mean(grad * z, axis=-1, keepdims=True)
    )


def total(value):
    return jnp.sum(value, axis=0, keepdims=True)


def gelu_parts(u):
    phi = 0.5 * (1.0 + lax.erf(u * math.sqrt(0.5)))
    return phi, phi + u * (jnp.exp(-0.5 * u * u) * (1.0 / math.sqrt(2.0 * math.pi)))


def fetch_kernel(*refs):
    count = (len(refs) - 1) // 2
    wait(copies(zip(refs[:count], refs[count:-1]), refs[-1], 0))


def forward_kernel(count, *refs):
    shards = refs[:count]
    embed_ref, qkv_ref, bias_ref, wo_ref, bo_ref, gain_ref, off_ref = refs[count : count + 7]
    cot_ref, up_ref, bu_ref, down_ref, bd_ref = refs[count + 7 : count + 12]
    refs = refs[count + 12 :]
    xlow_out, lse_ref, attn_ref, hot_ref, z1_ref, inverse_ref = refs[:6]
    result_ref, ydf_ref, dr2_ref, slope_ref, z2_sum_ref = refs[6:11]
    mask_ref, x_ref, xlow_ref, k_ref, v_ref, q_ref, sems = refs[11:]
    seq = lax.axis_index("seq")
    rows = attn_ref.shape[0]
    width = D
    parts = [slice(at * width, (at + 1) * width) for at in range(FF // width)]
    embed = jnp.concatenate(split3(embed_ref[...]), axis=0)
    places = lax.broadcasted_iota(jnp.int32, (DOCS, rows), 0).astype(F32)
    hot_own = None
    for at in range(count):
        ids = shards[at][rows : rows + 8, :rows].astype(F32)[:1]
        hot = (places == ids).astype(BF)
        hot_ref[:, at_lanes(seq ^ at, rows)] = hot
        x = shards[at][:rows, :].astype(F32) + tn(jnp.concatenate([hot] * 3, axis=0), embed)
        if at == 0:
            hot_own = hot
            x_ref[...] = x
            own = x.astype(BF)
        xlow_ref[at_rows(seq ^ at, rows), :] = x.astype(BF)
    moved = copy(xlow_ref, xlow_out, sems, 0)
    q_ref[...] = (
        (nn(own, qkv_ref[:, :D]) + bias_ref[:, :D]).astype(BF).astype(F32) * (HD**-0.5)
    ).astype(BF)
    step = 2 * rows
    for at in range(count * rows // step):
        piece = slice(at * step, (at + 1) * step)
        every = xlow_ref[piece, :]
        k_ref[piece, :] = nn(every, qkv_ref[:, D : 2 * D]).astype(BF)
        v_ref[piece, :] = (nn(every, qkv_ref[:, 2 * D :]) + bias_ref[:, D:]).astype(BF)
    mask_ref[...] = (tn(hot_own, hot_ref[...]) - 1.0) * -MASKED
    first = lax.broadcasted_iota(jnp.int32, (rows, PAIR), 1) < HD
    lane = lax.broadcasted_iota(jnp.int32, (rows, 128), 1)
    lse = jnp.zeros((rows, 128), F32)
    for pair in range(PAIRS):
        cols = slice(pair * PAIR, (pair + 1) * PAIR)
        q = q_ref[:, cols]
        halves = []
        for half in range(2):
            q_one = jnp.where(first if half == 0 else ~first, q, jnp.zeros_like(q))
            scores = nt(q_one, k_ref[:, cols]) + mask_ref[...]
            top = jnp.max(scores, axis=-1, keepdims=True)
            weights = jnp.exp(scores - top)
            summed = jnp.sum(weights, axis=-1, keepdims=True)
            halves.append(nn(weights.astype(BF), v_ref[:, cols]) * (1.0 / summed))
            lse = jnp.where(lane == 2 * pair + half, top + jnp.log(summed), lse)
        attn_ref[:, cols] = jnp.where(first, halves[0], halves[1])
    lse_ref[...] = lse
    z1, inverse = normalize(x_ref[...] + nn(attn_ref[...].astype(BF), wo_ref[...]) + bo_ref[...])
    z1_ref[...] = z1
    inverse_ref[...] = jnp.broadcast_to(inverse, (rows, 128))
    y1 = z1 * gain_ref[0:1, :] + off_ref[0:1, :]
    y1_low = y1.astype(BF)
    ydf_ref[:, :D] = y1_low
    r2 = y1 + bd_ref[...]
    for cols in parts:
        u = nn(y1_low, up_ref[:, cols]) + bu_ref[:, cols]
        phi, slope = gelu_parts(u)
        slope_ref[:, cols] = slope
        r2 = r2 + nn((u * phi).astype(BF), down_ref[cols, :])
    z2, inverse2 = normalize(r2)
    result_ref[...] = (z2 * gain_ref[1:2, :] + off_ref[1:2, :]).astype(BF)
    cot = cot_ref[...].astype(F32)
    dr2 = normalize_back(z2, inverse2, cot * gain_ref[1:2, :])
    ydf_ref[:, D:] = dr2.astype(BF)
    dr2_ref[...] = dr2
    z2_sum_ref[...] = total(cot * z2)
    moved.wait()


def backward_kernel(
    starts, chips,
    z1_ref, inverse_ref, dr2_ref, slope_ref, z2_sum_ref, attn_ref, cot_ref, hot_ref, lse_ref,
    wo_ref, up_ref, down_ref, gain_ref, ydf_ref,
    packed_ref, dr1_out, docs_out, hot_out, *refs,
):
    ado_outs, ados = refs[:chips], refs[-chips - 1 : -1]
    dr1_ref, docs_ref, sums_ref = refs[chips : chips + 3]
    sems = refs[-1]
    rows = z1_ref.shape[0]
    moved = [copy(hot_ref, hot_out, sems, 0)]
    if chips > 1:
        moved += copies([(ydf_ref, one.at[:, : 2 * D]) for one in ado_outs], sems, 3 + chips)
        ado_outs = [one.at[:, 2 * D :] for one in ado_outs]
    z1 = z1_ref[...]
    dr2 = dr2_ref[...]
    df_low = dr2.astype(BF)
    dy1 = dr2
    width = D
    for at in range(FF // width):
        cols = slice(at * width, (at + 1) * width)
        du_low = (nt(df_low, down_ref[cols, :]) * slope_ref[:, cols]).astype(BF)
        sums_ref[6 + at : 7 + at, :] = total(du_low.astype(F32))
        dy1 = dy1 + nt(du_low, up_ref[:, cols])
    dr1 = normalize_back(z1, inverse_ref[:, 0:1], dy1 * gain_ref[0:1, :])
    dr1_ref[...] = dr1
    moved.append(copy(dr1_ref, dr1_out, sems, 1))
    do_low = dr1.astype(BF)
    da = nt(do_low, wo_ref[...]).astype(BF)
    attn = attn_ref[...]
    to_heads = (
        lax.broadcasted_iota(jnp.int32, (D, 128), 0) // HD
        == lax.broadcasted_iota(jnp.int32, (D, 128), 1)
    ).astype(BF)
    high, middle, low = split3(da.astype(F32) * attn)
    delta = nn(high, to_heads) + nn(middle, to_heads) + nn(low, to_heads)
    lse_first, delta_first = lse_ref[...].T, delta.T
    cot = cot_ref[...].astype(F32)
    sums_ref[0:1, :] = total(dy1 * z1)
    sums_ref[1:2, :] = z2_sum_ref[...]
    sums_ref[2:3, :] = total(dy1)
    sums_ref[3:4, :] = total(cot)
    sums_ref[4:5, :] = total(do_low.astype(F32))
    sums_ref[5:6, :] = total(df_low.astype(F32))
    sums_ref[6 + FF // width :, :] = jnp.zeros((SUMS - 6 - FF // width, D), F32)
    share = D // len(starts)
    for at, start in enumerate(starts):
        packed_ref[at, :rows, :] = da[:, start : start + PAIR]
        head = start // HD
        lines = [lse_first[head : head + 2], delta_first[head : head + 2]]
        if chips > 1:
            mine = sums_ref[:6, at * share : (at + 1) * share]
            lines.append(jnp.concatenate([mine, jnp.zeros((6, 128 - share), F32)], axis=1))
            for part in range(3):
                first = at * 4 * share + part * 128
                lines.append(sums_ref[6 + first // D : 7 + first // D, first % D : first % D + 128])
        used = sum(one.shape[0] for one in lines)
        lines.append(jnp.zeros((SUMS - used, 128), F32))
        lines = jnp.concatenate(lines, axis=0)
        parts = jnp.concatenate([one.astype(F32) for one in split3(lines)], axis=0).astype(BF)
        packed_ref[at, rows:, :] = parts
    hot = hot_ref[:, at_lanes(lax.axis_index("seq"), rows)]
    high, middle, low = split3(dr1)
    docs_ref[...] = nn(hot, high) + nn(hot, middle) + nn(hot, low)
    moved.append(copy(docs_ref, docs_out, sems, 2))
    attn = attn.astype(BF)
    if chips == 1:
        high, low = split2(sums_ref[...])
        ados[0][:rows, :D] = attn
        ados[0][:rows, D:] = do_low
        ados[0][rows:, :D] = high
        ados[0][rows:, D:] = low
    else:
        near, across = lax.axis_index("seq") % 2, lax.axis_index("rows") // 2
        shares = [
            jnp.concatenate(
                [attn[:, (2 * z + y) * 96 : (2 * z + y + 1) * 96] for z in range(4)], axis=1
            )
            for y in range(2)
        ]
        sides = do_low[:, : D // 2], do_low[:, D // 2 :]
        for to, ref in enumerate(ados):
            swapped, over = to // 2, to % 2
            ref[:, : D // 2] = jnp.where(near == swapped, shares[0], shares[1])
            ref[:, D // 2 :] = jnp.where(across == over, sides[0], sides[1])
    moved += copies(zip(ados, ado_outs), sems, 3)
    wait(moved)


def heads_kernel(share, x_in, qkv_in, bias_ref, *refs):
    q_out, k_out, v_out, w_out, x_ref, q_ref, k_ref, v_ref, w_ref, wide_ref, sems = refs
    length = x_ref.shape[0]
    base, back = head_window(share)
    windows = copies(
        [
            (qkv_in.at[:, pl.ds(pl.multiple_of(base + kind * D, PAIR), 2 * PAIR)], wide_ref.at[kind])
            for kind in range(3)
        ],
        sems,
        0,
    )
    step = 256
    pieces = [slice(at * step, (at + 1) * step) for at in range(length // step)]
    loads = copies([(x_in.at[one, :], x_ref.at[one, :]) for one in pieces], sems, 3)
    biases = []
    for kind in range(3):
        windows[kind].wait()
        turned = pltpu.roll(wide_ref[kind].astype(F32), back, 1)[:, :PAIR]
        w_ref[:, kind * PAIR : (kind + 1) * PAIR] = turned.astype(BF)
        if kind == 1:
            biases.append(jnp.zeros((1, PAIR), F32))
        else:
            cols = pl.ds(pl.multiple_of(base + (kind // 2) * D, PAIR), 2 * PAIR)
            bias = jnp.broadcast_to(bias_ref[:, cols], (8, 2 * PAIR))
            biases.append(pltpu.roll(bias, back, 1)[:1, :PAIR])
    first = 3 + len(pieces)
    moved = [copy(w_ref, w_out, sems, first)]
    for at, piece in enumerate(pieces):
        loads[at].wait()
        three = nn(x_ref[piece, :], w_ref[...])
        q_ref[piece, :] = (
            (three[:, :PAIR] + biases[0]).astype(BF).astype(F32) * (HD**-0.5)
        ).astype(BF)
        k_ref[piece, :] = three[:, PAIR : 2 * PAIR].astype(BF)
        v_ref[piece, :] = (three[:, 2 * PAIR :] + biases[2]).astype(BF)
    moved += copies(((q_ref, q_out), (k_ref, k_out), (v_ref, v_out)), sems, first + 1)
    wait(moved)


def head_grad_kernel(step, share, split, *refs):
    w_in, q_in, k_in, v_in, hot_in, docs_in, x_in, da_ref, back_ref, sums_ref = refs[:10]
    w_ref, q_ref, k_ref, v_ref, hot_ref, docs_ref, x_ref = refs[-13:-6]
    dq_ref, dk_ref, dv_ref, heads_ref, grad_ref, sems = refs[-6:]
    outs = refs[10:-13]
    if split:
        *outs, own_ref = outs
    length = q_ref.shape[0]
    rows = length // (D // share)
    seq = lax.axis_index("seq")
    loads = copies(
        (
            (hot_in, hot_ref), (v_in, v_ref), (k_in, k_ref), (q_in, q_ref),
            (w_in, w_ref), (docs_in, docs_ref), (x_in, x_ref),
        ),
        sems,
        0,
    )
    wait(loads[:4])
    first = lax.broadcasted_iota(jnp.int32, (step, PAIR), 1) < HD
    each = step // rows
    sums = jnp.zeros((SUMS, rows), F32)
    for at in range(D // share):
        lines = da_ref[at, rows:, :].astype(F32)
        sums = sums + (lines[:SUMS] + lines[SUMS : 2 * SUMS] + lines[2 * SUMS :])
    sums_ref[...] = sums
    dk_ref[...] = jnp.zeros((length, PAIR), F32)
    dv_ref[...] = jnp.zeros((length, PAIR), F32)

    @functools.partial(loop, length // step)
    def _(at):
        piece = at_rows(at, step)
        blocks = [at * each + one for one in range(each)]
        da_all = jnp.concatenate([da_ref[one, :rows, :] for one in blocks], axis=0)
        stats = jnp.concatenate(
            [da_ref[one, rows:, :].astype(F32) for one in blocks], axis=1
        )
        stats = stats[:SUMS] + stats[SUMS : 2 * SUMS] + stats[2 * SUMS :]
        mask = (tn(hot_ref[...], hot_ref[:, at_lanes(at, step)]) - 1.0) * -MASKED
        halves = []
        for half in range(2):
            here = first if half == 0 else ~first
            q = jnp.where(here, q_ref[piece, :], jnp.zeros((step, PAIR), BF))
            da = jnp.where(here, da_all, jnp.zeros((step, PAIR), BF))
            probs = jnp.exp(nt(k_ref[...], q) + (mask - stats[half : half + 1]))
            ds = (probs * (nt(v_ref[...], da) - stats[2 + half : 3 + half])).astype(BF)
            halves.append(tn(ds, k_ref[...]))
            dk_ref[...] += nn(ds, q)
            dv_ref[...] += nn(probs.astype(BF), da)
        dq_ref[piece, :] = jnp.where(first, halves[0], halves[1]) * (HD**-0.5)

    wait(loads[4:])
    offset = seq * share - head_start(seq, share)
    left = (PAIR - offset) % PAIR
    for at in range(length // step):
        piece = slice(at * step, (at + 1) * step)
        heads_ref[piece, :] = jnp.concatenate(
            [pltpu.roll(ref[piece, :], left, 1)[:, :share] for ref in (dq_ref, dk_ref, dv_ref)],
            axis=1,
        ).astype(BF)
    doc_sums = nn(hot_ref[...], heads_ref[...])
    docs = docs_ref[...]
    for kind in range(3):
        piece = doc_sums[:, kind * share : (kind + 1) * share]
        piece = jnp.concatenate([piece, jnp.zeros((DOCS, PAIR - share), F32)], axis=1)
        parts = jnp.concatenate(split3(pltpu.roll(piece, offset, 1)), axis=0)
        product = nt(parts, w_ref[:, kind * PAIR : (kind + 1) * PAIR])
        docs = docs + (product[:DOCS] + product[DOCS : 2 * DOCS] + product[2 * DOCS :])
    docs = docs.astype(BF)
    extra = back_ref.shape[1] - 6 * DOCS
    full = 3 * share // PAIR
    rest = 3 * share % PAIR
    group = rows * rest // PAIR
    for at in range(D // share):
        for part in range(full):
            back_ref[at, part * rows : (part + 1) * rows, :] = heads_ref[
                at * rows : (at + 1) * rows, part * PAIR : (part + 1) * PAIR
            ]
        back_ref[at, full * rows : extra, :] = jnp.concatenate(
            [
                heads_ref[first : first + group, full * PAIR :]
                for first in range(at * rows, (at + 1) * rows, group)
            ],
            axis=1,
        )
        for col in range(PAIRS):
            back_ref[at, extra + col * DOCS : extra + (col + 1) * DOCS, :] = docs[
                :, col * PAIR : (col + 1) * PAIR
            ]
    if not split:
        outs[0][...] = tn(x_ref[...], heads_ref[...])
        outs[1][...] = total(doc_sums)
        return
    *sent, mine_out = outs
    grad_ref[...] = tn(x_ref[...], heads_ref[...])
    rank = lax.axis_index("rows")
    part = share // split
    high, low = split2(jnp.broadcast_to(total(doc_sums), (8, 3 * share)))
    row = lax.broadcasted_iota(jnp.int32, (8, 3 * share), 0)
    tail = jnp.where(row == 0, high.astype(F32), jnp.where(row == 1, low.astype(F32), 0.0))
    for to, ref in enumerate([own_ref] + list(sent)):
        for at in range(D // share):
            here = pl.ds(pl.multiple_of(at * share + (rank ^ to) * part, 8), part)
            ref[at, :part, :] = grad_ref[here, :].astype(ref.dtype)
            ref[at, part:, :] = tail.astype(ref.dtype)
        if to == 0:
            moved = copy(own_ref, mine_out, sems, 7)
    moved.wait()


def head_grad(apart, da, share, split):
    length = apart[1].shape[0]
    count = D // share
    rows = length // count
    outs = [((count, rows * 3 * share // PAIR + 6 * DOCS, PAIR), BF), ((SUMS, rows), F32)]
    if split:
        block = (count, share // split + 8, 3 * share)
        outs += [(block, BF)] * (split - 1) + [(block, F32, FAR)]
    else:
        outs += [((D, 3 * share), F32), ((1, 3 * share), F32)]
    scratch = [(block, F32)] if split else []
    scratch += [(one.shape, one.dtype) for one in apart] + [((length, PAIR), F32)] * 3
    scratch += [((length, 3 * share), BF), ((D, 3 * share), F32)]
    return call(
        functools.partial(head_grad_kernel, 512, share, split),
        "head_grad",
        (*(far(one) for one in apart), da),
        outs,
        scratch,
        24 if length <= 1024 else 44,
        8,
    )


def combine(blocks, out_ref):
    value = blocks[0][...]
    for ref in blocks[1:]:
        value = value + ref[...].astype(F32)
    count, rows, wide = value.shape
    out_ref[:, : rows - 8, :] = value[:, : rows - 8].astype(out_ref.dtype)
    row = lax.broadcasted_iota(jnp.int32, (8, wide), 0)
    for at in range(count):
        last = value[at, rows - 8 :]
        high, low = split2(jnp.broadcast_to(last[0:1] + last[1:2], (8, wide)))
        out_ref[at, rows - 8 :, :] = jnp.where(
            row == 0, high.astype(F32), jnp.where(row == 1, low.astype(F32), 0.0)
        ).astype(out_ref.dtype)


def input_grad_kernel(share, back_ref, dr1_in, qkv_in, sums_ref, *refs):
    blocks = ()
    if len(refs) > 5:
        blocks, held, refs = refs[:4], refs[-5:-1], refs[4:-5] + refs[-1:]
    grad_ref, docs_ref, *mine_ref, dr1_ref, qkv_ref, sems = refs
    blocks = copies(zip(blocks, held), sems, 4) if blocks else ()
    loads = copies(
        [(qkv_in.at[:, c], qkv_ref.at[:, c]) for c in [slice(i * D, i * D + D) for i in range(3)]],
        sems,
        0,
    )
    loads.append(copy(dr1_in, dr1_ref, sems, 3))
    rows = dr1_ref.shape[0]
    count = D // share
    extra = back_ref.shape[1] - 6 * DOCS
    full = 3 * share // PAIR
    rest = 3 * share % PAIR
    kinds = [[], [], []]
    for at in range(count):
        here = [back_ref[at, part * rows : (part + 1) * rows, :] for part in range(full)]
        last = back_ref[at, full * rows : extra, :]
        here.append(
            jnp.concatenate([last[:, c : c + rest] for c in range(0, PAIR, rest)], axis=0)
        )
        here = jnp.concatenate(here, axis=1)
        for kind in range(3):
            kinds[kind].append(here[:, kind * share : (kind + 1) * share])
    docs = jnp.zeros((6 * DOCS, PAIR), F32)
    for at in range(count):
        docs = docs + back_ref[at, extra:, :].astype(F32)
    docs_ref[:DOCS, :] = jnp.concatenate(
        [docs[at * DOCS : (at + 1) * DOCS] for at in range(PAIRS)], axis=1
    )
    docs_ref[DOCS:, :128] = sums_ref[...]
    docs_ref[DOCS:, 128:] = jnp.zeros((SUMS, D - 128), F32)
    loads[3].wait()
    result = dr1_ref[...]
    for kind in range(3):
        cols = slice(kind * D, (kind + 1) * D)
        loads[kind].wait()
        result = result + nt(jnp.concatenate(kinds[kind], axis=1), qkv_ref[:, cols])
    grad_ref[...] = result
    if blocks:
        wait(blocks)
        combine(held, mine_ref[0])


def unit_share(at):
    return 2 * (at % 4) + at // 4


def part_weights_kernel(up_in, bu_ref, up_out, bu_out, held_ref, up_ref, sems):
    back = (384 - lax.axis_index("rows") * 96) % 384
    loads = copies(
        [
            (up_in.at[:, unit_share(at) * 384 : (unit_share(at) + 1) * 384], held_ref.at[at])
            for at in range(8)
        ],
        sems,
        0,
    )
    ups, biases = [], []
    for at in range(8):
        cols = slice(unit_share(at) * 384, (unit_share(at) + 1) * 384)
        loads[at].wait()
        ups.append(pltpu.roll(held_ref[at].astype(F32), back, 1)[:, :96].astype(BF))
        bias = jnp.broadcast_to(bu_ref[:, cols], (8, 384))
        biases.append(pltpu.roll(bias, back, 1)[:1, :96])
    up_ref[...] = jnp.concatenate(ups, axis=1)
    moved = copy(up_ref, up_out, sems, 8)
    bu_out[...] = jnp.concatenate(biases, axis=1)
    moved.wait()


def feed_grad_kernel(*refs):
    pieces = refs[:8]
    up_in, bu_ref, down_in, up_own_out, up_sent_ref, down_own_out, down_sent_ref = refs[8:15]
    all_ref, up_ref, down_ref, g_ref, du_ref = refs[15:20]
    up_grad_ref, down_grad_ref, out_grad_ref, up_own_ref, down_own_ref, sems = refs[20:]
    seq, rank = lax.axis_index("seq"), lax.axis_index("rows")
    near, z = seq % 2, seq // 2
    rows = pieces[0].shape[0]
    loads = [copy(up_in, up_ref, sems, 8)]
    loads += copies([(pieces[at], all_ref.at[at]) for at in range(2)], sems, 0)
    first = rank * 96
    downs = copies(
        [
            (
                down_in.at[pl.ds(pl.multiple_of(unit_share(at) * 384 + first, 32), 96), :],
                down_ref.at[at * 96 : (at + 1) * 96, :],
            )
            for at in range(8)
        ],
        sems,
        9,
    )
    loads += copies([(pieces[at], all_ref.at[at]) for at in range(2, 8)], sems, 2)
    loads[0].wait()
    step = 2 * rows
    for at in range(4):
        wait(loads[1 + 2 * at : 3 + 2 * at])
        piece = slice(at * step, (at + 1) * step)
        two = slice(2 * at, 2 * at + 2)
        u = nn(all_ref[two, :, :D].reshape(step, D), up_ref[...]) + bu_ref[...]
        phi, slope = gelu_parts(u)
        if at == 0:
            wait(downs)
        g_ref[piece, :] = (u * phi).astype(BF)
        df = all_ref[two, :, D : 2 * D].reshape(step, D)
        du_ref[piece, :] = (nt(df, down_ref[...]) * slope).astype(BF)

    tokens = 8 * rows
    df = all_ref[:, :, D : 2 * D].reshape(tokens, D)
    down_grad_ref[...] = tn(g_ref[:, at_lanes(near, 384)], df)
    up_grad_ref[...] = tn(all_ref[:, :, :D].reshape(tokens, D), du_ref[...])
    base = pl.multiple_of(2 * D + D // 2 + (rank % 2) * 128, 128)
    attn = all_ref[:, :, 2 * D : 2 * D + D // 2].reshape(tokens, D // 2)
    do = all_ref[:, :, pl.ds(base, 256)].reshape(tokens, 256)
    back = (256 - (rank % 2) * 64) % 256
    out_grad_ref[...] = pltpu.roll(tn(attn, do), back, 1)
    for to in range(4):
        up_rows = pl.ds(pl.multiple_of((2 * (z ^ to) + near) * 96, 8), 96)
        down_rows = pl.ds(pl.multiple_of((z ^ to) * 96, 8), 96)
        ref = up_own_ref.at[to // 2] if to % 2 == 0 else up_sent_ref.at[to // 2]
        ref[:96, :] = up_grad_ref[up_rows, :].astype(ref.dtype)
        out = out_grad_ref[down_rows, :192]
        ref[96:, :] = jnp.concatenate(
            [out[part * 24 : (part + 1) * 24] for part in range(4)], axis=1
        ).astype(ref.dtype)
        ref = down_own_ref.at[to % 2] if to < 2 else down_sent_ref.at[to % 2]
        ref[...] = down_grad_ref[down_rows, :].astype(ref.dtype)
    wait(copies(((up_own_ref, up_own_out), (down_own_ref, down_own_out)), sems, 17))


def feed_grad(pieces, up, bias, down):
    tokens = 8 * pieces[0].shape[0]
    blocks = (2, 120, D), (2, 96, D)
    wide = ((tokens, D), BF)
    return call(
        feed_grad_kernel,
        "feed_grad",
        (*(far(one) for one in pieces), far(up), bias, far(down)),
        [one for block in blocks for one in ((block, F32, FAR), (block, BF))],
        [
            ((8, tokens // 8, 3 * D), BF), ((D, D), BF), ((D, D), BF), wide, wide,
            ((D, D), F32), ((384, D), F32), ((384, 256), F32),
            *((block, F32) for block in blocks),
        ],
        28,
        19,
    )


def combine_half_kernel(up_in, down_in, up_got_in, down_got_in, up_ref, down_ref, *refs):
    *held, sems = refs
    loads = copies(zip((up_in, down_in, up_got_in, down_got_in), held), sems, 0)
    wait(loads)
    up_ref[...] = (held[0][1] + held[2][1].astype(F32)).astype(BF)
    down_ref[...] = (held[1][1] + held[3][1].astype(F32)).astype(BF)


def combine_all_kernel(up_in, down_in, up_got_in, down_got_in, up_last_ref, down_last_ref, out_ref, *refs):
    *held, sems = refs
    sources = [one.at[0] for one in (up_in, down_in, up_got_in, down_got_in)]
    wait(copies(zip(sources, held), sems, 0))
    up = held[0][...] + held[2][...].astype(F32) + up_last_ref[...].astype(F32)
    down = held[1][...] + held[3][...].astype(F32) + down_last_ref[...].astype(F32)
    out_ref[:120, :] = up.astype(BF)
    out_ref[120:, :] = down.astype(BF)


def finish_all_kernel(a_ref, b_ref, c_ref, d_ref, up_ref, down_ref, out_ref, held_ref):
    rank = lax.axis_index("rows")
    for at, ref in enumerate((a_ref, b_ref, c_ref, d_ref)):
        held_ref[rank ^ at] = ref[:120, :].astype(F32)
        down_ref[pl.ds(pl.multiple_of((rank ^ at) * 96, 8), 96), :] = ref[120:, :].astype(F32)
    for share in range(8):
        at = (share // 2) + 4 * (share % 2)
        up_ref[:, share * 384 : (share + 1) * 384] = jnp.concatenate(
            [held_ref[r, :96, at * 96 : (at + 1) * 96] for r in range(4)], axis=1
        )
    for at in range(4):
        out_ref[at * 24 : (at + 1) * 24, :] = jnp.concatenate(
            [held_ref[r, 96:, at * 192 : (at + 1) * 192] for r in range(4)], axis=1
        )


def time_grad_kernel(*refs):
    features, docs, (out_ref, norm_ref, bias_ref, up_ref, left_ref, sems) = refs[:4], refs[4:8], refs[8:]
    seq = lax.axis_index("seq")
    wait(
        copies([(ref, left_ref.at[at * DOCS : (at + 1) * DOCS]) for at, ref in enumerate(features)], sems, 0)
    )
    left = left_ref[...].astype(F32)
    left = pltpu.roll(left, (D - seq * 96) % D, 1)[:, :96].astype(BF)
    high, middle, low = split3(jnp.concatenate([ref[:DOCS, :] for ref in docs], axis=0))
    out_ref[...] = tn(left, high) + tn(left, middle) + tn(left, low)
    sums = jnp.zeros((SUMS, 128), F32)
    for ref in docs:
        sums = sums + ref[DOCS:, :128]
    norm_ref[...] = sums[4:8, :96]
    bias_ref[...] = sums[8:10, :96]
    up_ref[...] = jnp.concatenate([sums[at : at + 1] for at in range(10, 13)], axis=1)


def finish_heads_kernel(a_ref, b_ref, c_ref, d_ref, out_ref, bias_ref):
    rank = lax.axis_index("rows")
    order = [(kind, at) for kind in range(3) for at in range(8)]
    for to, ref in enumerate((a_ref, b_ref, c_ref, d_ref)):
        value = jnp.concatenate(
            [ref[at, :24, kind * 96 : (kind + 1) * 96].astype(F32) for kind, at in order], axis=1
        )
        out_ref[pl.ds(pl.multiple_of((rank ^ to) * 24, 8), 24), :] = value
    tail = jnp.concatenate(
        [a_ref[at, 24:, kind * 96 : (kind + 1) * 96].astype(F32) for kind, at in order], axis=1
    )
    sums = tail[0:1] + tail[1:2]
    sums = jnp.concatenate([sums[:, :D], sums[:, 2 * D :]], axis=1)
    back = (2 * D - lax.axis_index("seq") * 192) % (2 * D)
    bias_ref[...] = pltpu.roll(jnp.broadcast_to(sums, (8, 2 * D)), back, 1)[:1, :192]


def after(value, *others):
    return lax.optimization_barrier((value,) + others)[0]


def after_all(values, *others):
    return list(lax.optimization_barrier((tuple(values), others))[0])


def gates(order):
    known = {}

    def gate(name, value):
        held = [known[one] for one in order.get(name, ()) if one in known]
        return lax.optimization_barrier((value, held))[0] if held else value

    return known, gate


def from_chips(own, over, near, both):
    pairs = [((s * 4 + r), ((s ^ 1) * 4 + (r ^ 2))) for s in range(8) for r in range(4)]
    across = lax.ppermute(both, ("seq", "rows"), pairs)
    return [own, swap(over, "rows", 2), swap(near, "seq", 1), across]


def with_twin(blocks):
    return blocks + [swap(one, "rows", 1) for one in blocks]


def spread_rows(block):
    across = swap(block, "rows", 2)
    return block, swap(block, "rows", 1), across, swap(across, "rows", 1)


def pick(blocks, index, axis=0):
    return lax.dynamic_index_in_dim(blocks, index, axis, keepdims=False)


def reduce_rows(blocks, place):
    bit = 1
    while blocks.shape[0] > 1:
        pairs = blocks.reshape((blocks.shape[0] // 2, 2) + blocks.shape[1:])
        mine = (place // bit) % 2
        sent = swap(pick(pairs, 1 - mine, 1).astype(BF), "rows", bit)
        blocks = pick(pairs, mine, 1).astype(F32) + sent.astype(F32)
        bit *= 2
    return blocks[0]


def gather_rows(block, place):
    count = lax.axis_size("rows")
    found = block[None]
    bit = count // 2
    while bit >= 1:
        other = swap(found, "rows", bit)
        mine = (place // bit) % 2
        low, high = jnp.where(mine == 0, found, other), jnp.where(mine == 0, other, found)
        if bit == count // 2:
            found = jnp.concatenate([low, high], axis=0)
        else:
            found = jnp.stack([low, high], axis=1).reshape((-1,) + block.shape)
        bit //= 2
    return found


def general_grads(ydf, ado, grad_heads, head_sums, up_weight, up_bias, down_weight):
    seqs, ranks = lax.axis_size("seq"), lax.axis_size("rows")
    seq, rank = lax.axis_index("seq"), lax.axis_index("rows")
    inner = seqs // Z_STEPS
    near = seq % inner
    share = D // seqs
    ff_share = FF // seqs
    ff_part = ff_share // ranks
    rows = ydf.shape[0]

    part = share // ranks
    grad_heads = grad_heads.reshape(seqs, ranks, part, 3 * share)
    mine = reduce_rows(jnp.moveaxis(grad_heads, 1, 0), rank)
    spread = lax.all_to_all(mine.astype(BF), "seq", 0, 0, tiled=True)
    columns = [
        spread[i, :, kind * share : (kind + 1) * share] for kind in range(3) for i in range(seqs)
    ]
    quarter = jnp.concatenate(columns, axis=1)
    grad_qkv = gather_rows(quarter, rank).reshape(share, 3 * D).astype(F32)

    def gather_near(block):
        found = [block]
        bit = 2
        while bit < ranks:
            found = found + [swap(one, "rows", bit) for one in found]
            bit *= 2
        for step in range(1, inner):
            found = found + [swap(one, "seq", step) for one in found[: len(found) // step]]
        mine = jnp.concatenate(found, axis=0)
        return jnp.concatenate([mine, swap(mine, "rows", 1)], axis=0)

    ydf_all = gather_near(ydf)
    y1_all, df_all = ydf_all[:, :D], ydf_all[:, D:]
    order = [far * inner + i for i in range(inner) for far in range(Z_STEPS)]
    ff_starts = [i * ff_share + rank * ff_part for i in order]
    take = lambda array, axis: jnp.concatenate(
        [lax.dynamic_slice_in_dim(array, a, ff_part, axis) for a in ff_starts], axis=axis
    )
    up_mine, down_mine, bias_mine = take(up_weight, 1), take(down_weight, 0), take(up_bias, 0)
    u = nn(y1_all, up_mine) + bias_mine
    phi, slope = gelu_parts(u)
    du_all = (nt(df_all, down_mine) * slope).astype(BF)
    g_all = (u * phi).astype(BF)
    group = Z_STEPS * ff_part
    g_near = lax.dynamic_slice_in_dim(g_all, near * group, group, 1)
    grad_down = tn(g_near, df_all).reshape(Z_STEPS, ff_part, D)
    grad_up = pick(tn(y1_all, du_all).reshape(Z_STEPS, inner, share, seqs * ff_part), near, 1)
    ado, grad_up, grad_down = lax.optimization_barrier((ado, grad_up, grad_down))
    ado_all = gather_near(ado[:rows])
    attn_all, do_all = ado_all[:, :D], ado_all[:, D:]
    out_part = D // ranks
    do_mine = lax.dynamic_slice_in_dim(do_all, rank * out_part, out_part, 1)
    grad_out = pick(tn(attn_all, do_mine).reshape(Z_STEPS, inner, share, out_part), near, 1)

    def reduce_far(blocks):
        blocks = blocks.astype(BF)
        far = seq // inner
        summed = pick(blocks, far).astype(F32)
        for step in range(1, Z_STEPS):
            summed = summed + swap(pick(blocks, far ^ step), "seq", step * inner).astype(F32)
        return gather_rows(summed.astype(BF), rank)

    grad_down = reduce_far(grad_down).reshape(ff_share, D).astype(F32)
    grad_up = reduce_far(grad_up).reshape(ranks, share, inner, Z_STEPS, ff_part)
    grad_up = jnp.transpose(grad_up, (1, 3, 2, 0, 4)).reshape(share, FF).astype(F32)
    grad_out = jnp.transpose(reduce_far(grad_out), (1, 0, 2)).reshape(share, D).astype(F32)

    sums = ado[rows:, :D].astype(F32) + ado[rows:, D:].astype(F32)
    placed = lambda kind: lax.dynamic_update_slice_in_dim(
        jnp.zeros((D,), F32), head_sums[0, kind * share : (kind + 1) * share], seq * share, 0
    )
    sums = sums.at[10].set(placed(0)).at[11].set(placed(2))
    for axis, count in (("rows", ranks), ("seq", seqs)):
        bit = 1
        while bit < count:
            sums = sums + swap(sums, axis, bit)
            bit *= 2
    return grad_qkv, sums[10:12].reshape(-1), grad_out, grad_up, grad_down, sums


def body(
    hidden, cotangent, segment_ids, timesteps, qkv_weight, qv_bias, out_weight, out_bias,
    up_weight, up_bias, down_weight, down_bias, norm_gain, norm_bias, time_weight,
):
    assert hidden.shape[0] == 1
    rows = hidden.shape[1]
    seqs, ranks = lax.axis_size("seq"), lax.axis_size("rows")
    length = seqs * rows
    seq, rank = lax.axis_index("seq"), lax.axis_index("rows")
    share = D // seqs
    inner = seqs // Z_STEPS
    fast = seqs == 8 and ranks == 4
    starts = [min(i * share // HD, H - 2) * HD for i in range(seqs)]

    known, gate = gates(ORDER if fast else {})
    features = time_features(timesteps[0]).astype(BF)
    up_row = up_bias.reshape(1, -1)
    weights = [((D, 3 * D), BF), ((D, D), BF), ((D, FF), BF), ((FF, D), BF)]

    def meanwhile():
        known["weights"] = call(
            fetch_kernel,
            "fetch",
            (far(gate("fetch", qkv_weight)), far(out_weight), far(up_weight), far(down_weight)),
            [(*one, NEAR) for one in weights],
            (),
            2,
            4,
        )
        known["fetch"] = known["weights"][1]

    ids = jnp.pad(segment_ids.astype(BF), ((0, 7), (0, D - rows)))
    shards = gather_seq(jnp.concatenate([hidden[0], ids], axis=0), known, gate, meanwhile)
    qkv_near, out_near, up_near, down_near = known["weights"]
    embed = nn(features, time_weight)
    if not fast:
        all_features = gather_rows(features, rank)
        all_features = lax.dynamic_slice_in_dim(all_features, seq * share, share, 2)
    qv_row = qv_bias.reshape(1, -1)
    tile = ((rows, D), BF)
    tile32 = ((rows, D), F32)
    narrow32 = ((rows, 128), F32)
    wide = ((length, D), BF)
    out_row, down_row = out_bias.reshape(1, -1), down_bias.reshape(1, -1)
    x_low, lse, attn, hot, z1, inverse1, result, ydf, dr2, slope, z2_sum = call(
        functools.partial(forward_kernel, seqs),
        "forward",
        (
            *shards, embed, qkv_near, qv_row, out_near, out_row, norm_gain,
            norm_bias, cotangent[0], up_near, up_row, down_near, down_row,
        ),
        [
            (*wide, FAR), narrow32,
            tile32, ((DOCS, length), BF), tile32, narrow32,
            tile, ((rows, 2 * D), BF), tile32, ((rows, FF), F32), ((1, D), F32),
        ],
        [((rows, length), F32), tile32, wide, wide, wide, tile],
        16 if fast else 28,
        1,
    )
    known["forward"] = z1
    if fast:
        ados = [((rows, 3 * D), BF)] * 4
    else:
        ados = [((rows + SUMS, 2 * D), BF)]
    hots = ((DOCS, length), BF)
    docs_shape = ((DOCS, D), F32)
    packed, dr1, docs, hot, *ado = call(
        functools.partial(backward_kernel, starts, len(ados)),
        "backward",
        (
            gate("backward", z1), inverse1, dr2, slope, z2_sum, attn, cotangent[0], hot, lse,
            out_near, up_near, down_near, norm_gain, ydf,
        ),
        [
            ((seqs, rows + 3 * SUMS, PAIR), BF), (*tile32, FAR), (*docs_shape, FAR), (*hots, FAR),
            *((*one, FAR) for one in ados),
        ],
        [tile32, docs_shape, ((SUMS, D), F32), *([tile] * 4 if fast else ados)],
        8,
        3 + 2 * len(ados),
    )
    known["backward"] = packed

    pair = ((length, PAIR), BF)
    head_shape = ((D, 3 * PAIR), BF)
    q_two, k_two, v_two, head_weight = call(
        functools.partial(heads_kernel, share),
        "heads",
        (far(x_low), far(qkv_weight), gate("heads", qv_row)),
        [(*one, FAR) for one in (pair, pair, pair, head_shape)],
        [wide, pair, pair, pair, head_shape, ((3, D, 2 * PAIR), BF)],
        16,
        7 + length // 256,
    )
    known["heads"] = q_two
    if fast:
        near_all = from_chips(*gate("E", ado))
        known["E"] = near_all[1:]
        own_twin = swap(gate("E0", near_all[0]), "rows", 1)
        known["E0"] = own_twin
    arrived = lax.all_to_all(gate("DA", packed), "seq", 0, 0, tiled=True)
    known["DA"] = arrived
    back, sums, *grads = gate(
        "headend",
        head_grad(
            (head_weight, q_two, k_two, v_two, hot, docs, x_low), gate("head", arrived), share,
            4 if fast else 0,
        ),
    )
    known["head"] = back
    if fast:
        up_part, bias_part = call(
            part_weights_kernel,
            "part_weights",
            (far(up_weight), gate("part", up_row)),
            [((D, D), BF, FAR), ((1, D), F32)],
            [((8, D, 384), BF), ((D, D), BF)],
            14,
            9,
        )
        known["part"] = bias_part
        all_features = spread_rows(gate("feat", features))
        known["feat"] = all_features[1:]
        twins = with_twin(gate("Etwin", near_all[1:]))
        near_all = [near_all[0], own_twin, *twins]
        known["Etwin"] = twins[3:]
        up_own, up_sent, down_own, down_sent = feed_grad(
            near_all, up_part, gate("feed", bias_part), down_weight
        )
        known["feed"] = up_own
        up_sent, down_sent = gate("RS1", (up_sent, down_sent))
        up_got, down_got = swap(up_sent, "seq", 2), swap(down_sent, "seq", 4)
        known["RS1"] = (up_got, down_got)
    back = lax.all_to_all(gate("BACK", back), "seq", 0, 0, tiled=True)
    known["BACK"] = back
    blocks, mines = (), ()
    if fast:
        *sent, own = gate("GRS", grads)
        sent = [swap(block, "rows", to + 1) for to, block in enumerate(sent)]
        known["GRS"] = sent
        blocks, mines = (own, *sent), ((own.shape, BF),)
    input_grad, doc_grad, *mine = call(
        functools.partial(input_grad_kernel, share),
        "input_grad",
        (gate("in", back), far(dr1), far(qkv_weight), sums, *(far(one) for one in blocks)),
        [tile32, ((DOCS + SUMS, D), F32), *mines],
        [tile32, ((D, 3 * D), BF), *((one.shape, one.dtype) for one in blocks)],
        12,
        8,
    )
    known["in"] = input_grad
    if fast:
        spread = lax.all_to_all(gate("GA2A", mine[0]), "seq", 0, 0, tiled=True)
        known["GA2A"] = spread
        docs_all = spread_rows(gate("DOCS", doc_grad))
        known["DOCS"] = docs_all[1:]
        up_got, down_got = gate("half", (up_got, down_got))
        halves = [far(one) for one in (up_own, down_own, up_got, down_got)]
        up_sent, down_sent = call(
            combine_half_kernel, "combine_half", halves,
            [((120, D), BF), ((96, D), BF)],
            [(one[1].shape, one[1].dtype) for one in halves],
            8,
            4,
        )
        known["half"] = up_sent
        up_sent, down_sent = gate("RS2", (up_sent, down_sent))
        up_last, down_last = swap(up_sent, "seq", 4), swap(down_sent, "seq", 2)
        known["RS2"] = (up_last, down_last)
        grad_time_weight, norm_sums, bias_sums, grad_up_bias = call(
            time_grad_kernel, "time_grad",
            (*(far(one) for one in all_features), *gate("time", docs_all)),
            [((share, D), F32), ((4, 96), F32), ((2, 96), F32), ((1, 384), F32)],
            [((4 * DOCS, D), BF)],
            8,
            4,
        )
        known["time"] = grad_time_weight
        heads_all = spread_rows(gate("AGG", spread))
        known["AGG"] = heads_all[1:]
        up_last, down_last = gate("all", (up_last, down_last))
        merged = call(
            combine_all_kernel, "combine_all", (*halves, up_last, down_last),
            [((216, D), BF)],
            [(one[1].shape[1:], one[1].dtype) for one in halves],
            8,
            4,
        )[0]
        known["all"] = merged
        merged = gate("AGF", merged)
        across = swap(merged, "rows", 2)
        feed_all = [merged, swap(merged, "rows", 1), across]
        grad_qkv_weight, grad_qv_bias = call(
            finish_heads_kernel, "finish_heads", gate("finh", heads_all),
            [((share, 3 * D), F32), ((1, 192), F32)],
        )
        known["finh"] = grad_qkv_weight
        grad_qv_bias, grad_up_bias = grad_qv_bias[0], grad_up_bias[0]
        grad_out_bias, grad_down_bias = bias_sums[0], bias_sums[1]
        grad_norm_gain, grad_norm_bias = norm_sums[:2], norm_sums[2:]
        others = (
            grad_qkv_weight, grad_qv_bias, grad_up_bias, grad_out_bias, grad_down_bias,
            grad_norm_gain, grad_norm_bias,
        )
        others, held = lax.optimization_barrier((others, across))
        (
            grad_qkv_weight, grad_qv_bias, grad_up_bias, grad_out_bias, grad_down_bias,
            grad_norm_gain, grad_norm_bias,
        ) = others
        feed_all.append(swap(held, "rows", 1))
        grad_up_weight, grad_down_weight, grad_out_weight = call(
            finish_all_kernel, "finish_all", gate("finf", feed_all),
            [((share, FF), F32), ((FF // seqs, D), F32), ((share, D), F32)],
            [((4, 120, D), F32)],
        )
        known["finf"] = grad_out_weight
    else:
        doc_grad = gather_rows(doc_grad[:DOCS], rank).reshape(ranks * DOCS, D)
        grad_time_weight = lax.dot_general(
            all_features.reshape(ranks * DOCS, share).astype(F32),
            doc_grad,
            (((0,), (0,)), ((), ())),
            precision=precise,
        )
        grad_qkv_weight, qv_sums, grad_out_weight, grad_up_weight, grad_down_weight, totals = (
            general_grads(ydf, ado[0], grads[0], grads[1], up_weight, up_bias, down_weight)
        )

        def part_of(vector, axis=0):
            size = vector.shape[axis] // seqs
            return lax.dynamic_slice_in_dim(vector, seq * size, size, axis)

        grad_qv_bias, grad_out_bias = part_of(qv_sums), part_of(totals[4])
        grad_up_bias = part_of(totals[6 : 6 + FF // D].reshape(-1))
        grad_down_bias = part_of(totals[5])
        grad_norm_gain, grad_norm_bias = part_of(totals[0:2], 1), part_of(totals[2:4], 1)

    return (
        result[None],
        input_grad[None],
        grad_qkv_weight,
        grad_qv_bias,
        grad_out_weight,
        grad_out_bias,
        grad_up_weight,
        grad_up_bias,
        grad_down_weight,
        grad_down_bias,
        grad_norm_gain,
        grad_norm_bias,
        grad_time_weight,
    )


def solution(mesh):
    tokens = P("rows", "seq", None)
    whole = P()
    return jax.shard_map(
        body,
        mesh=mesh,
        in_specs=(tokens, tokens, P("rows", "seq"), P("rows", None)) + (whole,) * 11,
        out_specs=(
            tokens,
            tokens,
            P("seq", None),
            P("seq"),
            P("seq", None),
            P("seq"),
            P("seq", None),
            P("seq"),
            P("seq", None),
            P("seq"),
            P(None, "seq"),
            P(None, "seq"),
            P("seq", None),
        ),
        check_vma=False,
    )
```
